256 devices in a mesh: dom: 8 (over y, core), feat: 32 (over z, x).
Axes of the slice: x: 4, y: 4, z: 8, core: 2. Of those that a mesh axis runs over, the one named last changes fastest.
Arguments:
- node_feats: bfloat16 [1024, 32768], P('feat', 'dom'), may hold values from -6 to 6
- send_rows: int32 [8192], P('dom'), may hold values from 0 to 4095
- hub_rows: int32 [1024], P('dom'), may hold values from 0 to 4095
- tile_dst: int32 [4096], P('dom'), may hold values from 0 to 7
- tile_src: int32 [4096], P('dom'), may hold values from 0 to 47
- tile_count: int32 [8], P('dom'), may hold values from 128 to 512, as said below
- tile_vals: bfloat16 [4096, 128, 128], P('dom'), may hold values from -0.0625 to 0.0625
- w_self: bfloat16 [1024, 1024], P('feat'), may hold values from -0.1875 to 0.1875
- w_neigh: bfloat16 [1024, 1024], P('feat'), may hold values from -0.1875 to 0.1875
- bias_vec: float32 [1024], P('feat'), may hold values from -3 to 3
- cotangent: bfloat16 [1024, 8192], P('feat', 'dom'), may hold values from -6 to 6
Outputs:
- activations: bfloat16 [1024, 8192], P('feat', 'dom')
- grad_feats: float32 [1024, 32768], P('feat', 'dom')
- grad_w_self: float32 [1024, 1024], P('feat')
- grad_w_neigh: float32 [1024, 1024], P('feat')
- grad_bias: float32 [1024], P('feat')
The draws below stay inside these ranges and needn't reach their ends.
Inputs may be any that keep to these rules, and one draw needn't show every extreme that they name: `tile_count`: every partition has at least 128 live slots, and some partition has all 512 live; slots at or past the count are not edges: their tile_vals may hold any values and must be ignored.
All inputs are finite; a program needn't handle non-finite values.
Results may differ from the reference program's by a relative error of at most 0.0075.
Values may be sent and summed in bfloat16 or wider, within the bound.
A program may use at most 128 MiB of HBM per device.

```python
import jax
import jax.numpy as jnp
from jax import lax

D = 1024
LOC_DEV = 4096
DST_DEV = 1024
BND = 128
HUB_DEV = 128
TILES = 512
TABLE = 6144
SRC = 32768
DST_ALL = 8192
N_DOM = 8


def draw_tile_count(key, part):
    first_key, second_key = jax.random.split(key)
    counts = jax.random.randint(first_key, (N_DOM,), TILES // 4, TILES + 1)
    busiest = jax.random.randint(second_key, (), 0, N_DOM)
    return jnp.where(jnp.arange(N_DOM) == busiest, TILES, counts).astype(jnp.int32)


def touch_ends(result, key, least, high):
    place = [jax.random.randint(jax.random.fold_in(key, axis), (), 0, length) for axis, length in enumerate(result.shape)]
    longest = result.shape.index(max(result.shape))
    beside = place[:longest] + [(place[longest] + 1) % result.shape[longest]] + place[longest + 1:]
    return result.at[tuple(place)].set(least).at[tuple(beside)].set(high)


def levels(rng, shape, shards, low, top_value):
    gain = 1.0
    for axis_at, blocks in shards:
        steps = jax.random.uniform(jax.random.fold_in(jax.random.fold_in(rng, 6), axis_at), (blocks,), jnp.float32, low / len(shards), top_value / len(shards))
        gain = gain * jnp.repeat(jnp.exp(steps), shape[axis_at] // blocks).reshape((-1,) + (1,) * (len(shape) - 1 - axis_at))
    return gain


def bell_draw(own_key, shape, deviation, reach, shards=(), kind=jnp.bfloat16):
    drawn = deviation * jax.random.normal(own_key, shape, jnp.float32)
    if shards:
        drawn = drawn * levels(own_key, shape, shards, -0.22, 0.18)
    return jnp.clip(drawn, -reach, reach).astype(kind)


def setup_inputs(seed: int = 0) -> dict:
    seeds = jax.random.split(jax.random.key(seed), 12)
    node_feats = bell_draw(seeds[0], (D, SRC), 1.0, 6.0, ((0, 32), (1, 8)))
    send_rows = touch_ends(jax.random.randint(seeds[1], (N_DOM * N_DOM * BND,), 0, LOC_DEV), jax.random.fold_in(seeds[1], 1), 0, LOC_DEV - 1).astype(jnp.int32)
    hub_rows = touch_ends(jax.random.randint(seeds[2], (N_DOM * HUB_DEV,), 0, LOC_DEV), jax.random.fold_in(seeds[2], 1), 0, LOC_DEV - 1).astype(jnp.int32)
    tile_dst = touch_ends(jax.random.randint(seeds[3], (N_DOM * TILES,), 0, DST_DEV // 128), jax.random.fold_in(seeds[3], 1), 0, (DST_DEV // 128) - 1).astype(jnp.int32)
    tile_src = touch_ends(jax.random.randint(seeds[4], (N_DOM * TILES,), 0, TABLE // 128), jax.random.fold_in(seeds[4], 1), 0, (TABLE // 128) - 1).astype(jnp.int32)
    tile_count = draw_tile_count(jax.random.fold_in(seeds[11], 71), 0)
    tile_vals = bell_draw(seeds[6], (N_DOM * TILES, 128, 128), (128 * TILES * 128 // DST_DEV) ** -0.5, 0.0625, ((0, 8),))
    w_self = bell_draw(seeds[7], (D, D), D ** -0.5, 0.1875, ((0, 32),))
    w_neigh = bell_draw(seeds[8], (D, D), D ** -0.5, 0.1875, ((0, 32),))
    bias_vec = bell_draw(seeds[9], (D,), 0.5, 3.0, ((0, 32),), jnp.float32)
    cotangent = bell_draw(seeds[10], (D, DST_ALL), 1.0, 6.0, ((0, 32), (1, 8)))
    return {"node_feats": node_feats, "send_rows": send_rows, "hub_rows": hub_rows, "tile_dst": tile_dst, "tile_src": tile_src, "tile_count": tile_count, "tile_vals": tile_vals, "w_self": w_self, "w_neigh": w_neigh, "bias_vec": bias_vec, "cotangent": cotangent}


def take_cols(columns, indices):
    return jnp.take(columns, indices, axis=1)


def add_cols(grads, indices, values):
    return grads.at[:, indices].add(values)


def reference(node_feats, send_rows, hub_rows, tile_dst, tile_src, tile_count, tile_vals, w_self, w_neigh, bias_vec, cotangent):
    tile_total = TABLE // 128
    dst_tiles = DST_DEV // 128
    parts = node_feats.reshape(D, N_DOM, LOC_DEV).transpose(1, 0, 2)
    sends = send_rows.reshape(N_DOM, N_DOM * BND)
    hubs = hub_rows.reshape(N_DOM, HUB_DEV)
    sent_cols = jax.vmap(take_cols)(parts, sends)
    halo_in = sent_cols.reshape(N_DOM, D, N_DOM, BND).transpose(2, 1, 0, 3).reshape(N_DOM, D, N_DOM * BND)
    hub_cols = jax.vmap(take_cols)(parts, hubs).transpose(1, 0, 2).reshape(D, N_DOM * HUB_DEV)
    dsts = tile_dst.reshape(N_DOM, TILES)
    srcs = tile_src.reshape(N_DOM, TILES)
    vals = tile_vals.reshape(N_DOM, TILES, 128, 128)

    def forward_part(items):
        owned, halo, dst_ids, src_ids, count, values = items
        source_table = jnp.concatenate([owned, halo, hub_cols], axis=1)
        live_mask = (jnp.arange(TILES) < count).astype(jnp.float32)
        dst_hot = (dst_ids[:, None] == jnp.arange(dst_tiles)[None, :]).astype(jnp.float32) * live_mask[:, None]
        picked = source_table.reshape(D, tile_total, 128)[:, src_ids, :]
        products = jnp.einsum("fkj,kij->fki", picked.astype(jnp.float32), values.astype(jnp.float32), precision=lax.Precision.HIGHEST)
        summed = jnp.einsum("fki,ku->fui", products, dst_hot, precision=lax.Precision.HIGHEST)
        return summed.reshape(D, DST_DEV).astype(jnp.bfloat16)

    aggs = lax.map(forward_part, (parts, halo_in, dsts, srcs, tile_count, vals))
    agg_whole = aggs.transpose(1, 0, 2).reshape(D, DST_ALL)
    dst_feats = parts[:, :, :DST_DEV].transpose(1, 0, 2).reshape(D, DST_ALL)
    pre_act = jnp.dot(w_self, dst_feats, preferred_element_type=jnp.float32) + jnp.dot(w_neigh, agg_whole, preferred_element_type=jnp.float32) + bias_vec[:, None]
    sig_val = jax.nn.sigmoid(pre_act)
    activations = (pre_act * sig_val).astype(jnp.bfloat16)
    grad_pre = (cotangent.astype(jnp.float32) * sig_val * (1.0 + pre_act * (1.0 - sig_val))).astype(jnp.bfloat16)
    grad_w_self = jnp.dot(grad_pre, dst_feats.T, preferred_element_type=jnp.float32)
    grad_w_neigh = jnp.dot(grad_pre, agg_whole.T, preferred_element_type=jnp.float32)
    grad_bias = jnp.sum(grad_pre.astype(jnp.float32), axis=1)
    grad_self_in = jnp.dot(w_self.T, grad_pre, preferred_element_type=jnp.float32)
    grad_agg = jnp.dot(w_neigh.T, grad_pre, preferred_element_type=jnp.float32).astype(jnp.bfloat16)
    grad_aggs = grad_agg.reshape(D, N_DOM, DST_DEV).transpose(1, 0, 2)

    def backward_part(items):
        upstream_all, dst_ids, src_ids, count, values = items
        live_mask = (jnp.arange(TILES) < count).astype(jnp.float32)
        src_hot = (src_ids[:, None] == jnp.arange(tile_total)[None, :]).astype(jnp.float32) * live_mask[:, None]
        upstream = upstream_all.reshape(D, dst_tiles, 128)[:, dst_ids, :]
        back_terms = jnp.einsum("fki,kij->fkj", upstream.astype(jnp.float32), values.astype(jnp.float32), precision=lax.Precision.HIGHEST)
        placed = jnp.einsum("fkj,kt->ftj", back_terms, src_hot, precision=lax.Precision.HIGHEST)
        return placed.reshape(D, TABLE)

    grad_tables = lax.map(backward_part, (grad_aggs, dsts, srcs, tile_count, vals))
    owned_grad = grad_tables[:, :, :LOC_DEV]
    halo_grad = grad_tables[:, :, LOC_DEV:LOC_DEV + N_DOM * BND].reshape(N_DOM, D, N_DOM, BND)
    halo_back = halo_grad.transpose(2, 1, 0, 3).reshape(N_DOM, D, N_DOM * BND)
    hub_grad = grad_tables[:, :, LOC_DEV + N_DOM * BND:].reshape(N_DOM, D, N_DOM, HUB_DEV)
    hub_back = jnp.sum(hub_grad, axis=0).transpose(1, 0, 2)
    grads = jax.vmap(add_cols)(owned_grad, sends, halo_back)
    grads = jax.vmap(add_cols)(grads, hubs, hub_back)
    grads = grads.at[:, :, :DST_DEV].add(grad_self_in.reshape(D, N_DOM, DST_DEV).transpose(1, 0, 2))
    grad_feats = grads.transpose(1, 0, 2).reshape(D, SRC)
    return (activations, grad_feats, grad_w_self, grad_w_neigh, grad_bias)
```

```python
import functools

import jax
import jax.numpy as jnp
from jax import lax
from jax.experimental import pallas as pl
from jax.experimental.pallas import tpu as pltpu
from jax.sharding import PartitionSpec as P

MESH = pl.DeviceIdType.MESH
F32 = jnp.float32
BF16 = jnp.bfloat16
ZH = 4
LANES = 128
VMEM_LIMIT = 48 * 1024 * 1024


def remote(src, dst, send_sem, recv_sem, where):
    return pltpu.make_async_remote_copy(
        src_ref=src,
        dst_ref=dst,
        send_sem=send_sem,
        recv_sem=recv_sem,
        device_id=where,
        device_id_type=MESH,
    )


def place(near):
    dom = lax.axis_index("dom")
    feat = lax.axis_index("feat")
    return dom, feat, lax.div(feat, near), lax.rem(feat, near)


def aligned(index, size):
    return pl.ds(pl.multiple_of(index * size, size), size)


def column_hot(index_row):
    low = jnp.bitwise_and(index_row, LANES - 1)
    rows = lax.broadcasted_iota(jnp.int32, (LANES, LANES), 0)
    return jnp.where(rows == low, 1.0, 0.0).astype(BF16)


def distribute_kernel(
    doms,
    near,
    feats_ref,
    send_ref,
    hub_ref,
    w_self_ref,
    w_neigh_ref,
    bias_ref,
    cot_ref,
    table,
    wrow,
    wcol,
    x_self,
    cot_part,
    bias_part,
    picked,
    w_both,
    w_regrouped,
    bias_wide,
    halo_s,
    halo_r,
    hub_s,
    hub_r,
    far_s,
    far_r,
    near_s,
    near_r,
    col_s,
    col_r,
    share_s,
    share_r,
):
    rows = feats_ref.shape[0]
    own_tiles = feats_ref.shape[1] // LANES
    width = w_self_ref.shape[1]
    chunk = width // doms
    quarter = cot_ref.shape[1] // ZH
    feat_total = ZH * near
    dom, feat, zh, nr = place(near)

    barrier = pltpu.get_barrier_semaphore()
    for i in range(1, doms):
        pl.semaphore_signal(
            barrier, inc=1, device_id={"dom": lax.rem(dom + i, doms)}, device_id_type=MESH
        )
    for i in range(1, ZH):
        pl.semaphore_signal(
            barrier,
            inc=1,
            device_id={"feat": lax.rem(zh + i, ZH) * near + nr},
            device_id_type=MESH,
        )
    for i in range(1, near):
        pl.semaphore_signal(
            barrier,
            inc=1,
            device_id={"feat": zh * near + lax.rem(nr + i, near)},
            device_id_type=MESH,
        )

    @pl.when(nr != dom)
    def _():
        for i in range(1, ZH):
            pl.semaphore_signal(
                barrier,
                inc=1,
                device_id={"feat": lax.rem(zh + i, ZH) * near + dom},
                device_id_type=MESH,
            )

    for t in range(own_tiles):
        table[t] = feats_ref[:, t * LANES : (t + 1) * LANES]
    stacked = table[0:own_tiles].reshape(own_tiles * rows, LANES)
    for block in range(doms + 1):
        index_row = hub_ref[...] if block == doms else send_ref[block : block + 1, :]
        high = jnp.right_shift(index_row, 7)
        found = jnp.dot(stacked, column_hot(index_row), preferred_element_type=F32)
        found = found.reshape(own_tiles, rows, LANES)
        total = jnp.zeros((rows, LANES), F32)
        for t in range(own_tiles):
            total = total + jnp.where(high == t, found[t], 0.0)
        picked[block] = total.astype(BF16)

    common = (doms - 1) + (ZH - 1) + (near - 1)

    @pl.when(nr == dom)
    def _():
        pl.semaphore_wait(barrier, common + (ZH - 1) * (near - 1))

    @pl.when(nr != dom)
    def _():
        pl.semaphore_wait(barrier, common)

    def halo_copy(i, source, target):
        return remote(
            picked.at[target],
            table.at[own_tiles + source],
            halo_s.at[i],
            halo_r.at[i],
            {"dom": target},
        )

    def hub_copy(i, source, target):
        return remote(
            picked.at[doms],
            table.at[own_tiles + doms + source],
            hub_s.at[i],
            hub_r.at[i],
            {"dom": target},
        )

    for i in range(1, doms):
        target = lax.rem(dom + i, doms)
        halo_copy(i, dom, target).start()
        hub_copy(i, dom, target).start()

    def far_copies(i, source, target):
        where = {"feat": target * near + nr}
        return (
            remote(
                feats_ref.at[:, aligned(target, quarter)],
                x_self.at[source, nr],
                far_s.at[0, i],
                far_r.at[0, i],
                where,
            ),
            remote(
                w_both.at[:, :, aligned(dom, chunk)],
                wrow.at[:, source, :, aligned(dom, chunk)],
                far_s.at[1, i],
                far_r.at[1, i],
                where,
            ),
            remote(
                cot_ref.at[:, aligned(target, quarter)],
                cot_part.at[source],
                far_s.at[2, i],
                far_r.at[2, i],
                where,
            ),
            remote(
                bias_wide,
                bias_part.at[source],
                far_s.at[3, i],
                far_r.at[3, i],
                where,
            ),
        )

    w_both[0] = w_self_ref[...]
    w_both[1] = w_neigh_ref[...]
    spot = lax.broadcasted_iota(jnp.int32, (rows, rows), 0)
    lane = lax.broadcasted_iota(jnp.int32, (rows, rows), 1)
    bias_column = jnp.sum(jnp.where(spot == lane, bias_ref[...], 0.0), axis=1, keepdims=True)
    bias_wide[...] = jnp.broadcast_to(bias_column, (rows, LANES))
    for i in range(1, ZH):
        for copy in far_copies(i, zh, lax.rem(zh + i, ZH)):
            copy.start()

    lanes_at = lax.broadcasted_iota(jnp.int32, (rows, LANES), 1)
    for m, w_ref in enumerate((w_self_ref, w_neigh_ref)):
        for n in range(near):
            joined = jnp.zeros((rows, LANES), F32)
            for h in range(ZH):
                first = (h * near + n) * rows
                base, offset = first // LANES * LANES, first % LANES
                piece = w_ref[:, base : base + LANES].astype(F32)
                shift = (h * rows - offset) % LANES
                if shift:
                    piece = pltpu.roll(piece, shift, 1)
                inside = (lanes_at >= h * rows) & (lanes_at < (h + 1) * rows)
                joined = jnp.where(inside, piece, joined)
            w_regrouped[n, m] = joined.astype(BF16)

    def col_copy(i, target):
        return remote(
            w_regrouped.at[lax.rem(target, near)],
            wcol.at[:, zh, nr],
            col_s.at[i],
            col_r.at[zh],
            {"feat": target},
        )

    @pl.when(nr == dom)
    def _():
        for i in range(1, feat_total):
            col_copy(i, lax.rem(feat + i, feat_total)).start()
        wcol[:, zh, nr] = w_regrouped[nr]

    x_self[zh, nr] = feats_ref[:, aligned(zh, quarter)]
    wrow[:, zh, :, aligned(dom, chunk)] = w_both[:, :, aligned(dom, chunk)]
    cot_part[zh] = cot_ref[:, aligned(zh, quarter)]
    bias_part[zh] = bias_wide[...]
    table[own_tiles + dom] = picked[dom]
    table[own_tiles + doms + dom] = picked[doms]

    for i in range(1, ZH):
        for copy in far_copies(i, lax.rem(zh + ZH - i, ZH), zh):
            copy.wait_recv()

    def near_copy(i, source, target):
        return remote(
            x_self.at[:, source],
            x_self.at[:, source],
            near_s.at[i],
            near_r.at[i],
            {"feat": zh * near + target},
        )

    for i in range(1, near):
        near_copy(i, nr, lax.rem(nr + i, near)).start()

    for h in range(ZH):

        @pl.when((nr != dom) | (zh != h))
        def _():
            remote(
                w_regrouped.at[0],
                wcol.at[:, h, dom],
                col_s.at[0],
                col_r.at[h],
                {"feat": feat},
            ).wait_recv()

    def share_copies(i, source, target):
        where = {"dom": target}
        return (
            remote(
                wrow.at[:, :, :, aligned(source, chunk)],
                wrow.at[:, :, :, aligned(source, chunk)],
                share_s.at[0, i],
                share_r.at[0, i],
                where,
            ),
            remote(
                wcol.at[:, :, source],
                wcol.at[:, :, source],
                share_s.at[1, i],
                share_r.at[1, i],
                where,
            ),
        )

    for i in range(1, doms):
        for copy in share_copies(i, dom, lax.rem(dom + i, doms)):
            copy.start()

    for i in range(1, doms):
        source = lax.rem(dom + doms - i, doms)
        halo_copy(i, source, dom).wait_recv()
        hub_copy(i, source, dom).wait_recv()
    for i in range(1, near):
        near_copy(i, lax.rem(nr + near - i, near), nr).wait_recv()
    for i in range(1, doms):
        for copy in share_copies(i, lax.rem(dom + doms - i, doms), dom):
            copy.wait_recv()

    for i in range(1, doms):
        target = lax.rem(dom + i, doms)
        halo_copy(i, dom, target).wait_send()
        hub_copy(i, dom, target).wait_send()
        for copy in share_copies(i, dom, target):
            copy.wait_send()
    for i in range(1, ZH):
        for copy in far_copies(i, zh, lax.rem(zh + i, ZH)):
            copy.wait_send()
    for i in range(1, near):
        near_copy(i, nr, lax.rem(nr + i, near)).wait_send()

    @pl.when(nr == dom)
    def _():
        for i in range(1, feat_total):
            col_copy(i, lax.rem(feat + i, feat_total)).wait_send()


def aggregate_kernel(group, src_ref, dst_ref, count_ref, vals_ref, table_ref, out_ref, acc):
    step = pl.program_id(0)
    tiles = acc.shape[0]

    @pl.when(step == 0)
    def _():
        acc[...] = jnp.zeros_like(acc)

    count = count_ref[0]

    @pl.when(step * group < count)
    def _():
        parts = []
        for t in range(group):
            parts.append(
                lax.dot_general(
                    table_ref[src_ref[step * group + t]],
                    vals_ref[t],
                    (((1,), (1,)), ((), ())),
                    preferred_element_type=F32,
                )
            )
        for t in range(group):
            at = dst_ref[step * group + t]
            acc[at] += jnp.where(step * group + t < count, parts[t], 0.0)

    @pl.when(step == pl.num_programs(0) - 1)
    def _():
        for u in range(tiles):
            out_ref[:, u * LANES : (u + 1) * LANES] = acc[u].astype(BF16)


def spread_kernel(
    group, own_tiles, src_ref, dst_ref, count_ref, vals_ref, grad_ref, own_ref, away_ref, acc
):
    step = pl.program_id(0)

    @pl.when(step == 0)
    def _():
        acc[...] = jnp.zeros_like(acc)

    count = count_ref[0]

    @pl.when(step * group < count)
    def _():
        parts = []
        for t in range(group):
            parts.append(
                jnp.dot(
                    grad_ref[dst_ref[step * group + t]],
                    vals_ref[t],
                    preferred_element_type=F32,
                )
            )
        for t in range(group):
            at = src_ref[step * group + t]
            acc[at] += jnp.where(step * group + t < count, parts[t], 0.0)

    @pl.when(step == pl.num_programs(0) - 1)
    def _():
        own_ref[...] = acc[0:own_tiles]
        away_ref[...] = acc[own_tiles:].astype(BF16)


def dense_kernel(
    doms,
    near,
    agg_ref,
    x_self,
    wrow,
    wcol,
    cot_ref,
    bias_ref,
    act_out,
    grad_agg,
    grad_self,
    w_final,
    x_agg,
    g_part,
    g_all,
    act_part,
    in_parts,
    w_parts,
    w_got,
    w_sums,
    w_zh,
    far_s,
    far_r,
    near_s,
    near_r,
    back_s,
    back_r,
    sum_s,
    sum_r,
):
    rows, columns = agg_ref.shape
    quarter = columns // ZH
    halves = quarter // LANES
    width = rows * ZH * near
    mine = ZH * rows
    wide = 2 * width // doms
    dom, feat, zh, nr = place(near)

    barrier = pltpu.get_barrier_semaphore()
    for i in range(1, doms):
        pl.semaphore_signal(
            barrier, inc=1, device_id={"dom": lax.rem(dom + i, doms)}, device_id_type=MESH
        )
    for i in range(1, ZH):
        pl.semaphore_signal(
            barrier,
            inc=1,
            device_id={"feat": lax.rem(zh + i, ZH) * near + nr},
            device_id_type=MESH,
        )
    for i in range(1, near):
        pl.semaphore_signal(
            barrier,
            inc=1,
            device_id={"feat": zh * near + lax.rem(nr + i, near)},
            device_id_type=MESH,
        )
    pl.semaphore_wait(barrier, (doms - 1) + (ZH - 1) + (near - 1))

    def far_copy(i, source, target):
        return remote(
            agg_ref.at[:, aligned(target, quarter)],
            x_agg.at[source, nr],
            far_s.at[i],
            far_r.at[i],
            {"feat": target * near + nr},
        )

    for i in range(1, ZH):
        far_copy(i, zh, lax.rem(zh + i, ZH)).start()
    x_agg[zh, nr] = agg_ref[:, aligned(zh, quarter)]
    pre = jnp.dot(
        wrow[0].reshape(mine, width),
        x_self[...].reshape(width, quarter),
        preferred_element_type=F32,
    )
    for i in range(1, ZH):
        far_copy(i, lax.rem(zh + ZH - i, ZH), zh).wait_recv()

    def near_copy(which, buffer, i, source, target):
        return remote(
            buffer.at[:, source],
            buffer.at[:, source],
            near_s.at[which, i],
            near_r.at[which, i],
            {"feat": zh * near + target},
        )

    for i in range(1, near):
        near_copy(0, x_agg, i, nr, lax.rem(nr + i, near)).start()
    for i in range(1, near):
        near_copy(0, x_agg, i, lax.rem(nr + near - i, near), nr).wait_recv()

    pre = pre + jnp.dot(
        wrow[1].reshape(mine, width),
        x_agg[...].reshape(width, quarter),
        preferred_element_type=F32,
    )
    bias = jnp.concatenate([bias_ref[...].reshape(mine, LANES)] * halves, axis=1)
    pre = pre + bias
    sig = jax.nn.sigmoid(pre)
    grad = cot_ref[...].reshape(mine, quarter).astype(F32) * sig * (1.0 + pre * (1.0 - sig))
    grad = grad.astype(BF16)
    g_part[...] = grad
    g_all[:, nr] = grad.reshape(ZH, rows, quarter)
    for i in range(1, near):
        near_copy(1, g_all, i, nr, lax.rem(nr + i, near)).start()

    act = (pre * sig).astype(BF16).reshape(ZH, rows, quarter)
    for h in range(halves):
        act_part[:, h] = act[:, :, h * LANES : (h + 1) * LANES]

    def back_copy(which, source_buffer, target_buffer, i, source, target):
        return remote(
            source_buffer.at[target],
            target_buffer.at[aligned(source, halves)],
            back_s.at[which, i],
            back_r.at[which, i],
            {"feat": target * near + nr},
        )

    for i in range(1, ZH):
        back_copy(0, act_part, act_out, i, zh, lax.rem(zh + i, ZH)).start()
    act_out[aligned(zh, halves)] = act_part[zh]

    over_x = (((1,), (1,)), ((), ()))
    half_doms = doms // 2
    bias_sum = jnp.sum(grad.astype(F32), axis=1, keepdims=True)
    bias_sum = jnp.broadcast_to(bias_sum, (mine, LANES)).astype(BF16)
    for m, x_ref in enumerate((x_self, x_agg)):
        product = lax.dot_general(
            g_part[...],
            x_ref[...].reshape(width, quarter),
            over_x,
            preferred_element_type=F32,
        ).astype(BF16)
        for d in range(half_doms):
            w_parts[m * half_doms + d, :, 0:wide] = product[:, d * wide : (d + 1) * wide]
    for d in range(doms):
        w_parts[d, :, wide:] = bias_sum

    def sum_copy(i, source, target):
        return remote(
            w_parts.at[target],
            w_got.at[source],
            sum_s.at[0, i],
            sum_r.at[0, i],
            {"dom": target},
        )

    for i in range(1, doms):
        sum_copy(i, dom, lax.rem(dom + i, doms)).start()

    for i in range(1, near):
        near_copy(1, g_all, i, lax.rem(nr + near - i, near), nr).wait_recv()
    over_out = (((0,), (0,)), ((), ()))
    for m, (target_buffer) in ((1, grad_agg), (0, grad_self)):
        back = lax.dot_general(
            wcol[m].reshape(width, mine),
            g_all[...].reshape(width, quarter),
            over_out,
            preferred_element_type=F32,
        )
        back = back.astype(BF16).reshape(ZH, rows, quarter)
        for h in range(halves):
            in_parts[m, :, h] = back[:, :, h * LANES : (h + 1) * LANES]
        for i in range(1, ZH):
            back_copy(
                1 + m, in_parts.at[m], target_buffer, i, zh, lax.rem(zh + i, ZH)
            ).start()
        target_buffer[aligned(zh, halves)] = in_parts[m, zh]

    for i in range(1, doms):
        sum_copy(i, lax.rem(dom + doms - i, doms), dom).wait_recv()
    w_got[dom] = w_parts[dom]
    total = w_got[0].astype(F32)
    for d in range(1, doms):
        total = total + w_got[d].astype(F32)
    w_sums[...] = total.reshape(ZH, rows, wide + LANES)

    def zh_copy(i, source, target):
        return remote(
            w_sums.at[target],
            w_zh.at[source],
            sum_s.at[1, i],
            sum_r.at[1, i],
            {"feat": target * near + nr},
        )

    for i in range(1, ZH):
        zh_copy(i, zh, lax.rem(zh + i, ZH)).start()
    w_zh[zh] = w_sums[zh]
    for i in range(1, ZH):
        zh_copy(i, lax.rem(zh + ZH - i, ZH), zh).wait_recv()
    total = w_zh[0]
    for h in range(1, ZH):
        total = total + w_zh[h]
    w_final[...] = total

    for i in range(1, ZH):
        source = lax.rem(zh + ZH - i, ZH)
        back_copy(0, act_part, act_out, i, source, zh).wait_recv()
        back_copy(1, in_parts.at[0], grad_self, i, source, zh).wait_recv()
        back_copy(2, in_parts.at[1], grad_agg, i, source, zh).wait_recv()
    for i in range(1, ZH):
        target = lax.rem(zh + i, ZH)
        far_copy(i, zh, target).wait_send()
        back_copy(0, act_part, act_out, i, zh, target).wait_send()
        back_copy(1, in_parts.at[0], grad_self, i, zh, target).wait_send()
        back_copy(2, in_parts.at[1], grad_agg, i, zh, target).wait_send()
        zh_copy(i, zh, target).wait_send()
    for i in range(1, near):
        target = lax.rem(nr + i, near)
        near_copy(0, x_agg, i, nr, target).wait_send()
        near_copy(1, g_all, i, nr, target).wait_send()
    for i in range(1, doms):
        sum_copy(i, dom, lax.rem(dom + i, doms)).wait_send()


def return_kernel(
    doms, near, away_ref, w_final, returned, hub_parts, w_all, ret_s, ret_r, hub_s, hub_r, w_s, w_r
):
    dom, feat, zh, nr = place(near)
    wide = w_all.shape[2]
    barrier = pltpu.get_barrier_semaphore()
    for i in range(1, doms):
        pl.semaphore_signal(
            barrier, inc=1, device_id={"dom": lax.rem(dom + i, doms)}, device_id_type=MESH
        )
    pl.semaphore_wait(barrier, doms - 1)

    def copies(i, source, target):
        where = {"dom": target}
        return (
            remote(away_ref.at[target], returned.at[source], ret_s.at[i], ret_r.at[i], where),
            remote(
                away_ref.at[doms + target], hub_parts.at[source], hub_s.at[i], hub_r.at[i], where
            ),
            remote(w_final.at[:, 0:wide], w_all.at[source], w_s.at[i], w_r.at[i], where),
        )

    for i in range(1, doms):
        for copy in copies(i, dom, lax.rem(dom + i, doms)):
            copy.start()
    returned[dom] = away_ref[dom]
    hub_parts[dom] = away_ref[doms + dom]
    w_all[dom] = w_final[:, 0:wide]
    for i in range(1, doms):
        for copy in copies(i, lax.rem(dom + doms - i, doms), dom):
            copy.wait_recv()
    for i in range(1, doms):
        for copy in copies(i, dom, lax.rem(dom + i, doms)):
            copy.wait_send()


def finish_kernel(
    doms,
    own_ref,
    returned_ref,
    hub_ref,
    self_ref,
    send_rows,
    hub_rows,
    w_all,
    w_final,
    act_ref,
    act_out,
    feats_out,
    w_self_out,
    w_neigh_out,
    bias_out,
    masked,
):
    own_tiles, rows, _ = own_ref.shape
    dst_tiles = self_ref.shape[0]
    wide = w_all.shape[2]
    hots = []
    for block in range(doms + 1):
        if block == doms:
            index_row = hub_rows[...]
            total = hub_ref[0].astype(F32)
            for d in range(1, doms):
                total = total + hub_ref[d].astype(F32)
            values = total.astype(BF16)
        else:
            index_row = send_rows[block : block + 1, :]
            values = returned_ref[block]
        high = jnp.right_shift(index_row, 7)
        values = values.astype(F32)
        for t in range(own_tiles):
            masked[t, :, block * LANES : (block + 1) * LANES] = jnp.where(
                high == t, values, 0.0
            ).astype(BF16)
        hots.append(column_hot(index_row))
    hot = jnp.concatenate(hots, axis=1)
    added = lax.dot_general(
        masked[...].reshape(own_tiles * rows, (doms + 1) * LANES),
        hot,
        (((1,), (1,)), ((), ())),
        preferred_element_type=F32,
    ).reshape(own_tiles, rows, LANES)
    for t in range(own_tiles):
        total = own_ref[t] + added[t]
        if t < dst_tiles:
            total = total + self_ref[t].astype(F32)
        feats_out[:, t * LANES : (t + 1) * LANES] = total
    for t in range(dst_tiles):
        act_out[:, t * LANES : (t + 1) * LANES] = act_ref[t]
    half = doms // 2
    for d in range(half):
        w_self_out[:, d * wide : (d + 1) * wide] = w_all[d]
        w_neigh_out[:, d * wide : (d + 1) * wide] = w_all[half + d]
    spot = lax.broadcasted_iota(jnp.int32, (rows, LANES), 0)
    lane = lax.broadcasted_iota(jnp.int32, (rows, LANES), 1)
    picked = jnp.where(spot == lane, w_final[:, wide:], 0.0)
    bias_out[...] = jnp.sum(picked, axis=0, keepdims=True)[:, 0:rows]


def vmem(count):
    return [pl.BlockSpec(memory_space=pltpu.VMEM)] * count


def shape(dims, dtype):
    return jax.ShapeDtypeStruct(dims, dtype)


def body(
    doms,
    feat_total,
    node_feats,
    send_rows,
    hub_rows,
    tile_dst,
    tile_src,
    tile_count,
    tile_vals,
    w_self,
    w_neigh,
    bias_vec,
    cotangent,
):
    near = feat_total // ZH
    rows, own = node_feats.shape
    own_tiles = own // LANES
    columns = cotangent.shape[1]
    dst_tiles = columns // LANES
    quarter = columns // ZH
    width = w_self.shape[1]
    mine = ZH * rows
    wide = 2 * width // doms
    all_tiles = own_tiles + 2 * doms
    tile_total = tile_src.shape[0]
    dma = pltpu.SemaphoreType.DMA

    send_grid = send_rows.reshape(doms, LANES)
    hub_grid = hub_rows.reshape(1, LANES)

    def params(identity):
        return pltpu.CompilerParams(
            collective_id=identity, has_side_effects=True, vmem_limit_bytes=VMEM_LIMIT
        )

    table, wrow, wcol, x_self, cot_part, bias_part = pl.pallas_call(
        functools.partial(distribute_kernel, doms, near),
        name="distribute",
        out_shape=(
            shape((all_tiles, rows, LANES), BF16),
            shape((2, ZH, rows, width), BF16),
            shape((2, ZH, near, rows, mine), BF16),
            shape((ZH, near, rows, quarter), BF16),
            shape((ZH, rows, quarter), BF16),
            shape((ZH, rows, LANES), F32),
        ),
        in_specs=vmem(7),
        out_specs=tuple(vmem(6)),
        scratch_shapes=[
            pltpu.VMEM((doms + 1, rows, LANES), BF16),
            pltpu.VMEM((2, rows, width), BF16),
            pltpu.VMEM((near, 2, rows, mine), BF16),
            pltpu.VMEM((rows, LANES), F32),
            dma((doms,)),
            dma((doms,)),
            dma((doms,)),
            dma((doms,)),
            dma((4, ZH)),
            dma((4, ZH)),
            dma((near,)),
            dma((near,)),
            dma((feat_total,)),
            dma((ZH,)),
            dma((2, doms)),
            dma((2, doms)),
        ],
        compiler_params=params(0),
    )(node_feats, send_grid, hub_grid, w_self, w_neigh, bias_vec.reshape(1, rows), cotangent)

    group = min(32, tile_total)

    def live_block(step, src, dst, count):
        last = lax.div(count[0] + group - 1, group) - 1
        return (jnp.minimum(step, last), 0, 0)

    def whole(rank):
        return lambda step, src, dst, count: (0,) * rank

    vals_spec = pl.BlockSpec((group, LANES, LANES), live_block)
    local = pltpu.CompilerParams(vmem_limit_bytes=VMEM_LIMIT)

    aggregate = pl.pallas_call(
        functools.partial(aggregate_kernel, group),
        name="aggregate",
        out_shape=shape((rows, columns), BF16),
        grid_spec=pltpu.PrefetchScalarGridSpec(
            num_scalar_prefetch=3,
            grid=(tile_total // group,),
            in_specs=[vals_spec, pl.BlockSpec((all_tiles, rows, LANES), whole(3))],
            out_specs=pl.BlockSpec((rows, columns), whole(2)),
            scratch_shapes=[pltpu.VMEM((dst_tiles, rows, LANES), F32)],
        ),
        compiler_params=local,
    )(tile_src, tile_dst, tile_count, tile_vals, table)

    act_tiles, grad_agg, grad_self, w_final = pl.pallas_call(
        functools.partial(dense_kernel, doms, near),
        name="dense",
        out_shape=(
            shape((dst_tiles, rows, LANES), BF16),
            shape((dst_tiles, rows, LANES), BF16),
            shape((dst_tiles, rows, LANES), BF16),
            shape((rows, wide + LANES), F32),
        ),
        in_specs=vmem(6),
        out_specs=tuple(vmem(4)),
        scratch_shapes=[
            pltpu.VMEM((ZH, near, rows, quarter), BF16),
            pltpu.VMEM((mine, quarter), BF16),
            pltpu.VMEM((ZH, near, rows, quarter), BF16),
            pltpu.VMEM((ZH, quarter // LANES, rows, LANES), BF16),
            pltpu.VMEM((2, ZH, quarter // LANES, rows, LANES), BF16),
            pltpu.VMEM((doms, mine, wide + LANES), BF16),
            pltpu.VMEM((doms, mine, wide + LANES), BF16),
            pltpu.VMEM((ZH, rows, wide + LANES), F32),
            pltpu.VMEM((ZH, rows, wide + LANES), F32),
            dma((ZH,)),
            dma((ZH,)),
            dma((2, near)),
            dma((2, near)),
            dma((3, ZH)),
            dma((3, ZH)),
            dma((2, max(doms, ZH))),
            dma((2, max(doms, ZH))),
        ],
        compiler_params=params(1),
    )(aggregate, x_self, wrow, wcol, cot_part, bias_part)

    grad_own, away = pl.pallas_call(
        functools.partial(spread_kernel, group, own_tiles),
        name="spread",
        out_shape=(
            shape((own_tiles, rows, LANES), F32),
            shape((2 * doms, rows, LANES), BF16),
        ),
        grid_spec=pltpu.PrefetchScalarGridSpec(
            num_scalar_prefetch=3,
            grid=(tile_total // group,),
            in_specs=[vals_spec, pl.BlockSpec((dst_tiles, rows, LANES), whole(3))],
            out_specs=(
                pl.BlockSpec((own_tiles, rows, LANES), whole(3)),
                pl.BlockSpec((2 * doms, rows, LANES), whole(3)),
            ),
            scratch_shapes=[pltpu.VMEM((all_tiles, rows, LANES), F32)],
        ),
        compiler_params=local,
    )(tile_src, tile_dst, tile_count, tile_vals, grad_agg)

    returned, hub_parts, w_all = pl.pallas_call(
        functools.partial(return_kernel, doms, near),
        name="give_back",
        out_shape=(
            shape((doms, rows, LANES), BF16),
            shape((doms, rows, LANES), BF16),
            shape((doms, rows, wide), F32),
        ),
        in_specs=vmem(2),
        out_specs=tuple(vmem(3)),
        scratch_shapes=[dma((doms,)) for _ in range(6)],
        compiler_params=params(2),
    )(away, w_final)

    activations, grad_feats, grad_w_self, grad_w_neigh, grad_bias = pl.pallas_call(
        functools.partial(finish_kernel, doms),
        name="finish",
        out_shape=(
            shape((rows, columns), BF16),
            shape((rows, own), F32),
            shape((rows, width), F32),
            shape((rows, width), F32),
            shape((1, rows), F32),
        ),
        in_specs=vmem(9),
        out_specs=tuple(vmem(5)),
        scratch_shapes=[pltpu.VMEM((own_tiles, rows, (doms + 1) * LANES), BF16)],
        compiler_params=local,
    )(
        grad_own,
        returned,
        hub_parts,
        grad_self,
        send_grid,
        hub_grid,
        w_all,
        w_final,
        act_tiles,
    )
    return (activations, grad_feats, grad_w_self, grad_w_neigh, grad_bias.reshape(rows))


def solution(mesh):
    return jax.shard_map(
        functools.partial(body, mesh.shape["dom"], mesh.shape["feat"]),
        mesh=mesh,
        in_specs=(
            P("feat", "dom"),
            P("dom"),
            P("dom"),
            P("dom"),
            P("dom"),
            P("dom"),
            P("dom", None, None),
            P("feat", None),
            P("feat", None),
            P("feat"),
            P("feat", "dom"),
        ),
        out_specs=(P("feat", "dom"), P("feat", "dom"), P("feat", None), P("feat", None), P("feat")),
        check_vma=False,
    )
```

```python
import functools

import jax
import jax.numpy as jnp
from jax import lax
from jax.experimental import pallas as pl
from jax.experimental.pallas import tpu as pltpu
from jax.sharding import PartitionSpec as P

MESH = pl.DeviceIdType.MESH
F32 = jnp.float32
BF16 = jnp.bfloat16
ZH = 4
LANES = 128
VMEM_LIMIT = 60 * 1024 * 1024
SUB = 64


def remote(src, dst, send_sem, recv_sem, where):
    return pltpu.make_async_remote_copy(
        src_ref=src,
        dst_ref=dst,
        send_sem=send_sem,
        recv_sem=recv_sem,
        device_id=where,
        device_id_type=MESH,
    )


def place(near):
    dom = lax.axis_index("dom")
    feat = lax.axis_index("feat")
    return dom, feat, lax.div(feat, near), lax.rem(feat, near)


def aligned(index, size):
    return pl.ds(pl.multiple_of(index * size, size), size)


def column_hot(index_row):
    low = jnp.bitwise_and(index_row, LANES - 1)
    rows = lax.broadcasted_iota(jnp.int32, (LANES, LANES), 0)
    return jnp.where(rows == low, 1.0, 0.0).astype(BF16)


def link_tiles(keys, count, links, first_row, last_row):
    blocks = keys.shape[0]
    none = blocks * LANES
    above = lax.broadcasted_iota(jnp.int32, (LANES, LANES), 0)
    lane = lax.broadcasted_iota(jnp.int32, (LANES, LANES), 1)
    spread = [
        jnp.transpose(jnp.broadcast_to(keys[b : b + 1, :], (LANES, LANES))) for b in range(blocks)
    ]
    for c in range(blocks):
        best = jnp.full((1, LANES), -1, jnp.int32)
        for b in range(c + 1):
            same = spread[b] == keys[c : c + 1, :]
            if b == c:
                same = same & (above < lane)
            found = jnp.where(same, above + b * LANES, -1)
            best = jnp.maximum(best, jnp.max(found, axis=0, keepdims=True))
        links[first_row + c : first_row + c + 1, :] = jnp.where(best < 0, none, best)
    best = jnp.full((1, LANES), -1, jnp.int32)
    for b in range(blocks):
        same = (spread[b] == lane) & (above + b * LANES < count)
        found = jnp.where(same, above + b * LANES, -1)
        best = jnp.maximum(best, jnp.max(found, axis=0, keepdims=True))
    links[last_row : last_row + 1, :] = jnp.where(best < 0, none, best)


def layer_kernel(
    doms,
    near,
    count_ref,
    feats_hbm,
    send_hbm,
    hub_hbm,
    dst_hbm,
    src_hbm,
    vals_hbm,
    w_self_hbm,
    w_neigh_hbm,
    bias_hbm,
    cot_hbm,
    act_out,
    grad_own,
    returned,
    w_all,
    w_final,
    feats,
    send,
    hub,
    dst,
    src,
    vals,
    flipped,
    runs,
    links,
    links_s,
    table,
    picked,
    w_both,
    w_regrouped,
    bias,
    bias_wide,
    bias_part,
    cot,
    cot_part,
    wrow,
    wcol,
    x_self,
    x_agg,
    agg,
    g_part,
    g_all,
    act_part,
    in_parts,
    grad_agg,
    grad_self,
    away,
    w_parts,
    w_got,
    w_sums,
    w_zh,
    load_sem,
    vals_sem,
    link_sem,
    halo_s,
    halo_r,
    far_s,
    far_r,
    near_s,
    near_r,
    col_s,
    col_r,
    share_s,
    share_r,
    agg_s,
    agg_r,
    back_s,
    back_r,
    sum_s,
    sum_r,
    ret_s,
    ret_r,
):
    rows = feats.shape[0]
    own_tiles = feats.shape[1] // LANES
    columns = cot.shape[1]
    dst_tiles = columns // LANES
    quarter = columns // ZH
    halves = quarter // LANES
    width = w_both.shape[2]
    chunk = width // doms
    mine = ZH * rows
    wide = 2 * width // doms
    tile_total = vals.shape[0]
    key_rows = tile_total // LANES
    feat_total = ZH * near
    dom, feat, zh, nr = place(near)

    barrier = pltpu.get_barrier_semaphore()
    for i in range(1, doms):
        pl.semaphore_signal(
            barrier, inc=1, device_id={"dom": lax.rem(dom + i, doms)}, device_id_type=MESH
        )
    for i in range(1, ZH):
        pl.semaphore_signal(
            barrier,
            inc=1,
            device_id={"feat": lax.rem(zh + i, ZH) * near + nr},
            device_id_type=MESH,
        )
    for i in range(1, near):
        pl.semaphore_signal(
            barrier,
            inc=1,
            device_id={"feat": zh * near + lax.rem(nr + i, near)},
            device_id_type=MESH,
        )

    @pl.when(nr != dom)
    def _():
        for i in range(1, ZH):
            pl.semaphore_signal(
                barrier,
                inc=1,
                device_id={"feat": lax.rem(zh + i, ZH) * near + dom},
                device_id_type=MESH,
            )

    loads = [
        pltpu.make_async_copy(source, target, load_sem.at[i])
        for i, (source, target) in enumerate(
            (
                (feats_hbm, feats),
                (send_hbm, send),
                (hub_hbm, hub),
                (dst_hbm, dst),
                (src_hbm, src),
                (w_self_hbm, w_both.at[0]),
                (w_neigh_hbm, w_both.at[1]),
                (bias_hbm, bias),
                (cot_hbm, cot),
            )
        )
    ]
    for load in loads:
        load.start()
    blocks = vals_sem.shape[0]
    block = tile_total // blocks
    vals_loads = [
        pltpu.make_async_copy(
            vals_hbm.at[b * block : (b + 1) * block],
            vals.at[b * block : (b + 1) * block],
            vals_sem.at[b],
        )
        for b in range(blocks)
    ]
    for load in vals_loads:
        load.start()
    for load in loads:
        load.wait()

    for t in range(own_tiles):
        table[t] = feats[:, t * LANES : (t + 1) * LANES]
    stacked = table[0:own_tiles].reshape(own_tiles * rows, LANES)
    for reader in range(doms + 1):
        index_row = hub[...] if reader == doms else send[reader : reader + 1, :]
        high = jnp.right_shift(index_row, 7)
        found = jnp.dot(stacked, column_hot(index_row), preferred_element_type=F32)
        found = found.reshape(own_tiles, rows, LANES)
        total = jnp.zeros((rows, LANES), F32)
        for t in range(own_tiles):
            total = total + jnp.where(high == t, found[t], 0.0)
        total = total.astype(BF16)
        if reader < doms:
            picked[reader, 0] = total
        else:
            for d in range(doms):
                picked[d, 1] = total

    common = (doms - 1) + (ZH - 1) + (near - 1)

    @pl.when(nr == dom)
    def _():
        pl.semaphore_wait(barrier, common + (ZH - 1) * (near - 1))

    @pl.when(nr != dom)
    def _():
        pl.semaphore_wait(barrier, common)

    def halo_copy(i, source, target):
        return remote(
            picked.at[target],
            table.at[pl.ds(own_tiles + 2 * source, 2)],
            halo_s.at[i],
            halo_r.at[i],
            {"dom": target},
        )

    for i in range(1, doms):
        halo_copy(i, dom, lax.rem(dom + i, doms)).start()

    def far_copy(which, i, source, target):
        sources = (
            feats.at[:, aligned(target, quarter)],
            w_both.at[:, :, aligned(dom, chunk)],
            cot.at[:, aligned(target, quarter)],
            bias_wide,
        )
        targets = (
            x_self.at[source, nr],
            wrow.at[:, source, :, aligned(dom, chunk)],
            cot_part.at[source],
            bias_part.at[source],
        )
        return remote(
            sources[which],
            targets[which],
            far_s.at[which, i],
            far_r.at[which, i],
            {"feat": target * near + nr},
        )

    for i in range(1, ZH):
        far_copy(0, i, zh, lax.rem(zh + i, ZH)).start()
    for i in range(1, ZH):
        far_copy(1, i, zh, lax.rem(zh + i, ZH)).start()

    lanes_at = lax.broadcasted_iota(jnp.int32, (rows, LANES), 1)
    for m in range(2):
        for n in range(near):
            joined = jnp.zeros((rows, LANES), F32)
            for h in range(ZH):
                first = (h * near + n) * rows
                base, offset = first // LANES * LANES, first % LANES
                piece = w_both[m, :, base : base + LANES].astype(F32)
                shift = (h * rows - offset) % LANES
                if shift:
                    piece = pltpu.roll(piece, shift, 1)
                inside = (lanes_at >= h * rows) & (lanes_at < (h + 1) * rows)
                joined = jnp.where(inside, piece, joined)
            w_regrouped[n, m] = joined.astype(BF16)

    def col_copy(i, target):
        return remote(
            w_regrouped.at[lax.rem(target, near)],
            wcol.at[:, zh, nr],
            col_s.at[i],
            col_r.at[zh],
            {"feat": target},
        )

    @pl.when(nr == dom)
    def _():
        for i in range(1, feat_total):
            col_copy(i, lax.rem(feat + i, feat_total)).start()
        wcol[:, zh, nr] = w_regrouped[nr]

    spot = lax.broadcasted_iota(jnp.int32, (rows, rows), 0)
    lane = lax.broadcasted_iota(jnp.int32, (rows, rows), 1)
    bias_column = jnp.sum(jnp.where(spot == lane, bias[...], 0.0), axis=1, keepdims=True)
    bias_wide[...] = jnp.broadcast_to(bias_column, (rows, LANES))
    for which in (2, 3):
        for i in range(1, ZH):
            far_copy(which, i, zh, lax.rem(zh + i, ZH)).start()

    x_self[zh, nr] = feats[:, aligned(zh, quarter)]
    wrow[:, zh, :, aligned(dom, chunk)] = w_both[:, :, aligned(dom, chunk)]
    cot_part[zh] = cot[:, aligned(zh, quarter)]
    bias_part[zh] = bias_wide[...]
    table[pl.ds(own_tiles + 2 * dom, 2)] = picked[dom]

    given = src[...]
    outside = given - own_tiles
    placed = own_tiles + 2 * lax.rem(outside, doms) + lax.div(outside, doms)
    placed = jnp.where(outside < 0, given, placed)
    key_dst = dst[...]
    links[0:key_rows, :] = key_dst
    links[key_rows : 2 * key_rows, :] = placed
    prev_dst, prev_src, last_dst = 2 * key_rows, 3 * key_rows, 4 * key_rows
    last_src = last_dst + 1
    link_tiles(key_dst, count_ref[0], links, prev_dst, last_dst)
    link_tiles(placed, count_ref[0], links, prev_src, last_src)
    link_copy = pltpu.make_async_copy(links, links_s, link_sem)
    link_copy.start()

    def flip(b):
        vals_loads[b].wait()

        def some(j, carry):
            for t in range(8):
                k = b * block + j * 8 + t
                flipped[k] = jnp.transpose(vals[k])
            return carry

        lax.fori_loop(0, block // 8, some, 0)

    early = blocks // 4
    for b in range(early):
        flip(b)

    for which in (0, 1):
        for i in range(1, ZH):
            far_copy(which, i, lax.rem(zh + ZH - i, ZH), zh).wait_recv()

    def near_copy(which, i, source, target):
        buffer = (x_self, x_agg, g_all)[which]
        return remote(
            buffer.at[:, source],
            buffer.at[:, source],
            near_s.at[which, i],
            near_r.at[which, i],
            {"feat": zh * near + target},
        )

    for i in range(1, near):
        near_copy(0, i, nr, lax.rem(nr + i, near)).start()

    for h in range(ZH):

        @pl.when((nr != dom) | (zh != h))
        def _():
            remote(
                w_regrouped.at[0],
                wcol.at[:, h, dom],
                col_s.at[0],
                col_r.at[h],
                {"feat": feat},
            ).wait_recv()

    def share_copy(which, i, source, target):
        part = wcol.at[:, :, source] if which else wrow.at[:, :, :, aligned(source, chunk)]
        return remote(part, part, share_s.at[which, i], share_r.at[which, i], {"dom": target})

    for which in (0, 1):
        for i in range(1, doms):
            share_copy(which, i, dom, lax.rem(dom + i, doms)).start()

    for b in range(early, blocks):
        flip(b)
    link_copy.wait()
    for i in range(1, doms):
        halo_copy(i, lax.rem(dom + doms - i, doms), dom).wait_recv()

    runs[tile_total] = jnp.zeros((rows, LANES), F32)

    def chain(left, left_row, tiles, prev_row):
        def some(j, carry):
            row = lax.div(j * SUB, LANES)
            start = lax.rem(j * SUB, LANES)
            for t in range(SUB):
                product = jnp.dot(
                    left[links_s[left_row + row, start + t]],
                    tiles[j * SUB + t],
                    preferred_element_type=F32,
                )
                runs[j * SUB + t] = runs[links_s[prev_row + row, start + t]] + product
            return carry

        lax.fori_loop(0, tile_total // SUB, some, 0)

    chain(table, key_rows, flipped, prev_dst)
    for u in range(dst_tiles):
        agg[:, u * LANES : (u + 1) * LANES] = runs[links_s[last_dst, u]].astype(BF16)

    def agg_copy(i, source, target):
        return remote(
            agg.at[:, aligned(target, quarter)],
            x_agg.at[source, nr],
            agg_s.at[i],
            agg_r.at[i],
            {"feat": target * near + nr},
        )

    for i in range(1, ZH):
        agg_copy(i, zh, lax.rem(zh + i, ZH)).start()
    x_agg[zh, nr] = agg[:, aligned(zh, quarter)]
    for i in range(1, near):
        near_copy(0, i, lax.rem(nr + near - i, near), nr).wait_recv()
    for i in range(1, doms):
        share_copy(0, i, lax.rem(dom + doms - i, doms), dom).wait_recv()
    pre = jnp.dot(
        wrow[0].reshape(mine, width),
        x_self[...].reshape(width, quarter),
        preferred_element_type=F32,
    )
    for i in range(1, ZH):
        agg_copy(i, lax.rem(zh + ZH - i, ZH), zh).wait_recv()
    for i in range(1, near):
        near_copy(1, i, nr, lax.rem(nr + i, near)).start()
    for which in (2, 3):
        for i in range(1, ZH):
            far_copy(which, i, lax.rem(zh + ZH - i, ZH), zh).wait_recv()
    bias_all = jnp.concatenate([bias_part[...].reshape(mine, LANES)] * halves, axis=1)
    pre = pre + bias_all
    for i in range(1, near):
        near_copy(1, i, lax.rem(nr + near - i, near), nr).wait_recv()
    pre = pre + jnp.dot(
        wrow[1].reshape(mine, width),
        x_agg[...].reshape(width, quarter),
        preferred_element_type=F32,
    )
    sig = jax.nn.sigmoid(pre)
    grad = cot_part[...].reshape(mine, quarter).astype(F32) * sig * (1.0 + pre * (1.0 - sig))
    grad = grad.astype(BF16)
    g_part[...] = grad
    g_all[:, nr] = grad.reshape(ZH, rows, quarter)
    for i in range(1, near):
        near_copy(2, i, nr, lax.rem(nr + i, near)).start()

    act = (pre * sig).astype(BF16).reshape(ZH, rows, quarter)
    for h in range(halves):
        act_part[:, h] = act[:, :, h * LANES : (h + 1) * LANES]

    def back_copy(which, i, source, target):
        source_buffer = (act_part, in_parts.at[0], in_parts.at[1])[which]
        target_buffer = (act_out, grad_self, grad_agg)[which]
        return remote(
            source_buffer.at[target],
            target_buffer.at[aligned(source, halves)],
            back_s.at[which, i],
            back_r.at[which, i],
            {"feat": target * near + nr},
        )

    over_x = (((1,), (1,)), ((), ()))
    half_doms = doms // 2
    bias_sum = jnp.sum(grad.astype(F32), axis=1, keepdims=True)
    bias_sum = jnp.broadcast_to(bias_sum, (mine, LANES)).astype(BF16)
    for m, x_ref in enumerate((x_self, x_agg)):
        product = lax.dot_general(
            g_part[...],
            x_ref[...].reshape(width, quarter),
            over_x,
            preferred_element_type=F32,
        ).astype(BF16)
        for d in range(half_doms):
            w_parts[m * half_doms + d, :, 0:wide] = product[:, d * wide : (d + 1) * wide]
    for d in range(doms):
        w_parts[d, :, wide:] = bias_sum

    def sum_copy(i, source, target):
        return remote(
            w_parts.at[target],
            w_got.at[source],
            sum_s.at[0, i],
            sum_r.at[0, i],
            {"dom": target},
        )

    for i in range(1, doms):
        sum_copy(i, dom, lax.rem(dom + i, doms)).start()
    for i in range(1, doms):
        share_copy(1, i, lax.rem(dom + doms - i, doms), dom).wait_recv()

    for i in range(1, near):
        near_copy(2, i, lax.rem(nr + near - i, near), nr).wait_recv()
    over_out = (((0,), (0,)), ((), ()))
    for m, target_buffer in ((1, grad_agg), (0, grad_self)):
        back = lax.dot_general(
            wcol[m].reshape(width, mine),
            g_all[...].reshape(width, quarter),
            over_out,
            preferred_element_type=F32,
        )
        back = back.astype(BF16).reshape(ZH, rows, quarter)
        for h in range(halves):
            in_parts[m, :, h] = back[:, :, h * LANES : (h + 1) * LANES]
        for i in range(1, ZH):
            back_copy(1 + m, i, zh, lax.rem(zh + i, ZH)).start()
        target_buffer[aligned(zh, halves)] = in_parts[m, zh]
    for i in range(1, ZH):
        back_copy(0, i, zh, lax.rem(zh + i, ZH)).start()
    act_out[aligned(zh, halves)] = act_part[zh]

    for i in range(1, doms):
        sum_copy(i, lax.rem(dom + doms - i, doms), dom).wait_recv()
    w_got[dom] = w_parts[dom]
    total = w_got[0].astype(F32)
    for d in range(1, doms):
        total = total + w_got[d].astype(F32)
    w_sums[...] = total.reshape(ZH, rows, wide + LANES)

    def zh_copy(i, source, target):
        return remote(
            w_sums.at[target],
            w_zh.at[source],
            sum_s.at[1, i],
            sum_r.at[1, i],
            {"feat": target * near + nr},
        )

    for i in range(1, ZH):
        zh_copy(i, zh, lax.rem(zh + i, ZH)).start()
    w_zh[zh] = w_sums[zh]

    for i in range(1, ZH):
        back_copy(2, i, lax.rem(zh + ZH - i, ZH), zh).wait_recv()
    chain(grad_agg, 0, vals, prev_src)

    for t in range(2 * doms):
        away[t] = runs[links_s[last_src, own_tiles + t]].astype(BF16)

    def return_copy(which, i, source, target):
        pieces = ((away.at[pl.ds(2 * target, 2)], returned), (w_final.at[:, 0:wide], w_all))
        part, buffer = pieces[which]
        return remote(
            part, buffer.at[source], ret_s.at[which, i], ret_r.at[which, i], {"dom": target}
        )

    for i in range(1, doms):
        return_copy(0, i, dom, lax.rem(dom + i, doms)).start()
    for i in range(1, ZH):
        zh_copy(i, lax.rem(zh + ZH - i, ZH), zh).wait_recv()
    total = w_zh[0]
    for h in range(1, ZH):
        total = total + w_zh[h]
    w_final[...] = total
    for i in range(1, doms):
        return_copy(1, i, dom, lax.rem(dom + i, doms)).start()
    returned[dom] = away[pl.ds(2 * dom, 2)]
    w_all[dom] = w_final[:, 0:wide]

    for i in range(1, ZH):
        back_copy(1, i, lax.rem(zh + ZH - i, ZH), zh).wait_recv()
    for t in range(own_tiles):
        total = runs[links_s[last_src, t]]
        if t < dst_tiles:
            total = total + grad_self[t].astype(F32)
        grad_own[t] = total

    for i in range(1, ZH):
        back_copy(0, i, lax.rem(zh + ZH - i, ZH), zh).wait_recv()
    for i in range(1, doms):
        source = lax.rem(dom + doms - i, doms)
        return_copy(0, i, source, dom).wait_recv()
        return_copy(1, i, source, dom).wait_recv()

    for i in range(1, doms):
        target = lax.rem(dom + i, doms)
        halo_copy(i, dom, target).wait_send()
        sum_copy(i, dom, target).wait_send()
        for which in (0, 1):
            share_copy(which, i, dom, target).wait_send()
            return_copy(which, i, dom, target).wait_send()
    for i in range(1, ZH):
        target = lax.rem(zh + i, ZH)
        for which in range(4):
            far_copy(which, i, zh, target).wait_send()
        for which in range(3):
            back_copy(which, i, zh, target).wait_send()
        agg_copy(i, zh, target).wait_send()
        zh_copy(i, zh, target).wait_send()
    for i in range(1, near):
        for which in range(3):
            near_copy(which, i, nr, lax.rem(nr + i, near)).wait_send()

    @pl.when(nr == dom)
    def _():
        for i in range(1, feat_total):
            col_copy(i, lax.rem(feat + i, feat_total)).wait_send()


def finish_kernel(
    doms,
    own_ref,
    returned_ref,
    send_rows,
    hub_rows,
    w_all,
    w_final,
    act_ref,
    act_out,
    feats_out,
    w_self_out,
    w_neigh_out,
    bias_out,
    masked,
):
    own_tiles, rows, _ = own_ref.shape
    dst_tiles = act_ref.shape[0]
    wide = w_all.shape[2]
    hots = []
    for block in range(doms + 1):
        if block == doms:
            index_row = hub_rows[...]
            total = returned_ref[0, 1].astype(F32)
            for d in range(1, doms):
                total = total + returned_ref[d, 1].astype(F32)
            values = total.astype(BF16)
        else:
            index_row = send_rows[block : block + 1, :]
            values = returned_ref[block, 0]
        high = jnp.right_shift(index_row, 7)
        values = values.astype(F32)
        for t in range(own_tiles):
            masked[t, :, block * LANES : (block + 1) * LANES] = jnp.where(
                high == t, values, 0.0
            ).astype(BF16)
        hots.append(column_hot(index_row))
    hot = jnp.concatenate(hots, axis=1)
    added = lax.dot_general(
        masked[...].reshape(own_tiles * rows, (doms + 1) * LANES),
        hot,
        (((1,), (1,)), ((), ())),
        preferred_element_type=F32,
    ).reshape(own_tiles, rows, LANES)
    for t in range(own_tiles):
        feats_out[:, t * LANES : (t + 1) * LANES] = own_ref[t] + added[t]
    for t in range(dst_tiles):
        act_out[:, t * LANES : (t + 1) * LANES] = act_ref[t]
    half = doms // 2
    for d in range(half):
        w_self_out[:, d * wide : (d + 1) * wide] = w_all[d]
        w_neigh_out[:, d * wide : (d + 1) * wide] = w_all[half + d]
    spot = lax.broadcasted_iota(jnp.int32, (rows, LANES), 0)
    lane = lax.broadcasted_iota(jnp.int32, (rows, LANES), 1)
    picked = jnp.where(spot == lane, w_final[:, wide:], 0.0)
    bias_out[...] = jnp.sum(picked, axis=0, keepdims=True)[:, 0:rows]


def shape(dims, dtype):
    return jax.ShapeDtypeStruct(dims, dtype)


def body(
    doms,
    feat_total,
    node_feats,
    send_rows,
    hub_rows,
    tile_dst,
    tile_src,
    tile_count,
    tile_vals,
    w_self,
    w_neigh,
    bias_vec,
    cotangent,
):
    near = feat_total // ZH
    rows, own = node_feats.shape
    own_tiles = own // LANES
    columns = cotangent.shape[1]
    dst_tiles = columns // LANES
    quarter = columns // ZH
    halves = quarter // LANES
    width = w_self.shape[1]
    mine = ZH * rows
    wide = 2 * width // doms
    all_tiles = own_tiles + 2 * doms
    tile_total = tile_src.shape[0]
    key_rows = tile_total // LANES
    dma = pltpu.SemaphoreType.DMA
    in_vmem = pl.BlockSpec(memory_space=pltpu.VMEM)

    send_grid = send_rows.reshape(doms, LANES)
    hub_grid = hub_rows.reshape(1, LANES)

    act_tiles, grad_own, returned, w_all, w_final = pl.pallas_call(
        functools.partial(layer_kernel, doms, near),
        name="layer",
        out_shape=(
            shape((dst_tiles, rows, LANES), BF16),
            shape((own_tiles, rows, LANES), F32),
            shape((doms, 2, rows, LANES), BF16),
            shape((doms, rows, wide), F32),
            shape((rows, wide + LANES), F32),
        ),
        in_specs=[pl.BlockSpec(memory_space=pltpu.SMEM)]
        + [pl.BlockSpec(memory_space=pltpu.HBM)] * 10,
        out_specs=(in_vmem,) * 5,
        scratch_shapes=[
            pltpu.VMEM((rows, own), BF16),
            pltpu.VMEM((doms, LANES), jnp.int32),
            pltpu.VMEM((1, LANES), jnp.int32),
            pltpu.VMEM((key_rows, LANES), jnp.int32),
            pltpu.VMEM((key_rows, LANES), jnp.int32),
            pltpu.VMEM((tile_total, LANES, LANES), BF16),
            pltpu.VMEM((tile_total, LANES, LANES), BF16),
            pltpu.VMEM((tile_total + 1, rows, LANES), F32),
            pltpu.VMEM((4 * key_rows + 8, LANES), jnp.int32),
            pltpu.SMEM((4 * key_rows + 8, LANES), jnp.int32),
            pltpu.VMEM((all_tiles, rows, LANES), BF16),
            pltpu.VMEM((doms, 2, rows, LANES), BF16),
            pltpu.VMEM((2, rows, width), BF16),
            pltpu.VMEM((near, 2, rows, mine), BF16),
            pltpu.VMEM((1, rows), F32),
            pltpu.VMEM((rows, LANES), F32),
            pltpu.VMEM((ZH, rows, LANES), F32),
            pltpu.VMEM((rows, columns), BF16),
            pltpu.VMEM((ZH, rows, quarter), BF16),
            pltpu.VMEM((2, ZH, rows, width), BF16),
            pltpu.VMEM((2, ZH, near, rows, mine), BF16),
            pltpu.VMEM((ZH, near, rows, quarter), BF16),
            pltpu.VMEM((ZH, near, rows, quarter), BF16),
            pltpu.VMEM((rows, columns), BF16),
            pltpu.VMEM((mine, quarter), BF16),
            pltpu.VMEM((ZH, near, rows, quarter), BF16),
            pltpu.VMEM((ZH, halves, rows, LANES), BF16),
            pltpu.VMEM((2, ZH, halves, rows, LANES), BF16),
            pltpu.VMEM((dst_tiles, rows, LANES), BF16),
            pltpu.VMEM((dst_tiles, rows, LANES), BF16),
            pltpu.VMEM((2 * doms, rows, LANES), BF16),
            pltpu.VMEM((doms, mine, wide + LANES), BF16),
            pltpu.VMEM((doms, mine, wide + LANES), BF16),
            pltpu.VMEM((ZH, rows, wide + LANES), F32),
            pltpu.VMEM((ZH, rows, wide + LANES), F32),
            dma((9,)),
            dma((16,)),
            dma,
            dma((doms,)),
            dma((doms,)),
            dma((4, ZH)),
            dma((4, ZH)),
            dma((3, near)),
            dma((3, near)),
            dma((feat_total,)),
            dma((ZH,)),
            dma((2, doms)),
            dma((2, doms)),
            dma((ZH,)),
            dma((ZH,)),
            dma((3, ZH)),
            dma((3, ZH)),
            dma((2, max(doms, ZH))),
            dma((2, max(doms, ZH))),
            dma((2, doms)),
            dma((2, doms)),
        ],
        compiler_params=pltpu.CompilerParams(
            collective_id=0, has_side_effects=True, vmem_limit_bytes=VMEM_LIMIT
        ),
    )(
        tile_count,
        node_feats,
        send_grid,
        hub_grid,
        tile_dst.reshape(key_rows, LANES),
        tile_src.reshape(key_rows, LANES),
        tile_vals,
        w_self,
        w_neigh,
        bias_vec.reshape(1, rows),
        cotangent,
    )

    activations, grad_feats, grad_w_self, grad_w_neigh, grad_bias = pl.pallas_call(
        functools.partial(finish_kernel, doms),
        name="finish",
        out_shape=(
            shape((rows, columns), BF16),
            shape((rows, own), F32),
            shape((rows, width), F32),
            shape((rows, width), F32),
            shape((1, rows), F32),
        ),
        in_specs=[in_vmem] * 7,
        out_specs=(in_vmem,) * 5,
        scratch_shapes=[pltpu.VMEM((own_tiles, rows, (doms + 1) * LANES), BF16)],
        compiler_params=pltpu.CompilerParams(vmem_limit_bytes=VMEM_LIMIT),
    )(grad_own, returned, send_grid, hub_grid, w_all, w_final, act_tiles)
    return (activations, grad_feats, grad_w_self, grad_w_neigh, grad_bias.reshape(rows))


def solution(mesh):
    return jax.shard_map(
        functools.partial(body, mesh.shape["dom"], mesh.shape["feat"]),
        mesh=mesh,
        in_specs=(
            P("feat", "dom"),
            P("dom"),
            P("dom"),
            P("dom"),
            P("dom"),
            P("dom"),
            P("dom", None, None),
            P("feat", None),
            P("feat", None),
            P("feat"),
            P("feat", "dom"),
        ),
        out_specs=(P("feat", "dom"), P("feat", "dom"), P("feat", None), P("feat", None), P("feat")),
        check_vma=False,
    )
```

```python
import functools

import jax
import jax.numpy as jnp
from jax import lax
from jax.experimental import pallas as pl
from jax.experimental.pallas import tpu as pltpu
from jax.sharding import PartitionSpec as P

MESH = pl.DeviceIdType.MESH
F32 = jnp.float32
BF16 = jnp.bfloat16
ZH = 4
LANES = 128
VMEM_LIMIT = 60 * 1024 * 1024
SUB = 128
SUBLANES = 8


def remote(src, dst, send_sem, recv_sem, where):
    return pltpu.make_async_remote_copy(
        src_ref=src,
        dst_ref=dst,
        send_sem=send_sem,
        recv_sem=recv_sem,
        device_id=where,
        device_id_type=MESH,
    )


def place(near):
    dom = lax.axis_index("dom")
    feat = lax.axis_index("feat")
    return dom, feat, lax.div(feat, near), lax.rem(feat, near)


def aligned(index, size):
    return pl.ds(pl.multiple_of(index * size, size), size)


def column_hot(index_row):
    low = jnp.bitwise_and(index_row, LANES - 1)
    rows = lax.broadcasted_iota(jnp.int32, (LANES, LANES), 0)
    return jnp.where(rows == low, 1.0, 0.0).astype(BF16)


def link_tiles(keys, count, links, first_row, last_row):
    blocks = keys.shape[0]
    none = blocks * LANES
    above = lax.broadcasted_iota(jnp.int32, (LANES, LANES), 0)
    lane = lax.broadcasted_iota(jnp.int32, (LANES, LANES), 1)
    spread = [
        jnp.transpose(jnp.broadcast_to(keys[b : b + 1, :], (LANES, LANES))) for b in range(blocks)
    ]
    for c in range(blocks):
        best = jnp.full((1, LANES), -1, jnp.int32)
        for b in range(c + 1):
            same = spread[b] == keys[c : c + 1, :]
            if b == c:
                same = same & (above < lane)
            found = jnp.where(same, above + b * LANES, -1)
            best = jnp.maximum(best, jnp.max(found, axis=0, keepdims=True))
        links[first_row + c : first_row + c + 1, :] = jnp.where(best < 0, none, best)
    best = jnp.full((1, LANES), -1, jnp.int32)
    for b in range(blocks):
        same = (spread[b] == lane) & (above + b * LANES < count)
        found = jnp.where(same, above + b * LANES, -1)
        best = jnp.maximum(best, jnp.max(found, axis=0, keepdims=True))
    links[last_row : last_row + 1, :] = jnp.where(best < 0, none, best)


def layer_kernel(
    doms,
    near,
    count_ref,
    feats_hbm,
    send_hbm,
    hub_hbm,
    dst_hbm,
    src_hbm,
    vals_hbm,
    w_self_hbm,
    w_neigh_hbm,
    bias_hbm,
    cot_hbm,
    act_out,
    grad_own,
    returned,
    w_all,
    w_final,
    feats,
    send,
    hub,
    dst,
    src,
    vals,
    flipped,
    runs,
    links,
    links_s,
    table,
    picked,
    w_both,
    w_regrouped,
    w_columns,
    bias,
    bias_wide,
    bias_part,
    cot,
    cot_part,
    wrow,
    wcol,
    x_self,
    x_agg,
    agg,
    g_part,
    g_all,
    act_part,
    in_parts,
    grad_agg,
    grad_self,
    away,
    w_parts,
    w_got,
    w_sums,
    w_zh,
    load_sem,
    vals_sem,
    link_sem,
    halo_s,
    halo_r,
    far_s,
    far_r,
    near_s,
    near_r,
    col_s,
    col_r,
    col_near_r,
    share_s,
    share_r,
    agg_s,
    agg_r,
    back_s,
    back_r,
    sum_s,
    sum_r,
    ret_s,
    ret_r,
):
    rows = feats.shape[0]
    own_tiles = feats.shape[1] // LANES
    columns = cot.shape[1]
    dst_tiles = columns // LANES
    quarter = columns // ZH
    halves = quarter // LANES
    width = w_both.shape[2]
    chunk = width // doms
    mine = ZH * rows
    wide = 2 * width // doms
    tile_total = vals.shape[0]
    key_rows = tile_total // LANES
    dom, feat, zh, nr = place(near)

    barrier = pltpu.get_barrier_semaphore()
    for i in range(1, doms):
        pl.semaphore_signal(
            barrier, inc=1, device_id={"dom": lax.rem(dom + i, doms)}, device_id_type=MESH
        )
    for i in range(1, ZH):
        pl.semaphore_signal(
            barrier,
            inc=1,
            device_id={"feat": lax.rem(zh + i, ZH) * near + nr},
            device_id_type=MESH,
        )
    for i in range(1, near):
        pl.semaphore_signal(
            barrier,
            inc=1,
            device_id={"feat": zh * near + lax.rem(nr + i, near)},
            device_id_type=MESH,
        )

    loads = [
        pltpu.make_async_copy(source, target, load_sem.at[i])
        for i, (source, target) in enumerate(
            (
                (feats_hbm, feats),
                (send_hbm, send),
                (hub_hbm, hub),
                (dst_hbm, dst),
                (src_hbm, src),
                (w_self_hbm, w_both.at[0]),
                (w_neigh_hbm, w_both.at[1]),
                (bias_hbm, bias),
                (cot_hbm, cot),
            )
        )
    ]
    for load in loads:
        load.start()
    blocks = vals_sem.shape[0]
    block = tile_total // blocks
    vals_loads = [
        pltpu.make_async_copy(
            vals_hbm.at[b * block : (b + 1) * block],
            vals.at[b * block : (b + 1) * block],
            vals_sem.at[b],
        )
        for b in range(blocks)
    ]
    for load in vals_loads:
        load.start()
    for load in loads:
        load.wait()

    for t in range(own_tiles):
        table[t] = feats[:, t * LANES : (t + 1) * LANES]
    stacked = table[0:own_tiles].reshape(own_tiles * rows, LANES)
    for reader in range(doms + 1):
        index_row = hub[...] if reader == doms else send[reader : reader + 1, :]
        high = jnp.right_shift(index_row, 7)
        found = jnp.dot(stacked, column_hot(index_row), preferred_element_type=F32)
        found = found.reshape(own_tiles, rows, LANES)
        total = jnp.zeros((rows, LANES), F32)
        for t in range(own_tiles):
            total = total + jnp.where(high == t, found[t], 0.0)
        total = total.astype(BF16)
        if reader < doms:
            picked[reader, 0] = total
        else:
            for d in range(doms):
                picked[d, 1] = total

    lanes_at = lax.broadcasted_iota(jnp.int32, (rows, LANES), 1)
    for m in range(2):
        for n in range(near):
            joined = jnp.zeros((rows, LANES), F32)
            for h in range(ZH):
                first = (h * near + n) * rows
                base, offset = first // LANES * LANES, first % LANES
                piece = w_both[m, :, base : base + LANES].astype(F32)
                shift = (h * rows - offset) % LANES
                if shift:
                    piece = pltpu.roll(piece, shift, 1)
                inside = (lanes_at >= h * rows) & (lanes_at < (h + 1) * rows)
                joined = jnp.where(inside, piece, joined)
            w_regrouped[m, n] = joined.astype(BF16)

    spot = lax.broadcasted_iota(jnp.int32, (rows, rows), 0)
    lane = lax.broadcasted_iota(jnp.int32, (rows, rows), 1)
    bias_column = jnp.sum(jnp.where(spot == lane, bias[...], 0.0), axis=1, keepdims=True)
    bias_wide[...] = jnp.broadcast_to(bias_column, (rows, LANES))
    x_self[zh, nr] = feats[:, aligned(zh, quarter)]
    wrow[:, zh, :, aligned(dom, chunk)] = w_both[:, :, aligned(dom, chunk)]
    cot_part[zh] = cot[:, aligned(zh, quarter)]
    bias_part[zh] = bias_wide[...]
    table[pl.ds(own_tiles + 2 * dom, 2)] = picked[dom]


    @pl.when(nr == dom)
    def _():
        w_columns[:, zh] = w_regrouped[...]

    given = src[...]
    outside = given - own_tiles
    placed = own_tiles + 2 * lax.rem(outside, doms) + lax.div(outside, doms)
    placed = jnp.where(outside < 0, given, placed)
    key_dst = dst[...]
    links[0:key_rows, :] = key_dst
    links[key_rows : 2 * key_rows, :] = placed
    prev_dst, prev_src, last_dst = 2 * key_rows, 3 * key_rows, 4 * key_rows
    last_src = last_dst + 1
    link_tiles(key_dst, count_ref[0], links, prev_dst, last_dst)
    link_tiles(placed, count_ref[0], links, prev_src, last_src)
    link_copy = pltpu.make_async_copy(links, links_s, link_sem)
    link_copy.start()

    pl.semaphore_wait(barrier, (doms - 1) + (ZH - 1) + (near - 1))

    def halo_copy(i, source, target):
        return remote(
            picked.at[target],
            table.at[pl.ds(own_tiles + 2 * source, 2)],
            halo_s.at[i],
            halo_r.at[i],
            {"dom": target},
        )

    for i in range(1, doms):
        halo_copy(i, dom, lax.rem(dom + i, doms)).start()

    def far_copy(which, i, source, target):
        sources = (
            feats.at[:, aligned(target, quarter)],
            w_both.at[:, :, aligned(dom, chunk)],
            cot.at[:, aligned(target, quarter)],
            bias_wide,
        )
        targets = (
            x_self.at[source, nr],
            wrow.at[:, source, :, aligned(dom, chunk)],
            cot_part.at[source],
            bias_part.at[source],
        )
        return remote(
            sources[which],
            targets[which],
            far_s.at[which, i],
            far_r.at[which, i],
            {"feat": target * near + nr},
        )

    for i in range(1, ZH):
        far_copy(0, i, zh, lax.rem(zh + i, ZH)).start()
    for i in range(1, ZH):
        far_copy(1, i, zh, lax.rem(zh + i, ZH)).start()

    def col_far_copy(i, source, target):
        return remote(
            w_regrouped,
            w_columns.at[:, source],
            col_s.at[0, i],
            col_r.at[i],
            {"feat": target * near + nr},
        )

    def col_near_copy(i, target):
        return remote(
            w_columns.at[:, :, target],
            wcol.at[:, :, dom],
            col_s.at[1, i],
            col_near_r,
            {"feat": zh * near + target},
        )

    @pl.when(nr == dom)
    def _():
        for i in range(1, ZH):
            col_far_copy(i, zh, lax.rem(zh + i, ZH)).start()

    for which in (2, 3):
        for i in range(1, ZH):
            far_copy(which, i, zh, lax.rem(zh + i, ZH)).start()


    for b in range(blocks):
        vals_loads[b].wait()

        def flip(k, carry):
            flipped[k] = jnp.transpose(vals[k])
            return carry

        lax.fori_loop(b * block, (b + 1) * block, flip, 0, unroll=True)

    def near_copy(which, i, source, target):
        buffer = (x_self, x_agg, g_all)[which]
        return remote(
            buffer.at[:, source],
            buffer.at[:, source],
            near_s.at[which, i],
            near_r.at[which, i],
            {"feat": zh * near + target},
        )

    for i in range(1, ZH):
        far_copy(0, i, lax.rem(zh + ZH - i, ZH), zh).wait_recv()
    for i in range(1, near):
        near_copy(0, i, nr, lax.rem(nr + i, near)).start()

    @pl.when(nr == dom)
    def _():
        for i in range(1, ZH):
            col_far_copy(i, lax.rem(zh + ZH - i, ZH), zh).wait_recv()
        for i in range(1, near):
            col_near_copy(i, lax.rem(nr + i, near)).start()
        wcol[:, :, dom] = w_columns[:, :, nr]

    def share_copy(which, i, source, target):
        part = wcol.at[:, :, source] if which else wrow.at[:, :, :, aligned(source, chunk)]
        return remote(part, part, share_s.at[which, i], share_r.at[which, i], {"dom": target})

    for i in range(1, ZH):
        far_copy(1, i, lax.rem(zh + ZH - i, ZH), zh).wait_recv()
    for i in range(1, doms):
        share_copy(0, i, dom, lax.rem(dom + i, doms)).start()

    link_copy.wait()
    for i in range(1, doms):
        halo_copy(i, lax.rem(dom + doms - i, doms), dom).wait_recv()

    runs[tile_total] = jnp.zeros((rows, LANES), F32)

    def chain(left, left_row, tiles, prev_row, first, last):
        def some(j, carry):
            row = lax.div(j * SUB, LANES)
            start = lax.rem(j * SUB, LANES)
            for t in range(SUB):
                product = jnp.dot(
                    left[links_s[left_row + row, start + t]],
                    tiles[j * SUB + t],
                    preferred_element_type=F32,
                )
                runs[j * SUB + t] = runs[links_s[prev_row + row, start + t]] + product
            return carry

        lax.fori_loop(first, last, some, 0)

    steps = tile_total // SUB
    chain(table, key_rows, flipped, prev_dst, 0, steps)
    for u in range(dst_tiles):
        agg[:, u * LANES : (u + 1) * LANES] = runs[links_s[last_dst, u]].astype(BF16)

    def agg_copy(i, source, target):
        return remote(
            agg.at[:, aligned(target, quarter)],
            x_agg.at[source, nr],
            agg_s.at[i],
            agg_r.at[i],
            {"feat": target * near + nr},
        )

    for i in range(1, ZH):
        agg_copy(i, zh, lax.rem(zh + i, ZH)).start()
    x_agg[zh, nr] = agg[:, aligned(zh, quarter)]

    @pl.when(nr != dom)
    def _():
        col_near_copy(0, nr).wait_recv()

    for i in range(1, doms):
        share_copy(1, i, dom, lax.rem(dom + i, doms)).start()
    for i in range(1, near):
        near_copy(0, i, lax.rem(nr + near - i, near), nr).wait_recv()
    for i in range(1, doms):
        share_copy(0, i, lax.rem(dom + doms - i, doms), dom).wait_recv()
    pre = jnp.dot(
        wrow[0].reshape(mine, width),
        x_self[...].reshape(width, quarter),
        preferred_element_type=F32,
    )
    for i in range(1, ZH):
        agg_copy(i, lax.rem(zh + ZH - i, ZH), zh).wait_recv()
    for i in range(1, near):
        near_copy(1, i, nr, lax.rem(nr + i, near)).start()
    for which in (2, 3):
        for i in range(1, ZH):
            far_copy(which, i, lax.rem(zh + ZH - i, ZH), zh).wait_recv()
    bias_all = jnp.concatenate([bias_part[...].reshape(mine, LANES)] * halves, axis=1)
    pre = pre + bias_all
    for i in range(1, near):
        near_copy(1, i, lax.rem(nr + near - i, near), nr).wait_recv()
    pre = pre + jnp.dot(
        wrow[1].reshape(mine, width),
        x_agg[...].reshape(width, quarter),
        preferred_element_type=F32,
    )
    sig = jax.nn.sigmoid(pre)
    grad = cot_part[...].reshape(mine, quarter).astype(F32) * sig * (1.0 + pre * (1.0 - sig))
    grad = grad.astype(BF16)
    g_part[...] = grad
    g_all[:, nr] = grad.reshape(ZH, rows, quarter)
    for i in range(1, near):
        near_copy(2, i, nr, lax.rem(nr + i, near)).start()

    act = (pre * sig).astype(BF16).reshape(ZH, rows, quarter)
    for h in range(halves):
        act_part[:, h] = act[:, :, h * LANES : (h + 1) * LANES]

    def back_copy(which, i, source, target):
        source_buffer = (act_part, in_parts.at[0], in_parts.at[1])[which]
        target_buffer = (act_out, grad_self, grad_agg)[which]
        return remote(
            source_buffer.at[target],
            target_buffer.at[aligned(source, halves)],
            back_s.at[which, i],
            back_r.at[which, i],
            {"feat": target * near + nr},
        )

    over_x = (((1,), (1,)), ((), ()))
    half_doms = doms // 2
    ones = jnp.ones((2 * SUBLANES, quarter), BF16)
    bias_sum = lax.dot_general(ones, g_part[...], over_x, preferred_element_type=F32)
    bias_sum = bias_sum.astype(BF16)
    for m, x_ref in enumerate((x_self, x_agg)):
        product = lax.dot_general(
            g_part[...],
            x_ref[...].reshape(width, quarter),
            over_x,
            preferred_element_type=F32,
        ).astype(BF16)
        for d in range(half_doms):
            w_parts[m * half_doms + d, 0:mine] = product[:, d * wide : (d + 1) * wide]
    for d in range(doms):
        w_parts[d, mine:, 0:mine] = bias_sum
        w_parts[d, mine:, mine:] = jnp.zeros((2 * SUBLANES, wide - mine), BF16)

    def sum_copy(i, source, target):
        return remote(
            w_parts.at[target],
            w_got.at[source],
            sum_s.at[0, i],
            sum_r.at[0, i],
            {"dom": target},
        )

    for i in range(1, doms):
        sum_copy(i, dom, lax.rem(dom + i, doms)).start()
    for i in range(1, doms):
        share_copy(1, i, lax.rem(dom + doms - i, doms), dom).wait_recv()

    for i in range(1, near):
        near_copy(2, i, lax.rem(nr + near - i, near), nr).wait_recv()
    over_out = (((0,), (0,)), ((), ()))
    for m, target_buffer in ((1, grad_agg), (0, grad_self)):
        back = lax.dot_general(
            wcol[m].reshape(width, mine),
            g_all[...].reshape(width, quarter),
            over_out,
            preferred_element_type=F32,
        )
        back = back.astype(BF16).reshape(ZH, rows, quarter)
        for h in range(halves):
            in_parts[m, :, h] = back[:, :, h * LANES : (h + 1) * LANES]
        for i in range(1, ZH):
            back_copy(1 + m, i, zh, lax.rem(zh + i, ZH)).start()
        target_buffer[aligned(zh, halves)] = in_parts[m, zh]
    for i in range(1, ZH):
        back_copy(0, i, zh, lax.rem(zh + i, ZH)).start()
    act_out[aligned(zh, halves)] = act_part[zh]

    for i in range(1, doms):
        sum_copy(i, lax.rem(dom + doms - i, doms), dom).wait_recv()
    w_got[dom] = w_parts[dom]
    total = w_got[0].astype(F32)
    for d in range(1, doms):
        total = total + w_got[d].astype(F32)
    w_sums[:, 0:rows] = total[0:mine].reshape(ZH, rows, wide)
    for h in range(ZH):
        w_sums[h, rows:] = total[mine : mine + SUBLANES]

    def zh_copy(i, source, target):
        return remote(
            w_sums.at[target],
            w_zh.at[source],
            sum_s.at[1, i],
            sum_r.at[1, i],
            {"feat": target * near + nr},
        )

    for i in range(1, ZH):
        zh_copy(i, zh, lax.rem(zh + i, ZH)).start()
    w_zh[zh] = w_sums[zh]

    for i in range(1, ZH):
        back_copy(2, i, lax.rem(zh + ZH - i, ZH), zh).wait_recv()
    def return_copy(which, i, source, target):
        pieces = ((away.at[pl.ds(2 * target, 2)], returned), (w_final.at[:, 0:wide], w_all))
        part, buffer = pieces[which]
        return remote(
            part, buffer.at[source], ret_s.at[which, i], ret_r.at[which, i], {"dom": target}
        )

    chain(grad_agg, 0, vals, prev_src, 0, steps // 2)

    for i in range(1, ZH):
        zh_copy(i, lax.rem(zh + ZH - i, ZH), zh).wait_recv()
    total = w_zh[0]
    for h in range(1, ZH):
        total = total + w_zh[h]
    spot = lax.broadcasted_iota(jnp.int32, (rows, mine), 0) + zh * rows
    lane = lax.broadcasted_iota(jnp.int32, (rows, mine), 1)
    bias_row = total[rows : rows + 1, 0:mine]
    bias_column = jnp.sum(jnp.where(spot == lane, bias_row, 0.0), axis=1, keepdims=True)
    w_final[:, 0:wide] = total[0:rows]
    w_final[:, wide:] = jnp.broadcast_to(bias_column, (rows, LANES))
    for i in range(1, doms):
        return_copy(1, i, dom, lax.rem(dom + i, doms)).start()
    chain(grad_agg, 0, vals, prev_src, steps // 2, steps)

    for t in range(2 * doms):
        away[t] = runs[links_s[last_src, own_tiles + t]].astype(BF16)

    for i in range(1, doms):
        return_copy(0, i, dom, lax.rem(dom + i, doms)).start()
    returned[dom] = away[pl.ds(2 * dom, 2)]
    w_all[dom] = w_final[:, 0:wide]

    for i in range(1, ZH):
        back_copy(1, i, lax.rem(zh + ZH - i, ZH), zh).wait_recv()
    for t in range(own_tiles):
        total = runs[links_s[last_src, t]]
        if t < dst_tiles:
            total = total + grad_self[t].astype(F32)
        grad_own[t] = total

    for i in range(1, ZH):
        back_copy(0, i, lax.rem(zh + ZH - i, ZH), zh).wait_recv()
    for i in range(1, doms):
        source = lax.rem(dom + doms - i, doms)
        return_copy(0, i, source, dom).wait_recv()
        return_copy(1, i, source, dom).wait_recv()

    for i in range(1, doms):
        target = lax.rem(dom + i, doms)
        halo_copy(i, dom, target).wait_send()
        sum_copy(i, dom, target).wait_send()
        for which in (0, 1):
            share_copy(which, i, dom, target).wait_send()
            return_copy(which, i, dom, target).wait_send()
    for i in range(1, ZH):
        target = lax.rem(zh + i, ZH)
        for which in range(4):
            far_copy(which, i, zh, target).wait_send()
        for which in range(3):
            back_copy(which, i, zh, target).wait_send()
        agg_copy(i, zh, target).wait_send()
        zh_copy(i, zh, target).wait_send()
    for i in range(1, near):
        for which in range(3):
            near_copy(which, i, nr, lax.rem(nr + i, near)).wait_send()

    @pl.when(nr == dom)
    def _():
        for i in range(1, ZH):
            col_far_copy(i, zh, lax.rem(zh + i, ZH)).wait_send()
        for i in range(1, near):
            col_near_copy(i, lax.rem(nr + i, near)).wait_send()


def finish_kernel(
    doms,
    own_ref,
    returned_ref,
    send_rows,
    hub_rows,
    w_all,
    w_final,
    act_ref,
    act_out,
    feats_out,
    w_self_out,
    w_neigh_out,
    bias_out,
    masked,
):
    own_tiles, rows, _ = own_ref.shape
    dst_tiles = act_ref.shape[0]
    wide = w_all.shape[2]
    hots = []
    for block in range(doms + 1):
        if block == doms:
            index_row = hub_rows[...]
            total = returned_ref[0, 1].astype(F32)
            for d in range(1, doms):
                total = total + returned_ref[d, 1].astype(F32)
            values = total.astype(BF16)
        else:
            index_row = send_rows[block : block + 1, :]
            values = returned_ref[block, 0]
        high = jnp.right_shift(index_row, 7)
        values = values.astype(F32)
        for t in range(own_tiles):
            masked[t, :, block * LANES : (block + 1) * LANES] = jnp.where(
                high == t, values, 0.0
            ).astype(BF16)
        hots.append(column_hot(index_row))
    hot = jnp.concatenate(hots, axis=1)
    added = lax.dot_general(
        masked[...].reshape(own_tiles * rows, (doms + 1) * LANES),
        hot,
        (((1,), (1,)), ((), ())),
        preferred_element_type=F32,
    ).reshape(own_tiles, rows, LANES)
    for t in range(own_tiles):
        feats_out[:, t * LANES : (t + 1) * LANES] = own_ref[t] + added[t]
    for t in range(dst_tiles):
        act_out[:, t * LANES : (t + 1) * LANES] = act_ref[t]
    half = doms // 2
    for d in range(half):
        w_self_out[:, d * wide : (d + 1) * wide] = w_all[d]
        w_neigh_out[:, d * wide : (d + 1) * wide] = w_all[half + d]
    spot = lax.broadcasted_iota(jnp.int32, (rows, LANES), 0)
    lane = lax.broadcasted_iota(jnp.int32, (rows, LANES), 1)
    picked = jnp.where(spot == lane, w_final[:, wide:], 0.0)
    bias_out[...] = jnp.sum(picked, axis=0, keepdims=True)[:, 0:rows]


def shape(dims, dtype):
    return jax.ShapeDtypeStruct(dims, dtype)


def body(
    doms,
    feat_total,
    node_feats,
    send_rows,
    hub_rows,
    tile_dst,
    tile_src,
    tile_count,
    tile_vals,
    w_self,
    w_neigh,
    bias_vec,
    cotangent,
):
    near = feat_total // ZH
    rows, own = node_feats.shape
    own_tiles = own // LANES
    columns = cotangent.shape[1]
    dst_tiles = columns // LANES
    quarter = columns // ZH
    halves = quarter // LANES
    width = w_self.shape[1]
    mine = ZH * rows
    wide = 2 * width // doms
    all_tiles = own_tiles + 2 * doms
    tile_total = tile_src.shape[0]
    key_rows = tile_total // LANES
    dma = pltpu.SemaphoreType.DMA
    in_vmem = pl.BlockSpec(memory_space=pltpu.VMEM)

    send_grid = send_rows.reshape(doms, LANES)
    hub_grid = hub_rows.reshape(1, LANES)

    act_tiles, grad_own, returned, w_all, w_final = pl.pallas_call(
        functools.partial(layer_kernel, doms, near),
        name="layer",
        out_shape=(
            shape((dst_tiles, rows, LANES), BF16),
            shape((own_tiles, rows, LANES), F32),
            shape((doms, 2, rows, LANES), BF16),
            shape((doms, rows, wide), F32),
            shape((rows, wide + LANES), F32),
        ),
        in_specs=[pl.BlockSpec(memory_space=pltpu.SMEM)]
        + [pl.BlockSpec(memory_space=pltpu.HBM)] * 10,
        out_specs=(in_vmem,) * 5,
        scratch_shapes=[
            pltpu.VMEM((rows, own), BF16),
            pltpu.VMEM((doms, LANES), jnp.int32),
            pltpu.VMEM((1, LANES), jnp.int32),
            pltpu.VMEM((key_rows, LANES), jnp.int32),
            pltpu.VMEM((key_rows, LANES), jnp.int32),
            pltpu.VMEM((tile_total, LANES, LANES), BF16),
            pltpu.VMEM((tile_total, LANES, LANES), BF16),
            pltpu.VMEM((tile_total + 1, rows, LANES), F32),
            pltpu.VMEM((4 * key_rows + 8, LANES), jnp.int32),
            pltpu.SMEM((4 * key_rows + 8, LANES), jnp.int32),
            pltpu.VMEM((all_tiles, rows, LANES), BF16),
            pltpu.VMEM((doms, 2, rows, LANES), BF16),
            pltpu.VMEM((2, rows, width), BF16),
            pltpu.VMEM((2, near, rows, mine), BF16),
            pltpu.VMEM((2, ZH, near, rows, mine), BF16),
            pltpu.VMEM((1, rows), F32),
            pltpu.VMEM((rows, LANES), F32),
            pltpu.VMEM((ZH, rows, LANES), F32),
            pltpu.VMEM((rows, columns), BF16),
            pltpu.VMEM((ZH, rows, quarter), BF16),
            pltpu.VMEM((2, ZH, rows, width), BF16),
            pltpu.VMEM((2, ZH, near, rows, mine), BF16),
            pltpu.VMEM((ZH, near, rows, quarter), BF16),
            pltpu.VMEM((ZH, near, rows, quarter), BF16),
            pltpu.VMEM((rows, columns), BF16),
            pltpu.VMEM((mine, quarter), BF16),
            pltpu.VMEM((ZH, near, rows, quarter), BF16),
            pltpu.VMEM((ZH, halves, rows, LANES), BF16),
            pltpu.VMEM((2, ZH, halves, rows, LANES), BF16),
            pltpu.VMEM((dst_tiles, rows, LANES), BF16),
            pltpu.VMEM((dst_tiles, rows, LANES), BF16),
            pltpu.VMEM((2 * doms, rows, LANES), BF16),
            pltpu.VMEM((doms, mine + 2 * SUBLANES, wide), BF16),
            pltpu.VMEM((doms, mine + 2 * SUBLANES, wide), BF16),
            pltpu.VMEM((ZH, rows + SUBLANES, wide), F32),
            pltpu.VMEM((ZH, rows + SUBLANES, wide), F32),
            dma((9,)),
            dma((16,)),
            dma,
            dma((doms,)),
            dma((doms,)),
            dma((4, ZH)),
            dma((4, ZH)),
            dma((3, near)),
            dma((3, near)),
            dma((2, max(near, ZH))),
            dma((ZH,)),
            dma,
            dma((2, doms)),
            dma((2, doms)),
            dma((ZH,)),
            dma((ZH,)),
            dma((3, ZH)),
            dma((3, ZH)),
            dma((2, max(doms, ZH))),
            dma((2, max(doms, ZH))),
            dma((2, doms)),
            dma((2, doms)),
        ],
        compiler_params=pltpu.CompilerParams(
            collective_id=0, has_side_effects=True, vmem_limit_bytes=VMEM_LIMIT
        ),
    )(
        tile_count,
        node_feats,
        send_grid,
        hub_grid,
        tile_dst.reshape(key_rows, LANES),
        tile_src.reshape(key_rows, LANES),
        tile_vals,
        w_self,
        w_neigh,
        bias_vec.reshape(1, rows),
        cotangent,
    )

    activations, grad_feats, grad_w_self, grad_w_neigh, grad_bias = pl.pallas_call(
        functools.partial(finish_kernel, doms),
        name="finish",
        out_shape=(
            shape((rows, columns), BF16),
            shape((rows, own), F32),
            shape((rows, width), F32),
            shape((rows, width), F32),
            shape((1, rows), F32),
        ),
        in_specs=[in_vmem] * 7,
        out_specs=(in_vmem,) * 5,
        scratch_shapes=[pltpu.VMEM((own_tiles, rows, (doms + 1) * LANES), BF16)],
        compiler_params=pltpu.CompilerParams(vmem_limit_bytes=VMEM_LIMIT),
    )(grad_own, returned, send_grid, hub_grid, w_all, w_final, act_tiles)
    return (activations, grad_feats, grad_w_self, grad_w_neigh, grad_bias.reshape(rows))


def solution(mesh):
    return jax.shard_map(
        functools.partial(body, mesh.shape["dom"], mesh.shape["feat"]),
        mesh=mesh,
        in_specs=(
            P("feat", "dom"),
            P("dom"),
            P("dom"),
            P("dom"),
            P("dom"),
            P("dom"),
            P("dom", None, None),
            P("feat", None),
            P("feat", None),
            P("feat"),
            P("feat", "dom"),
        ),
        out_specs=(P("feat", "dom"), P("feat", "dom"), P("feat", None), P("feat", None), P("feat")),
        check_vma=False,
    )
```

```python
import functools

import jax
import jax.numpy as jnp
from jax import lax
from jax.experimental import pallas as pl
from jax.experimental.pallas import tpu as pltpu
from jax.sharding import PartitionSpec as P

MESH = pl.DeviceIdType.MESH
F32 = jnp.float32
BF16 = jnp.bfloat16
ZH = 4
LANES = 128
VMEM_LIMIT = 60 * 1024 * 1024
SUB = 128
SUBLANES = 8


def remote(src, dst, send_sem, recv_sem, where):
    return pltpu.make_async_remote_copy(
        src_ref=src,
        dst_ref=dst,
        send_sem=send_sem,
        recv_sem=recv_sem,
        device_id=where,
        device_id_type=MESH,
    )


def place(near):
    dom = lax.axis_index("dom")
    feat = lax.axis_index("feat")
    return dom, feat, lax.div(feat, near), lax.rem(feat, near)


def aligned(index, size):
    return pl.ds(pl.multiple_of(index * size, size), size)


def column_hot(index_row):
    low = jnp.bitwise_and(index_row, LANES - 1)
    rows = lax.broadcasted_iota(jnp.int32, (LANES, LANES), 0)
    return jnp.where(rows == low, 1.0, 0.0).astype(BF16)


def link_tiles(keys, count, links, first_row, last_row):
    blocks = keys.shape[0]
    none = blocks * LANES
    above = lax.broadcasted_iota(jnp.int32, (LANES, LANES), 0)
    lane = lax.broadcasted_iota(jnp.int32, (LANES, LANES), 1)
    spread = [
        jnp.transpose(jnp.broadcast_to(keys[b : b + 1, :], (LANES, LANES))) for b in range(blocks)
    ]
    for c in range(blocks):
        best = jnp.full((1, LANES), -1, jnp.int32)
        for b in range(c + 1):
            same = spread[b] == keys[c : c + 1, :]
            if b == c:
                same = same & (above < lane)
            found = jnp.where(same, above + b * LANES, -1)
            best = jnp.maximum(best, jnp.max(found, axis=0, keepdims=True))
        links[first_row + c : first_row + c + 1, :] = jnp.where(best < 0, none, best)
    best = jnp.full((1, LANES), -1, jnp.int32)
    for b in range(blocks):
        same = (spread[b] == lane) & (above + b * LANES < count)
        found = jnp.where(same, above + b * LANES, -1)
        best = jnp.maximum(best, jnp.max(found, axis=0, keepdims=True))
    links[last_row : last_row + 1, :] = jnp.where(best < 0, none, best)


def layer_kernel(
    doms,
    near,
    count_ref,
    feats_hbm,
    send_hbm,
    hub_hbm,
    dst_hbm,
    src_hbm,
    vals_hbm,
    w_self_hbm,
    w_neigh_hbm,
    bias_hbm,
    cot_hbm,
    act_out,
    grad_own,
    returned,
    w_all,
    w_final,
    feats,
    send,
    hub,
    dst,
    src,
    vals,
    flipped,
    runs,
    links,
    links_s,
    table,
    picked,
    w_both,
    w_regrouped,
    w_columns,
    bias,
    bias_wide,
    bias_part,
    cot,
    cot_part,
    wrow,
    wcol,
    x_self,
    x_agg,
    agg,
    g_part,
    g_all,
    act_part,
    in_parts,
    grad_agg,
    grad_self,
    away,
    w_parts,
    w_got,
    w_sums,
    w_zh,
    load_sem,
    vals_sem,
    link_sem,
    halo_s,
    halo_r,
    far_s,
    far_r,
    near_s,
    near_r,
    col_s,
    col_r,
    col_near_r,
    share_s,
    share_r,
    agg_s,
    agg_r,
    back_s,
    back_r,
    sum_s,
    sum_r,
    ret_s,
    ret_r,
):
    rows = feats.shape[0]
    own_tiles = feats.shape[1] // LANES
    columns = cot.shape[1]
    dst_tiles = columns // LANES
    quarter = columns // ZH
    halves = quarter // LANES
    width = w_both.shape[2]
    chunk = width // doms
    mine = ZH * rows
    wide = 2 * width // doms
    tile_total = vals.shape[0]
    key_rows = tile_total // LANES
    dom, feat, zh, nr = place(near)

    loads = [
        pltpu.make_async_copy(source, target, load_sem.at[i])
        for i, (source, target) in enumerate(
            (
                (feats_hbm, feats),
                (send_hbm, send),
                (hub_hbm, hub),
                (dst_hbm, dst),
                (src_hbm, src),
                (w_self_hbm, w_both.at[0]),
                (w_neigh_hbm, w_both.at[1]),
                (bias_hbm, bias),
                (cot_hbm, cot),
            )
        )
    ]
    for load in loads:
        load.start()
    blocks = vals_sem.shape[0]
    block = tile_total // blocks
    vals_loads = [
        pltpu.make_async_copy(
            vals_hbm.at[b * block : (b + 1) * block],
            vals.at[b * block : (b + 1) * block],
            vals_sem.at[b],
        )
        for b in range(blocks)
    ]
    for load in vals_loads:
        load.start()

    barrier = pltpu.get_barrier_semaphore()
    for i in range(1, doms):
        pl.semaphore_signal(
            barrier, inc=1, device_id={"dom": lax.rem(dom + i, doms)}, device_id_type=MESH
        )
    for i in range(1, ZH):
        pl.semaphore_signal(
            barrier,
            inc=1,
            device_id={"feat": lax.rem(zh + i, ZH) * near + nr},
            device_id_type=MESH,
        )
    for i in range(1, near):
        pl.semaphore_signal(
            barrier,
            inc=1,
            device_id={"feat": zh * near + lax.rem(nr + i, near)},
            device_id_type=MESH,
        )

    for load in loads:
        load.wait()

    for t in range(own_tiles):
        table[t] = feats[:, t * LANES : (t + 1) * LANES]
    stacked = table[0:own_tiles].reshape(own_tiles * rows, LANES)
    for reader in range(doms + 1):
        index_row = hub[...] if reader == doms else send[reader : reader + 1, :]
        high = jnp.right_shift(index_row, 7)
        found = jnp.dot(stacked, column_hot(index_row), preferred_element_type=F32)
        found = found.reshape(own_tiles, rows, LANES)
        total = jnp.zeros((rows, LANES), F32)
        for t in range(own_tiles):
            total = total + jnp.where(high == t, found[t], 0.0)
        total = total.astype(BF16)
        if reader < doms:
            picked[reader, 0] = total
        else:
            for d in range(doms):
                picked[d, 1] = total

    lanes_at = lax.broadcasted_iota(jnp.int32, (rows, LANES), 1)
    for m in range(2):
        for n in range(near):
            joined = jnp.zeros((rows, LANES), F32)
            for h in range(ZH):
                first = (h * near + n) * rows
                base, offset = first // LANES * LANES, first % LANES
                piece = w_both[m, :, base : base + LANES].astype(F32)
                shift = (h * rows - offset) % LANES
                if shift:
                    piece = pltpu.roll(piece, shift, 1)
                inside = (lanes_at >= h * rows) & (lanes_at < (h + 1) * rows)
                joined = jnp.where(inside, piece, joined)
            w_regrouped[m, n] = joined.astype(BF16)

    spot = lax.broadcasted_iota(jnp.int32, (rows, rows), 0)
    lane = lax.broadcasted_iota(jnp.int32, (rows, rows), 1)
    bias_column = jnp.sum(jnp.where(spot == lane, bias[...], 0.0), axis=1, keepdims=True)
    bias_wide[...] = jnp.broadcast_to(bias_column, (rows, LANES))
    x_self[zh, nr] = feats[:, aligned(zh, quarter)]
    wrow[:, zh, :, aligned(dom, chunk)] = w_both[:, :, aligned(dom, chunk)]
    cot_part[zh] = cot[:, aligned(zh, quarter)]
    bias_part[zh] = bias_wide[...]
    table[pl.ds(own_tiles + 2 * dom, 2)] = picked[dom]


    @pl.when(nr == dom)
    def _():
        w_columns[:, zh] = w_regrouped[...]

    given = src[...]
    outside = given - own_tiles
    placed = own_tiles + 2 * lax.rem(outside, doms) + lax.div(outside, doms)
    placed = jnp.where(outside < 0, given, placed)
    key_dst = dst[...]
    links[0:key_rows, :] = key_dst
    links[key_rows : 2 * key_rows, :] = placed
    prev_dst, prev_src, last_dst = 2 * key_rows, 3 * key_rows, 4 * key_rows
    last_src = last_dst + 1
    link_tiles(key_dst, count_ref[0], links, prev_dst, last_dst)
    link_tiles(placed, count_ref[0], links, prev_src, last_src)
    link_copy = pltpu.make_async_copy(links, links_s, link_sem)
    link_copy.start()

    pl.semaphore_wait(barrier, (doms - 1) + (ZH - 1) + (near - 1))

    def halo_copy(i, source, target):
        return remote(
            picked.at[target],
            table.at[pl.ds(own_tiles + 2 * source, 2)],
            halo_s.at[i],
            halo_r.at[i],
            {"dom": target},
        )

    for i in range(1, doms):
        halo_copy(i, dom, lax.rem(dom + i, doms)).start()

    def far_copy(which, i, source, target):
        sources = (
            feats.at[:, aligned(target, quarter)],
            w_both.at[:, :, aligned(dom, chunk)],
            cot.at[:, aligned(target, quarter)],
            bias_wide,
        )
        targets = (
            x_self.at[source, nr],
            wrow.at[:, source, :, aligned(dom, chunk)],
            cot_part.at[source],
            bias_part.at[source],
        )
        return remote(
            sources[which],
            targets[which],
            far_s.at[which, i],
            far_r.at[which, i],
            {"feat": target * near + nr},
        )

    for i in range(1, ZH):
        far_copy(0, i, zh, lax.rem(zh + i, ZH)).start()
    for i in range(1, ZH):
        far_copy(1, i, zh, lax.rem(zh + i, ZH)).start()

    def col_far_copy(i, source, target):
        return remote(
            w_regrouped,
            w_columns.at[:, source],
            col_s.at[0, i],
            col_r.at[i],
            {"feat": target * near + nr},
        )

    def col_near_copy(i, target):
        return remote(
            w_columns.at[:, :, target],
            wcol.at[:, :, dom],
            col_s.at[1, i],
            col_near_r,
            {"feat": zh * near + target},
        )

    @pl.when(nr == dom)
    def _():
        for i in range(1, ZH):
            col_far_copy(i, zh, lax.rem(zh + i, ZH)).start()


    for b in range(blocks):
        vals_loads[b].wait()

        def flip(k, carry):
            flipped[k] = jnp.transpose(vals[k])
            return carry

        lax.fori_loop(b * block, (b + 1) * block, flip, 0, unroll=True)

    def near_copy(which, i, source, target):
        buffer = (x_self, x_agg, g_all)[which]
        return remote(
            buffer.at[:, source],
            buffer.at[:, source],
            near_s.at[which, i],
            near_r.at[which, i],
            {"feat": zh * near + target},
        )

    link_copy.wait()
    for i in range(1, doms):
        halo_copy(i, lax.rem(dom + doms - i, doms), dom).wait_recv()

    runs[tile_total] = jnp.zeros((rows, LANES), F32)

    def chain(left, left_row, tiles, prev_row, first, last):
        def some(j, carry):
            row = lax.div(j * SUB, LANES)
            start = lax.rem(j * SUB, LANES)
            for t in range(SUB):
                product = jnp.dot(
                    left[links_s[left_row + row, start + t]],
                    tiles[j * SUB + t],
                    preferred_element_type=F32,
                )
                runs[j * SUB + t] = runs[links_s[prev_row + row, start + t]] + product
            return carry

        lax.fori_loop(first, last, some, 0)

    steps = tile_total // SUB
    chain(table, key_rows, flipped, prev_dst, 0, steps)
    for u in range(dst_tiles):
        agg[:, u * LANES : (u + 1) * LANES] = runs[links_s[last_dst, u]].astype(BF16)

    def agg_copy(i, source, target):
        return remote(
            agg.at[:, aligned(target, quarter)],
            x_agg.at[source, nr],
            agg_s.at[i],
            agg_r.at[i],
            {"feat": target * near + nr},
        )

    for i in range(1, ZH):
        agg_copy(i, zh, lax.rem(zh + i, ZH)).start()
    x_agg[zh, nr] = agg[:, aligned(zh, quarter)]

    def share_copy(which, i, source, target):
        part = wcol.at[:, :, source] if which else wrow.at[:, :, :, aligned(source, chunk)]
        return remote(part, part, share_s.at[which, i], share_r.at[which, i], {"dom": target})

    for i in range(1, ZH):
        far_copy(0, i, lax.rem(zh + ZH - i, ZH), zh).wait_recv()
    for i in range(1, near):
        near_copy(0, i, nr, lax.rem(nr + i, near)).start()

    @pl.when(nr == dom)
    def _():
        for i in range(1, ZH):
            col_far_copy(i, lax.rem(zh + ZH - i, ZH), zh).wait_recv()
        for i in range(1, near):
            col_near_copy(i, lax.rem(nr + i, near)).start()
        wcol[:, :, dom] = w_columns[:, :, nr]

    for i in range(1, ZH):
        far_copy(1, i, lax.rem(zh + ZH - i, ZH), zh).wait_recv()
    for i in range(1, doms):
        share_copy(0, i, dom, lax.rem(dom + i, doms)).start()

    for which in (2, 3):
        for i in range(1, ZH):
            far_copy(which, i, zh, lax.rem(zh + i, ZH)).start()

    for i in range(1, ZH):
        agg_copy(i, lax.rem(zh + ZH - i, ZH), zh).wait_recv()
    for i in range(1, near):
        near_copy(1, i, nr, lax.rem(nr + i, near)).start()

    @pl.when(nr != dom)
    def _():
        col_near_copy(0, nr).wait_recv()

    for i in range(1, doms):
        share_copy(1, i, dom, lax.rem(dom + i, doms)).start()
    for i in range(1, near):
        near_copy(0, i, lax.rem(nr + near - i, near), nr).wait_recv()
    for i in range(1, doms):
        share_copy(0, i, lax.rem(dom + doms - i, doms), dom).wait_recv()
    pre = jnp.dot(
        wrow[0].reshape(mine, width),
        x_self[...].reshape(width, quarter),
        preferred_element_type=F32,
    )
    for which in (2, 3):
        for i in range(1, ZH):
            far_copy(which, i, lax.rem(zh + ZH - i, ZH), zh).wait_recv()
    bias_all = jnp.concatenate([bias_part[...].reshape(mine, LANES)] * halves, axis=1)
    pre = pre + bias_all
    for i in range(1, near):
        near_copy(1, i, lax.rem(nr + near - i, near), nr).wait_recv()
    pre = pre + jnp.dot(
        wrow[1].reshape(mine, width),
        x_agg[...].reshape(width, quarter),
        preferred_element_type=F32,
    )
    sig = jax.nn.sigmoid(pre)
    grad = cot_part[...].reshape(mine, quarter).astype(F32) * sig * (1.0 + pre * (1.0 - sig))
    grad = grad.astype(BF16)
    g_part[...] = grad
    g_all[:, nr] = grad.reshape(ZH, rows, quarter)
    for i in range(1, near):
        near_copy(2, i, nr, lax.rem(nr + i, near)).start()

    act = (pre * sig).astype(BF16).reshape(ZH, rows, quarter)
    for h in range(halves):
        act_part[:, h] = act[:, :, h * LANES : (h + 1) * LANES]

    def back_copy(which, i, source, target):
        source_buffer = (act_part, in_parts.at[0], in_parts.at[1])[which]
        target_buffer = (act_out, grad_self, grad_agg)[which]
        return remote(
            source_buffer.at[target],
            target_buffer.at[aligned(source, halves)],
            back_s.at[which, i],
            back_r.at[which, i],
            {"feat": target * near + nr},
        )

    over_x = (((1,), (1,)), ((), ()))
    half_doms = doms // 2
    ones = jnp.ones((2 * SUBLANES, quarter), BF16)
    bias_sum = lax.dot_general(ones, g_part[...], over_x, preferred_element_type=F32)
    bias_sum = bias_sum.astype(BF16)
    for m, x_ref in enumerate((x_self, x_agg)):
        product = lax.dot_general(
            g_part[...],
            x_ref[...].reshape(width, quarter),
            over_x,
            preferred_element_type=F32,
        ).astype(BF16)
        for d in range(half_doms):
            w_parts[m * half_doms + d, 0:mine] = product[:, d * wide : (d + 1) * wide]
    for d in range(doms):
        w_parts[d, mine:, 0:mine] = bias_sum
        w_parts[d, mine:, mine:] = jnp.zeros((2 * SUBLANES, wide - mine), BF16)

    def sum_copy(i, source, target):
        return remote(
            w_parts.at[target],
            w_got.at[source],
            sum_s.at[0, i],
            sum_r.at[0, i],
            {"dom": target},
        )

    for i in range(1, doms):
        sum_copy(i, dom, lax.rem(dom + i, doms)).start()
    for i in range(1, doms):
        share_copy(1, i, lax.rem(dom + doms - i, doms), dom).wait_recv()

    for i in range(1, near):
        near_copy(2, i, lax.rem(nr + near - i, near), nr).wait_recv()
    over_out = (((0,), (0,)), ((), ()))
    for m, target_buffer in ((1, grad_agg), (0, grad_self)):
        back = lax.dot_general(
            wcol[m].reshape(width, mine),
            g_all[...].reshape(width, quarter),
            over_out,
            preferred_element_type=F32,
        )
        back = back.astype(BF16).reshape(ZH, rows, quarter)
        for h in range(halves):
            in_parts[m, :, h] = back[:, :, h * LANES : (h + 1) * LANES]
        for i in range(1, ZH):
            back_copy(1 + m, i, zh, lax.rem(zh + i, ZH)).start()
        target_buffer[aligned(zh, halves)] = in_parts[m, zh]
    for i in range(1, ZH):
        back_copy(0, i, zh, lax.rem(zh + i, ZH)).start()
    act_out[aligned(zh, halves)] = act_part[zh]

    for i in range(1, doms):
        sum_copy(i, lax.rem(dom + doms - i, doms), dom).wait_recv()
    w_got[dom] = w_parts[dom]
    total = w_got[0].astype(F32)
    for d in range(1, doms):
        total = total + w_got[d].astype(F32)
    w_sums[:, 0:rows] = total[0:mine].reshape(ZH, rows, wide)
    for h in range(ZH):
        w_sums[h, rows:] = total[mine : mine + SUBLANES]

    def zh_copy(i, source, target):
        return remote(
            w_sums.at[target],
            w_zh.at[source],
            sum_s.at[1, i],
            sum_r.at[1, i],
            {"feat": target * near + nr},
        )

    for i in range(1, ZH):
        zh_copy(i, zh, lax.rem(zh + i, ZH)).start()
    w_zh[zh] = w_sums[zh]

    for i in range(1, ZH):
        back_copy(2, i, lax.rem(zh + ZH - i, ZH), zh).wait_recv()
    def return_copy(which, i, source, target):
        pieces = ((away.at[pl.ds(2 * target, 2)], returned), (w_final.at[:, 0:wide], w_all))
        part, buffer = pieces[which]
        return remote(
            part, buffer.at[source], ret_s.at[which, i], ret_r.at[which, i], {"dom": target}
        )

    chain(grad_agg, 0, vals, prev_src, 0, steps // 2)

    for i in range(1, ZH):
        zh_copy(i, lax.rem(zh + ZH - i, ZH), zh).wait_recv()
    total = w_zh[0]
    for h in range(1, ZH):
        total = total + w_zh[h]
    spot = lax.broadcasted_iota(jnp.int32, (rows, mine), 0) + zh * rows
    lane = lax.broadcasted_iota(jnp.int32, (rows, mine), 1)
    bias_row = total[rows : rows + 1, 0:mine]
    bias_column = jnp.sum(jnp.where(spot == lane, bias_row, 0.0), axis=1, keepdims=True)
    w_final[:, 0:wide] = total[0:rows]
    w_final[:, wide:] = jnp.broadcast_to(bias_column, (rows, LANES))
    for i in range(1, doms):
        return_copy(1, i, dom, lax.rem(dom + i, doms)).start()
    chain(grad_agg, 0, vals, prev_src, steps // 2, steps)

    for t in range(2 * doms):
        away[t] = runs[links_s[last_src, own_tiles + t]].astype(BF16)

    for i in range(1, doms):
        return_copy(0, i, dom, lax.rem(dom + i, doms)).start()
    returned[dom] = away[pl.ds(2 * dom, 2)]
    w_all[dom] = w_final[:, 0:wide]

    for i in range(1, ZH):
        back_copy(1, i, lax.rem(zh + ZH - i, ZH), zh).wait_recv()
    for t in range(own_tiles):
        total = runs[links_s[last_src, t]]
        if t < dst_tiles:
            total = total + grad_self[t].astype(F32)
        grad_own[t] = total

    for i in range(1, ZH):
        back_copy(0, i, lax.rem(zh + ZH - i, ZH), zh).wait_recv()
    for i in range(1, doms):
        target = lax.rem(dom + i, doms)
        halo_copy(i, dom, target).wait_send()
        sum_copy(i, dom, target).wait_send()
        for which in (0, 1):
            share_copy(which, i, dom, target).wait_send()
    for i in range(1, ZH):
        target = lax.rem(zh + i, ZH)
        for which in range(4):
            far_copy(which, i, zh, target).wait_send()
        for which in range(3):
            back_copy(which, i, zh, target).wait_send()
        agg_copy(i, zh, target).wait_send()
        zh_copy(i, zh, target).wait_send()
    for i in range(1, near):
        for which in range(3):
            near_copy(which, i, nr, lax.rem(nr + i, near)).wait_send()

    @pl.when(nr == dom)
    def _():
        for i in range(1, ZH):
            col_far_copy(i, zh, lax.rem(zh + i, ZH)).wait_send()
        for i in range(1, near):
            col_near_copy(i, lax.rem(nr + i, near)).wait_send()

    for i in range(1, doms):
        source = lax.rem(dom + doms - i, doms)
        for which in (0, 1):
            return_copy(which, i, source, dom).wait_recv()
            return_copy(which, i, dom, lax.rem(dom + i, doms)).wait_send()


def finish_kernel(
    doms,
    own_ref,
    returned_ref,
    send_rows,
    hub_rows,
    w_all,
    w_final,
    act_ref,
    act_out,
    feats_out,
    w_self_out,
    w_neigh_out,
    bias_out,
    masked,
):
    own_tiles, rows, _ = own_ref.shape
    dst_tiles = act_ref.shape[0]
    wide = w_all.shape[2]
    hots = []
    for block in range(doms + 1):
        if block == doms:
            index_row = hub_rows[...]
            total = returned_ref[0, 1].astype(F32)
            for d in range(1, doms):
                total = total + returned_ref[d, 1].astype(F32)
            values = total.astype(BF16)
        else:
            index_row = send_rows[block : block + 1, :]
            values = returned_ref[block, 0]
        high = jnp.right_shift(index_row, 7)
        values = values.astype(F32)
        for t in range(own_tiles):
            masked[t, :, block * LANES : (block + 1) * LANES] = jnp.where(
                high == t, values, 0.0
            ).astype(BF16)
        hots.append(column_hot(index_row))
    hot = jnp.concatenate(hots, axis=1)
    added = lax.dot_general(
        masked[...].reshape(own_tiles * rows, (doms + 1) * LANES),
        hot,
        (((1,), (1,)), ((), ())),
        preferred_element_type=F32,
    ).reshape(own_tiles, rows, LANES)
    for t in range(own_tiles):
        feats_out[:, t * LANES : (t + 1) * LANES] = own_ref[t] + added[t]
    for t in range(dst_tiles):
        act_out[:, t * LANES : (t + 1) * LANES] = act_ref[t]
    half = doms // 2
    for d in range(half):
        w_self_out[:, d * wide : (d + 1) * wide] = w_all[d]
        w_neigh_out[:, d * wide : (d + 1) * wide] = w_all[half + d]
    spot = lax.broadcasted_iota(jnp.int32, (rows, LANES), 0)
    lane = lax.broadcasted_iota(jnp.int32, (rows, LANES), 1)
    picked = jnp.where(spot == lane, w_final[:, wide:], 0.0)
    bias_out[...] = jnp.sum(picked, axis=0, keepdims=True)[:, 0:rows]


def shape(dims, dtype):
    return jax.ShapeDtypeStruct(dims, dtype)


def body(
    doms,
    feat_total,
    node_feats,
    send_rows,
    hub_rows,
    tile_dst,
    tile_src,
    tile_count,
    tile_vals,
    w_self,
    w_neigh,
    bias_vec,
    cotangent,
):
    near = feat_total // ZH
    rows, own = node_feats.shape
    own_tiles = own // LANES
    columns = cotangent.shape[1]
    dst_tiles = columns // LANES
    quarter = columns // ZH
    halves = quarter // LANES
    width = w_self.shape[1]
    mine = ZH * rows
    wide = 2 * width // doms
    all_tiles = own_tiles + 2 * doms
    tile_total = tile_src.shape[0]
    key_rows = tile_total // LANES
    dma = pltpu.SemaphoreType.DMA
    in_vmem = pl.BlockSpec(memory_space=pltpu.VMEM)

    send_grid = send_rows.reshape(doms, LANES)
    hub_grid = hub_rows.reshape(1, LANES)

    act_tiles, grad_own, returned, w_all, w_final = pl.pallas_call(
        functools.partial(layer_kernel, doms, near),
        name="layer",
        out_shape=(
            shape((dst_tiles, rows, LANES), BF16),
            shape((own_tiles, rows, LANES), F32),
            shape((doms, 2, rows, LANES), BF16),
            shape((doms, rows, wide), F32),
            shape((rows, wide + LANES), F32),
        ),
        in_specs=[pl.BlockSpec(memory_space=pltpu.SMEM)]
        + [pl.BlockSpec(memory_space=pltpu.HBM)] * 10,
        out_specs=(in_vmem,) * 5,
        scratch_shapes=[
            pltpu.VMEM((rows, own), BF16),
            pltpu.VMEM((doms, LANES), jnp.int32),
            pltpu.VMEM((1, LANES), jnp.int32),
            pltpu.VMEM((key_rows, LANES), jnp.int32),
            pltpu.VMEM((key_rows, LANES), jnp.int32),
            pltpu.VMEM((tile_total, LANES, LANES), BF16),
            pltpu.VMEM((tile_total, LANES, LANES), BF16),
            pltpu.VMEM((tile_total + 1, rows, LANES), F32),
            pltpu.VMEM((4 * key_rows + 8, LANES), jnp.int32),
            pltpu.SMEM((4 * key_rows + 8, LANES), jnp.int32),
            pltpu.VMEM((all_tiles, rows, LANES), BF16),
            pltpu.VMEM((doms, 2, rows, LANES), BF16),
            pltpu.VMEM((2, rows, width), BF16),
            pltpu.VMEM((2, near, rows, mine), BF16),
            pltpu.VMEM((2, ZH, near, rows, mine), BF16),
            pltpu.VMEM((1, rows), F32),
            pltpu.VMEM((rows, LANES), F32),
            pltpu.VMEM((ZH, rows, LANES), F32),
            pltpu.VMEM((rows, columns), BF16),
            pltpu.VMEM((ZH, rows, quarter), BF16),
            pltpu.VMEM((2, ZH, rows, width), BF16),
            pltpu.VMEM((2, ZH, near, rows, mine), BF16),
            pltpu.VMEM((ZH, near, rows, quarter), BF16),
            pltpu.VMEM((ZH, near, rows, quarter), BF16),
            pltpu.VMEM((rows, columns), BF16),
            pltpu.VMEM((mine, quarter), BF16),
            pltpu.VMEM((ZH, near, rows, quarter), BF16),
            pltpu.VMEM((ZH, halves, rows, LANES), BF16),
            pltpu.VMEM((2, ZH, halves, rows, LANES), BF16),
            pltpu.VMEM((dst_tiles, rows, LANES), BF16),
            pltpu.VMEM((dst_tiles, rows, LANES), BF16),
            pltpu.VMEM((2 * doms, rows, LANES), BF16),
            pltpu.VMEM((doms, mine + 2 * SUBLANES, wide), BF16),
            pltpu.VMEM((doms, mine + 2 * SUBLANES, wide), BF16),
            pltpu.VMEM((ZH, rows + SUBLANES, wide), F32),
            pltpu.VMEM((ZH, rows + SUBLANES, wide), F32),
            dma((9,)),
            dma((16,)),
            dma,
            dma((doms,)),
            dma((doms,)),
            dma((4, ZH)),
            dma((4, ZH)),
            dma((3, near)),
            dma((3, near)),
            dma((2, max(near, ZH))),
            dma((ZH,)),
            dma,
            dma((2, doms)),
            dma((2, doms)),
            dma((ZH,)),
            dma((ZH,)),
            dma((3, ZH)),
            dma((3, ZH)),
            dma((2, max(doms, ZH))),
            dma((2, max(doms, ZH))),
            dma((2, doms)),
            dma((2, doms)),
        ],
        compiler_params=pltpu.CompilerParams(
            collective_id=0, has_side_effects=True, vmem_limit_bytes=VMEM_LIMIT
        ),
    )(
        tile_count,
        node_feats,
        send_grid,
        hub_grid,
        tile_dst.reshape(key_rows, LANES),
        tile_src.reshape(key_rows, LANES),
        tile_vals,
        w_self,
        w_neigh,
        bias_vec.reshape(1, rows),
        cotangent,
    )

    activations, grad_feats, grad_w_self, grad_w_neigh, grad_bias = pl.pallas_call(
        functools.partial(finish_kernel, doms),
        name="finish",
        out_shape=(
            shape((rows, columns), BF16),
            shape((rows, own), F32),
            shape((rows, width), F32),
            shape((rows, width), F32),
            shape((1, rows), F32),
        ),
        in_specs=[in_vmem] * 7,
        out_specs=(in_vmem,) * 5,
        scratch_shapes=[pltpu.VMEM((own_tiles, rows, (doms + 1) * LANES), BF16)],
        compiler_params=pltpu.CompilerParams(vmem_limit_bytes=VMEM_LIMIT),
    )(grad_own, returned, send_grid, hub_grid, w_all, w_final, act_tiles)
    return (activations, grad_feats, grad_w_self, grad_w_neigh, grad_bias.reshape(rows))


def solution(mesh):
    return jax.shard_map(
        functools.partial(body, mesh.shape["dom"], mesh.shape["feat"]),
        mesh=mesh,
        in_specs=(
            P("feat", "dom"),
            P("dom"),
            P("dom"),
            P("dom"),
            P("dom"),
            P("dom"),
            P("dom", None, None),
            P("feat", None),
            P("feat", None),
            P("feat"),
            P("feat", "dom"),
        ),
        out_specs=(P("feat", "dom"), P("feat", "dom"), P("feat", None), P("feat", None), P("feat")),
        check_vma=False,
    )
```

```python
import functools

import jax
import jax.numpy as jnp
from jax import lax
from jax.experimental import pallas as pl
from jax.experimental.pallas import tpu as pltpu
from jax.sharding import PartitionSpec as P

MESH = pl.DeviceIdType.MESH
F32 = jnp.float32
BF16 = jnp.bfloat16
ZH = 4
LANES = 128
VMEM_LIMIT = 52 * 1024 * 1024
SUB = 128
SUBLANES = 8


def remote(src, dst, send_sem, recv_sem, where):
    return pltpu.make_async_remote_copy(
        src_ref=src,
        dst_ref=dst,
        send_sem=send_sem,
        recv_sem=recv_sem,
        device_id=where,
        device_id_type=MESH,
    )


def place(near):
    dom = lax.axis_index("dom")
    feat = lax.axis_index("feat")
    return dom, feat, lax.div(feat, near), lax.rem(feat, near)


def aligned(index, size):
    return pl.ds(pl.multiple_of(index * size, size), size)


def column_hot(index_row):
    low = jnp.bitwise_and(index_row, LANES - 1)
    rows = lax.broadcasted_iota(jnp.int32, (LANES, LANES), 0)
    return jnp.where(rows == low, 1.0, 0.0).astype(BF16)


def link_tiles(keys, count, links, first_row, last_row):
    blocks = keys.shape[0]
    none = blocks * LANES
    above = lax.broadcasted_iota(jnp.int32, (LANES, LANES), 0)
    lane = lax.broadcasted_iota(jnp.int32, (LANES, LANES), 1)
    spread = [
        jnp.transpose(jnp.broadcast_to(keys[b : b + 1, :], (LANES, LANES))) for b in range(blocks)
    ]
    for c in range(blocks):
        best = jnp.full((1, LANES), -1, jnp.int32)
        for b in range(c + 1):
            same = spread[b] == keys[c : c + 1, :]
            if b == c:
                same = same & (above < lane)
            found = jnp.where(same, above + b * LANES, -1)
            best = jnp.maximum(best, jnp.max(found, axis=0, keepdims=True))
        links[first_row + c : first_row + c + 1, :] = jnp.where(best < 0, none, best)
    best = jnp.full((1, LANES), -1, jnp.int32)
    for b in range(blocks):
        same = (spread[b] == lane) & (above + b * LANES < count)
        found = jnp.where(same, above + b * LANES, -1)
        best = jnp.maximum(best, jnp.max(found, axis=0, keepdims=True))
    links[last_row : last_row + 1, :] = jnp.where(best < 0, none, best)


def layer_kernel(
    doms,
    near,
    count_ref,
    feats_hbm,
    send_hbm,
    hub_hbm,
    dst_hbm,
    src_hbm,
    vals_hbm,
    w_self_hbm,
    w_neigh_hbm,
    bias_hbm,
    cot_hbm,
    act_out,
    grad_own,
    returned,
    w_all,
    w_final,
    feats,
    send,
    hub,
    dst,
    src,
    vals,
    flipped,
    runs,
    links,
    links_s,
    table,
    picked,
    w_both,
    w_regrouped,
    w_columns,
    bias,
    bias_wide,
    bias_part,
    cot,
    cot_part,
    wrow,
    wcol,
    x_self,
    x_agg,
    agg,
    g_part,
    g_all,
    act_part,
    in_parts,
    grad_agg,
    grad_self,
    away,
    w_parts,
    w_got,
    w_sums,
    w_zh,
    load_sem,
    vals_sem,
    link_sem,
    halo_s,
    halo_r,
    far_s,
    far_r,
    near_s,
    near_r,
    col_s,
    col_r,
    col_near_r,
    share_s,
    share_r,
    agg_s,
    agg_r,
    back_s,
    back_r,
    sum_s,
    sum_r,
    ret_s,
    ret_r,
):
    rows = feats.shape[0]
    own_tiles = feats.shape[1] // LANES
    columns = cot.shape[1]
    dst_tiles = columns // LANES
    quarter = columns // ZH
    halves = quarter // LANES
    width = w_both.shape[2]
    chunk = width // doms
    mine = ZH * rows
    wide = 2 * width // doms
    tile_total = vals.shape[0]
    key_rows = tile_total // LANES
    dom, feat, zh, nr = place(near)

    loads = [
        pltpu.make_async_copy(source, target, load_sem.at[i])
        for i, (source, target) in enumerate(
            (
                (feats_hbm, feats),
                (send_hbm, send),
                (hub_hbm, hub),
                (dst_hbm, dst),
                (src_hbm, src),
                (w_self_hbm, w_both.at[0]),
                (w_neigh_hbm, w_both.at[1]),
                (bias_hbm, bias),
                (cot_hbm, cot),
            )
        )
    ]
    for load in loads:
        load.start()
    blocks = vals_sem.shape[0]
    block = tile_total // blocks
    vals_loads = [
        pltpu.make_async_copy(
            vals_hbm.at[b * block : (b + 1) * block],
            vals.at[b * block : (b + 1) * block],
            vals_sem.at[b],
        )
        for b in range(blocks)
    ]
    for load in vals_loads:
        load.start()

    barrier = pltpu.get_barrier_semaphore()
    for i in range(1, doms):
        pl.semaphore_signal(
            barrier, inc=1, device_id={"dom": lax.rem(dom + i, doms)}, device_id_type=MESH
        )
    for i in range(1, ZH):
        pl.semaphore_signal(
            barrier,
            inc=1,
            device_id={"feat": lax.rem(zh + i, ZH) * near + nr},
            device_id_type=MESH,
        )
    for i in range(1, near):
        pl.semaphore_signal(
            barrier,
            inc=1,
            device_id={"feat": zh * near + lax.rem(nr + i, near)},
            device_id_type=MESH,
        )

    for load in loads:
        load.wait()

    for t in range(own_tiles):
        table[t] = feats[:, t * LANES : (t + 1) * LANES]
    stacked = table[0:own_tiles].reshape(own_tiles * rows, LANES)
    for reader in range(doms + 1):
        index_row = hub[...] if reader == doms else send[reader : reader + 1, :]
        high = jnp.right_shift(index_row, 7)
        found = jnp.dot(stacked, column_hot(index_row), preferred_element_type=F32)
        found = found.reshape(own_tiles, rows, LANES)
        total = jnp.zeros((rows, LANES), F32)
        for t in range(own_tiles):
            total = total + jnp.where(high == t, found[t], 0.0)
        total = total.astype(BF16)
        if reader < doms:
            picked[reader, 0] = total
        else:
            for d in range(doms):
                picked[d, 1] = total

    lanes_at = lax.broadcasted_iota(jnp.int32, (rows, LANES), 1)
    for m in range(2):
        for n in range(near):
            joined = jnp.zeros((rows, LANES), F32)
            for h in range(ZH):
                first = (h * near + n) * rows
                base, offset = first // LANES * LANES, first % LANES
                piece = w_both[m, :, base : base + LANES].astype(F32)
                shift = (h * rows - offset) % LANES
                if shift:
                    piece = pltpu.roll(piece, shift, 1)
                inside = (lanes_at >= h * rows) & (lanes_at < (h + 1) * rows)
                joined = jnp.where(inside, piece, joined)
            w_regrouped[m, n] = joined.astype(BF16)

    spot = lax.broadcasted_iota(jnp.int32, (rows, rows), 0)
    lane = lax.broadcasted_iota(jnp.int32, (rows, rows), 1)
    bias_column = jnp.sum(jnp.where(spot == lane, bias[...], 0.0), axis=1, keepdims=True)
    bias_wide[...] = jnp.broadcast_to(bias_column, (rows, LANES))
    x_self[zh, nr] = feats[:, aligned(zh, quarter)]
    wrow[:, zh, :, aligned(dom, chunk)] = w_both[:, :, aligned(dom, chunk)]
    cot_part[zh] = cot[:, aligned(zh, quarter)]
    bias_part[zh] = bias_wide[...]
    table[pl.ds(own_tiles + 2 * dom, 2)] = picked[dom]


    @pl.when(nr == dom)
    def _():
        w_columns[:, zh] = w_regrouped[...]

    given = src[...]
    outside = given - own_tiles
    placed = own_tiles + 2 * lax.rem(outside, doms) + lax.div(outside, doms)
    placed = jnp.where(outside < 0, given, placed)
    key_dst = dst[...]
    links[0:key_rows, :] = key_dst
    links[key_rows : 2 * key_rows, :] = placed
    prev_dst, prev_src, last_dst = 2 * key_rows, 3 * key_rows, 4 * key_rows
    last_src = last_dst + 1
    link_tiles(key_dst, count_ref[0], links, prev_dst, last_dst)
    link_tiles(placed, count_ref[0], links, prev_src, last_src)
    link_copy = pltpu.make_async_copy(links, links_s, link_sem)
    link_copy.start()

    pl.semaphore_wait(barrier, (doms - 1) + (ZH - 1) + (near - 1))

    def halo_copy(i, source, target):
        return remote(
            picked.at[target],
            table.at[pl.ds(own_tiles + 2 * source, 2)],
            halo_s.at[i],
            halo_r.at[i],
            {"dom": target},
        )

    for i in range(1, doms):
        halo_copy(i, dom, lax.rem(dom + i, doms)).start()

    def far_copy(which, i, source, target):
        sources = (
            feats.at[:, aligned(target, quarter)],
            w_both.at[:, :, aligned(dom, chunk)],
            cot.at[:, aligned(target, quarter)],
            bias_wide,
        )
        targets = (
            x_self.at[source, nr],
            wrow.at[:, source, :, aligned(dom, chunk)],
            cot_part.at[source],
            bias_part.at[source],
        )
        return remote(
            sources[which],
            targets[which],
            far_s.at[which, i],
            far_r.at[which, i],
            {"feat": target * near + nr},
        )

    for i in range(1, ZH):
        far_copy(0, i, zh, lax.rem(zh + i, ZH)).start()
    for i in range(1, ZH):
        far_copy(1, i, zh, lax.rem(zh + i, ZH)).start()

    def col_far_copy(i, source, target):
        return remote(
            w_regrouped,
            w_columns.at[:, source],
            col_s.at[0, i],
            col_r.at[i],
            {"feat": target * near + nr},
        )

    def col_near_copy(i, target):
        return remote(
            w_columns.at[:, :, target],
            wcol.at[:, :, dom],
            col_s.at[1, i],
            col_near_r,
            {"feat": zh * near + target},
        )

    @pl.when(nr == dom)
    def _():
        for i in range(1, ZH):
            col_far_copy(i, zh, lax.rem(zh + i, ZH)).start()


    for b in range(blocks):
        vals_loads[b].wait()

        def flip(k, carry):
            flipped[k] = jnp.transpose(vals[k])
            return carry

        lax.fori_loop(b * block, (b + 1) * block, flip, 0, unroll=True)

    def near_copy(which, i, source, target):
        buffer = (x_self, x_agg, g_all)[which]
        return remote(
            buffer.at[:, source],
            buffer.at[:, source],
            near_s.at[which, i],
            near_r.at[which, i],
            {"feat": zh * near + target},
        )

    for i in range(1, ZH):
        far_copy(0, i, lax.rem(zh + ZH - i, ZH), zh).wait_recv()
    for i in range(1, near):
        near_copy(0, i, nr, lax.rem(nr + i, near)).start()
    link_copy.wait()
    for i in range(1, doms):
        halo_copy(i, lax.rem(dom + doms - i, doms), dom).wait_recv()

    runs[tile_total] = jnp.zeros((rows, LANES), F32)

    def chain(left, left_row, tiles, prev_row, first, last):
        def some(j, carry):
            row = lax.div(j * SUB, LANES)
            start = lax.rem(j * SUB, LANES)
            for t in range(SUB):
                product = jnp.dot(
                    left[links_s[left_row + row, start + t]],
                    tiles[j * SUB + t],
                    preferred_element_type=F32,
                )
                runs[j * SUB + t] = runs[links_s[prev_row + row, start + t]] + product
            return carry

        lax.fori_loop(first, last, some, 0)

    steps = tile_total // SUB
    chain(table, key_rows, flipped, prev_dst, 0, steps)
    for u in range(dst_tiles):
        agg[:, u * LANES : (u + 1) * LANES] = runs[links_s[last_dst, u]].astype(BF16)

    def agg_copy(i, source, target):
        return remote(
            agg.at[:, aligned(target, quarter)],
            x_agg.at[source, nr],
            agg_s.at[i],
            agg_r.at[i],
            {"feat": target * near + nr},
        )

    for i in range(1, ZH):
        agg_copy(i, zh, lax.rem(zh + i, ZH)).start()
    x_agg[zh, nr] = agg[:, aligned(zh, quarter)]

    def share_copy(which, i, source, target):
        part = wcol.at[:, :, source] if which else wrow.at[:, :, :, aligned(source, chunk)]
        return remote(part, part, share_s.at[which, i], share_r.at[which, i], {"dom": target})


    @pl.when(nr == dom)
    def _():
        for i in range(1, ZH):
            col_far_copy(i, lax.rem(zh + ZH - i, ZH), zh).wait_recv()
        for i in range(1, near):
            col_near_copy(i, lax.rem(nr + i, near)).start()
        wcol[:, :, dom] = w_columns[:, :, nr]

    for i in range(1, ZH):
        far_copy(1, i, lax.rem(zh + ZH - i, ZH), zh).wait_recv()
    for i in range(1, doms):
        share_copy(0, i, dom, lax.rem(dom + i, doms)).start()

    for which in (2, 3):
        for i in range(1, ZH):
            far_copy(which, i, zh, lax.rem(zh + i, ZH)).start()

    for i in range(1, ZH):
        agg_copy(i, lax.rem(zh + ZH - i, ZH), zh).wait_recv()
    for i in range(1, near):
        near_copy(1, i, nr, lax.rem(nr + i, near)).start()

    @pl.when(nr != dom)
    def _():
        col_near_copy(0, nr).wait_recv()

    for i in range(1, doms):
        share_copy(1, i, dom, lax.rem(dom + i, doms)).start()
    for i in range(1, near):
        near_copy(0, i, lax.rem(nr + near - i, near), nr).wait_recv()
    for i in range(1, doms):
        share_copy(0, i, lax.rem(dom + doms - i, doms), dom).wait_recv()
    pre = jnp.dot(
        wrow[0].reshape(mine, width),
        x_self[...].reshape(width, quarter),
        preferred_element_type=F32,
    )
    for which in (2, 3):
        for i in range(1, ZH):
            far_copy(which, i, lax.rem(zh + ZH - i, ZH), zh).wait_recv()
    bias_all = jnp.concatenate([bias_part[...].reshape(mine, LANES)] * halves, axis=1)
    pre = pre + bias_all
    for i in range(1, near):
        near_copy(1, i, lax.rem(nr + near - i, near), nr).wait_recv()
    pre = pre + jnp.dot(
        wrow[1].reshape(mine, width),
        x_agg[...].reshape(width, quarter),
        preferred_element_type=F32,
    )
    sig = jax.nn.sigmoid(pre)
    grad = cot_part[...].reshape(mine, quarter).astype(F32) * sig * (1.0 + pre * (1.0 - sig))
    grad = grad.astype(BF16)
    g_part[...] = grad
    g_all[:, nr] = grad.reshape(ZH, rows, quarter)
    for i in range(1, near):
        near_copy(2, i, nr, lax.rem(nr + i, near)).start()

    act = (pre * sig).astype(BF16).reshape(ZH, rows, quarter)
    for h in range(halves):
        act_part[:, h] = act[:, :, h * LANES : (h + 1) * LANES]

    def back_copy(which, i, source, target):
        source_buffer = (act_part, in_parts.at[0], in_parts.at[1])[which]
        target_buffer = (act_out, grad_self, grad_agg)[which]
        return remote(
            source_buffer.at[target],
            target_buffer.at[aligned(source, halves)],
            back_s.at[which, i],
            back_r.at[which, i],
            {"feat": target * near + nr},
        )

    over_x = (((1,), (1,)), ((), ()))
    half_doms = doms // 2
    ones = jnp.ones((2 * SUBLANES, quarter), BF16)
    bias_sum = lax.dot_general(ones, g_part[...], over_x, preferred_element_type=F32)
    bias_sum = bias_sum.astype(BF16)
    for m, x_ref in enumerate((x_self, x_agg)):
        product = lax.dot_general(
            g_part[...],
            x_ref[...].reshape(width, quarter),
            over_x,
            preferred_element_type=F32,
        ).astype(BF16)
        for d in range(half_doms):
            w_parts[m * half_doms + d, 0:mine] = product[:, d * wide : (d + 1) * wide]
    for d in range(doms):
        w_parts[d, mine:, 0:mine] = bias_sum
        w_parts[d, mine:, mine:] = jnp.zeros((2 * SUBLANES, wide - mine), BF16)

    def sum_copy(i, source, target):
        return remote(
            w_parts.at[target],
            w_got.at[source],
            sum_s.at[0, i],
            sum_r.at[0, i],
            {"dom": target},
        )

    for i in range(1, doms):
        sum_copy(i, dom, lax.rem(dom + i, doms)).start()
    for i in range(1, doms):
        share_copy(1, i, lax.rem(dom + doms - i, doms), dom).wait_recv()

    for i in range(1, near):
        near_copy(2, i, lax.rem(nr + near - i, near), nr).wait_recv()
    over_out = (((0,), (0,)), ((), ()))
    for m, target_buffer in ((1, grad_agg), (0, grad_self)):
        back = lax.dot_general(
            wcol[m].reshape(width, mine),
            g_all[...].reshape(width, quarter),
            over_out,
            preferred_element_type=F32,
        )
        back = back.astype(BF16).reshape(ZH, rows, quarter)
        for h in range(halves):
            in_parts[m, :, h] = back[:, :, h * LANES : (h + 1) * LANES]
        for i in range(1, ZH):
            back_copy(1 + m, i, zh, lax.rem(zh + i, ZH)).start()
        target_buffer[aligned(zh, halves)] = in_parts[m, zh]
    for i in range(1, ZH):
        back_copy(0, i, zh, lax.rem(zh + i, ZH)).start()
    act_out[aligned(zh, halves)] = act_part[zh]

    for i in range(1, doms):
        sum_copy(i, lax.rem(dom + doms - i, doms), dom).wait_recv()
    w_got[dom] = w_parts[dom]
    total = w_got[0].astype(F32)
    for d in range(1, doms):
        total = total + w_got[d].astype(F32)
    w_sums[:, 0:rows] = total[0:mine].reshape(ZH, rows, wide)
    for h in range(ZH):
        w_sums[h, rows:] = total[mine : mine + SUBLANES]

    def zh_copy(i, source, target):
        return remote(
            w_sums.at[target],
            w_zh.at[source],
            sum_s.at[1, i],
            sum_r.at[1, i],
            {"feat": target * near + nr},
        )

    for i in range(1, ZH):
        zh_copy(i, zh, lax.rem(zh + i, ZH)).start()
    w_zh[zh] = w_sums[zh]

    for i in range(1, ZH):
        back_copy(2, i, lax.rem(zh + ZH - i, ZH), zh).wait_recv()
    def return_copy(which, i, source, target):
        pieces = ((away.at[pl.ds(2 * target, 2)], returned), (w_final.at[:, 0:wide], w_all))
        part, buffer = pieces[which]
        return remote(
            part, buffer.at[source], ret_s.at[which, i], ret_r.at[which, i], {"dom": target}
        )

    chain(grad_agg, 0, vals, prev_src, 0, steps // 2)

    for i in range(1, ZH):
        zh_copy(i, lax.rem(zh + ZH - i, ZH), zh).wait_recv()
    total = w_zh[0]
    for h in range(1, ZH):
        total = total + w_zh[h]
    spot = lax.broadcasted_iota(jnp.int32, (rows, mine), 0) + zh * rows
    lane = lax.broadcasted_iota(jnp.int32, (rows, mine), 1)
    bias_row = total[rows : rows + 1, 0:mine]
    bias_column = jnp.sum(jnp.where(spot == lane, bias_row, 0.0), axis=1, keepdims=True)
    w_final[:, 0:wide] = total[0:rows]
    w_final[:, wide:] = jnp.broadcast_to(bias_column, (rows, LANES))
    for i in range(1, doms):
        return_copy(1, i, dom, lax.rem(dom + i, doms)).start()
    chain(grad_agg, 0, vals, prev_src, steps // 2, steps)

    for t in range(2 * doms):
        away[t] = runs[links_s[last_src, own_tiles + t]].astype(BF16)

    for i in range(1, doms):
        return_copy(0, i, dom, lax.rem(dom + i, doms)).start()
    returned[dom] = away[pl.ds(2 * dom, 2)]
    w_all[dom] = w_final[:, 0:wide]

    for i in range(1, ZH):
        back_copy(1, i, lax.rem(zh + ZH - i, ZH), zh).wait_recv()
    for t in range(own_tiles):
        total = runs[links_s[last_src, t]]
        if t < dst_tiles:
            total = total + grad_self[t].astype(F32)
        grad_own[t] = total

    for i in range(1, ZH):
        back_copy(0, i, lax.rem(zh + ZH - i, ZH), zh).wait_recv()
    for i in range(1, doms):
        target = lax.rem(dom + i, doms)
        halo_copy(i, dom, target).wait_send()
        sum_copy(i, dom, target).wait_send()
        for which in (0, 1):
            share_copy(which, i, dom, target).wait_send()
    for i in range(1, ZH):
        target = lax.rem(zh + i, ZH)
        for which in range(4):
            far_copy(which, i, zh, target).wait_send()
        for which in range(3):
            back_copy(which, i, zh, target).wait_send()
        agg_copy(i, zh, target).wait_send()
        zh_copy(i, zh, target).wait_send()
    for i in range(1, near):
        for which in range(3):
            near_copy(which, i, nr, lax.rem(nr + i, near)).wait_send()

    @pl.when(nr == dom)
    def _():
        for i in range(1, ZH):
            col_far_copy(i, zh, lax.rem(zh + i, ZH)).wait_send()
        for i in range(1, near):
            col_near_copy(i, lax.rem(nr + i, near)).wait_send()

    for i in range(1, doms):
        source = lax.rem(dom + doms - i, doms)
        for which in (0, 1):
            return_copy(which, i, source, dom).wait_recv()
            return_copy(which, i, dom, lax.rem(dom + i, doms)).wait_send()


def finish_kernel(
    doms,
    own_ref,
    returned_ref,
    send_rows,
    hub_rows,
    w_all,
    w_final,
    act_ref,
    act_out,
    feats_out,
    w_self_out,
    w_neigh_out,
    bias_out,
    masked,
):
    own_tiles, rows, _ = own_ref.shape
    dst_tiles = act_ref.shape[0]
    wide = w_all.shape[2]
    hots = []
    for block in range(doms + 1):
        if block == doms:
            index_row = hub_rows[...]
            total = returned_ref[0, 1].astype(F32)
            for d in range(1, doms):
                total = total + returned_ref[d, 1].astype(F32)
            values = total.astype(BF16)
        else:
            index_row = send_rows[block : block + 1, :]
            values = returned_ref[block, 0]
        high = jnp.right_shift(index_row, 7)
        values = values.astype(F32)
        for t in range(own_tiles):
            masked[t, :, block * LANES : (block + 1) * LANES] = jnp.where(
                high == t, values, 0.0
            ).astype(BF16)
        hots.append(column_hot(index_row))
    hot = jnp.concatenate(hots, axis=1)
    added = lax.dot_general(
        masked[...].reshape(own_tiles * rows, (doms + 1) * LANES),
        hot,
        (((1,), (1,)), ((), ())),
        preferred_element_type=F32,
    ).reshape(own_tiles, rows, LANES)
    for t in range(own_tiles):
        feats_out[:, t * LANES : (t + 1) * LANES] = own_ref[t] + added[t]
    for t in range(dst_tiles):
        act_out[:, t * LANES : (t + 1) * LANES] = act_ref[t]
    half = doms // 2
    for d in range(half):
        w_self_out[:, d * wide : (d + 1) * wide] = w_all[d]
        w_neigh_out[:, d * wide : (d + 1) * wide] = w_all[half + d]
    spot = lax.broadcasted_iota(jnp.int32, (rows, LANES), 0)
    lane = lax.broadcasted_iota(jnp.int32, (rows, LANES), 1)
    picked = jnp.where(spot == lane, w_final[:, wide:], 0.0)
    bias_out[...] = jnp.sum(picked, axis=0, keepdims=True)[:, 0:rows]


def shape(dims, dtype):
    return jax.ShapeDtypeStruct(dims, dtype)


def body(
    doms,
    feat_total,
    node_feats,
    send_rows,
    hub_rows,
    tile_dst,
    tile_src,
    tile_count,
    tile_vals,
    w_self,
    w_neigh,
    bias_vec,
    cotangent,
):
    near = feat_total // ZH
    rows, own = node_feats.shape
    own_tiles = own // LANES
    columns = cotangent.shape[1]
    dst_tiles = columns // LANES
    quarter = columns // ZH
    halves = quarter // LANES
    width = w_self.shape[1]
    mine = ZH * rows
    wide = 2 * width // doms
    all_tiles = own_tiles + 2 * doms
    tile_total = tile_src.shape[0]
    key_rows = tile_total // LANES
    dma = pltpu.SemaphoreType.DMA
    in_vmem = pl.BlockSpec(memory_space=pltpu.VMEM)

    send_grid = send_rows.reshape(doms, LANES)
    hub_grid = hub_rows.reshape(1, LANES)

    act_tiles, grad_own, returned, w_all, w_final = pl.pallas_call(
        functools.partial(layer_kernel, doms, near),
        name="layer",
        out_shape=(
            shape((dst_tiles, rows, LANES), BF16),
            shape((own_tiles, rows, LANES), F32),
            shape((doms, 2, rows, LANES), BF16),
            shape((doms, rows, wide), F32),
            shape((rows, wide + LANES), F32),
        ),
        in_specs=[pl.BlockSpec(memory_space=pltpu.SMEM)]
        + [pl.BlockSpec(memory_space=pltpu.HBM)] * 10,
        out_specs=(in_vmem,) * 5,
        scratch_shapes=[
            pltpu.VMEM((rows, own), BF16),
            pltpu.VMEM((doms, LANES), jnp.int32),
            pltpu.VMEM((1, LANES), jnp.int32),
            pltpu.VMEM((key_rows, LANES), jnp.int32),
            pltpu.VMEM((key_rows, LANES), jnp.int32),
            pltpu.VMEM((tile_total, LANES, LANES), BF16),
            pltpu.VMEM((tile_total, LANES, LANES), BF16),
            pltpu.VMEM((tile_total + 1, rows, LANES), F32),
            pltpu.VMEM((4 * key_rows + 8, LANES), jnp.int32),
            pltpu.SMEM((4 * key_rows + 8, LANES), jnp.int32),
            pltpu.VMEM((all_tiles, rows, LANES), BF16),
            pltpu.VMEM((doms, 2, rows, LANES), BF16),
            pltpu.VMEM((2, rows, width), BF16),
            pltpu.VMEM((2, near, rows, mine), BF16),
            pltpu.VMEM((2, ZH, near, rows, mine), BF16),
            pltpu.VMEM((1, rows), F32),
            pltpu.VMEM((rows, LANES), F32),
            pltpu.VMEM((ZH, rows, LANES), F32),
            pltpu.VMEM((rows, columns), BF16),
            pltpu.VMEM((ZH, rows, quarter), BF16),
            pltpu.VMEM((2, ZH, rows, width), BF16),
            pltpu.VMEM((2, ZH, near, rows, mine), BF16),
            pltpu.VMEM((ZH, near, rows, quarter), BF16),
            pltpu.VMEM((ZH, near, rows, quarter), BF16),
            pltpu.VMEM((rows, columns), BF16),
            pltpu.VMEM((mine, quarter), BF16),
            pltpu.VMEM((ZH, near, rows, quarter), BF16),
            pltpu.VMEM((ZH, halves, rows, LANES), BF16),
            pltpu.VMEM((2, ZH, halves, rows, LANES), BF16),
            pltpu.VMEM((dst_tiles, rows, LANES), BF16),
            pltpu.VMEM((dst_tiles, rows, LANES), BF16),
            pltpu.VMEM((2 * doms, rows, LANES), BF16),
            pltpu.VMEM((doms, mine + 2 * SUBLANES, wide), BF16),
            pltpu.VMEM((doms, mine + 2 * SUBLANES, wide), BF16),
            pltpu.VMEM((ZH, rows + SUBLANES, wide), F32),
            pltpu.VMEM((ZH, rows + SUBLANES, wide), F32),
            dma((9,)),
            dma((16,)),
            dma,
            dma((doms,)),
            dma((doms,)),
            dma((4, ZH)),
            dma((4, ZH)),
            dma((3, near)),
            dma((3, near)),
            dma((2, max(near, ZH))),
            dma((ZH,)),
            dma,
            dma((2, doms)),
            dma((2, doms)),
            dma((ZH,)),
            dma((ZH,)),
            dma((3, ZH)),
            dma((3, ZH)),
            dma((2, max(doms, ZH))),
            dma((2, max(doms, ZH))),
            dma((2, doms)),
            dma((2, doms)),
        ],
        compiler_params=pltpu.CompilerParams(
            collective_id=0, has_side_effects=True, vmem_limit_bytes=VMEM_LIMIT
        ),
    )(
        tile_count,
        *[
            pltpu.with_memory_space_constraint(array, pltpu.HBM)
            for array in (
                node_feats,
                send_grid,
                hub_grid,
                tile_dst.reshape(key_rows, LANES),
                tile_src.reshape(key_rows, LANES),
                tile_vals,
                w_self,
                w_neigh,
                bias_vec.reshape(1, rows),
                cotangent,
            )
        ],
    )

    activations, grad_feats, grad_w_self, grad_w_neigh, grad_bias = pl.pallas_call(
        functools.partial(finish_kernel, doms),
        name="finish",
        out_shape=(
            shape((rows, columns), BF16),
            shape((rows, own), F32),
            shape((rows, width), F32),
            shape((rows, width), F32),
            shape((1, rows), F32),
        ),
        in_specs=[in_vmem] * 7,
        out_specs=(in_vmem,) * 5,
        scratch_shapes=[pltpu.VMEM((own_tiles, rows, (doms + 1) * LANES), BF16)],
        compiler_params=pltpu.CompilerParams(vmem_limit_bytes=VMEM_LIMIT),
    )(grad_own, returned, send_grid, hub_grid, w_all, w_final, act_tiles)
    return (activations, grad_feats, grad_w_self, grad_w_neigh, grad_bias.reshape(rows))


def solution(mesh):
    return jax.shard_map(
        functools.partial(body, mesh.shape["dom"], mesh.shape["feat"]),
        mesh=mesh,
        in_specs=(
            P("feat", "dom"),
            P("dom"),
            P("dom"),
            P("dom"),
            P("dom"),
            P("dom"),
            P("dom", None, None),
            P("feat", None),
            P("feat", None),
            P("feat"),
            P("feat", "dom"),
        ),
        out_specs=(P("feat", "dom"), P("feat", "dom"), P("feat", None), P("feat", None), P("feat")),
        check_vma=False,
    )
```

```python
import functools

import jax
import jax.numpy as jnp
from jax import lax
from jax.experimental import pallas as pl
from jax.experimental.pallas import tpu as pltpu
from jax.sharding import PartitionSpec as P

MESH = pl.DeviceIdType.MESH
F32 = jnp.float32
BF16 = jnp.bfloat16
ZH = 4
LANES = 128
VMEM_LIMIT = 52 * 1024 * 1024
SUB = 128
SUBLANES = 8


def remote(src, dst, send_sem, recv_sem, where):
    return pltpu.make_async_remote_copy(
        src_ref=src,
        dst_ref=dst,
        send_sem=send_sem,
        recv_sem=recv_sem,
        device_id=where,
        device_id_type=MESH,
    )


def place(near):
    dom = lax.axis_index("dom")
    feat = lax.axis_index("feat")
    return dom, feat, lax.div(feat, near), lax.rem(feat, near)


def aligned(index, size):
    return pl.ds(pl.multiple_of(index * size, size), size)


def column_hot(index_row):
    low = jnp.bitwise_and(index_row, LANES - 1)
    rows = lax.broadcasted_iota(jnp.int32, (LANES, LANES), 0)
    return jnp.where(rows == low, 1.0, 0.0).astype(BF16)


def link_tiles(keys, count, links, first_row, last_row):
    blocks = keys.shape[0]
    none = blocks * LANES
    above = lax.broadcasted_iota(jnp.int32, (LANES, LANES), 0)
    lane = lax.broadcasted_iota(jnp.int32, (LANES, LANES), 1)
    spread = [
        jnp.transpose(jnp.broadcast_to(keys[b : b + 1, :], (LANES, LANES))) for b in range(blocks)
    ]
    for c in range(blocks):
        best = jnp.full((1, LANES), -1, jnp.int32)
        for b in range(c + 1):
            same = spread[b] == keys[c : c + 1, :]
            if b == c:
                same = same & (above < lane)
            found = jnp.where(same, above + b * LANES, -1)
            best = jnp.maximum(best, jnp.max(found, axis=0, keepdims=True))
        links[first_row + c : first_row + c + 1, :] = jnp.where(best < 0, none, best)
    best = jnp.full((1, LANES), -1, jnp.int32)
    for b in range(blocks):
        same = (spread[b] == lane) & (above + b * LANES < count)
        found = jnp.where(same, above + b * LANES, -1)
        best = jnp.maximum(best, jnp.max(found, axis=0, keepdims=True))
    links[last_row : last_row + 1, :] = jnp.where(best < 0, none, best)


def layer_kernel(
    doms,
    near,
    count_ref,
    feats_hbm,
    send_hbm,
    hub_hbm,
    dst_hbm,
    src_hbm,
    vals_hbm,
    w_self_hbm,
    w_neigh_hbm,
    bias_hbm,
    cot_hbm,
    act_out,
    grad_own,
    returned,
    w_all,
    w_final,
    feats,
    send,
    hub,
    dst,
    src,
    vals,
    flipped,
    runs,
    links,
    links_s,
    table,
    picked,
    w_both,
    w_regrouped,
    w_columns,
    bias,
    bias_wide,
    bias_part,
    cot,
    cot_part,
    wrow,
    wcol,
    x_self,
    x_agg,
    agg,
    g_part,
    g_all,
    act_part,
    in_parts,
    grad_agg,
    grad_self,
    away,
    w_parts,
    w_got,
    w_sums,
    w_zh,
    load_sem,
    vals_sem,
    link_sem,
    halo_s,
    halo_r,
    far_s,
    far_r,
    near_s,
    near_r,
    col_s,
    col_r,
    col_near_r,
    share_s,
    share_r,
    agg_s,
    agg_r,
    back_s,
    back_r,
    sum_s,
    sum_r,
    ret_s,
    ret_r,
):
    rows = feats.shape[0]
    own_tiles = feats.shape[1] // LANES
    columns = cot.shape[1]
    dst_tiles = columns // LANES
    quarter = columns // ZH
    halves = quarter // LANES
    width = w_both.shape[2]
    chunk = width // doms
    mine = ZH * rows
    wide = 2 * width // doms
    tile_total = vals.shape[0]
    key_rows = tile_total // LANES
    dom, feat, zh, nr = place(near)

    loads = [
        pltpu.make_async_copy(source, target, load_sem.at[i])
        for i, (source, target) in enumerate(
            (
                (feats_hbm, feats),
                (send_hbm, send),
                (hub_hbm, hub),
                (dst_hbm, dst),
                (src_hbm, src),
                (w_self_hbm, w_both.at[0]),
                (w_neigh_hbm, w_both.at[1]),
                (bias_hbm, bias),
                (cot_hbm, cot),
            )
        )
    ]
    for load in loads:
        load.start()
    blocks = vals_sem.shape[0]
    block = tile_total // blocks
    vals_loads = [
        pltpu.make_async_copy(
            vals_hbm.at[b * block : (b + 1) * block],
            vals.at[b * block : (b + 1) * block],
            vals_sem.at[b],
        )
        for b in range(blocks)
    ]
    for load in vals_loads:
        load.start()

    barrier = pltpu.get_barrier_semaphore()
    for i in range(1, doms):
        pl.semaphore_signal(
            barrier, inc=1, device_id={"dom": lax.rem(dom + i, doms)}, device_id_type=MESH
        )
    for i in range(1, ZH):
        pl.semaphore_signal(
            barrier,
            inc=1,
            device_id={"feat": lax.rem(zh + i, ZH) * near + nr},
            device_id_type=MESH,
        )
    for i in range(1, near):
        pl.semaphore_signal(
            barrier,
            inc=1,
            device_id={"feat": zh * near + lax.rem(nr + i, near)},
            device_id_type=MESH,
        )

    for load in loads:
        load.wait()

    for t in range(own_tiles):
        table[t] = feats[:, t * LANES : (t + 1) * LANES]
    stacked = table[0:own_tiles].reshape(own_tiles * rows, LANES)
    for reader in range(doms + 1):
        index_row = hub[...] if reader == doms else send[reader : reader + 1, :]
        high = jnp.right_shift(index_row, 7)
        found = jnp.dot(stacked, column_hot(index_row), preferred_element_type=F32)
        found = found.reshape(own_tiles, rows, LANES)
        total = jnp.zeros((rows, LANES), F32)
        for t in range(own_tiles):
            total = total + jnp.where(high == t, found[t], 0.0)
        total = total.astype(BF16)
        if reader < doms:
            picked[reader, 0] = total
        else:
            for d in range(doms):
                picked[d, 1] = total

    lanes_at = lax.broadcasted_iota(jnp.int32, (rows, LANES), 1)
    for m in range(2):
        for n in range(near):
            joined = jnp.zeros((rows, LANES), F32)
            for h in range(ZH):
                first = (h * near + n) * rows
                base, offset = first // LANES * LANES, first % LANES
                piece = w_both[m, :, base : base + LANES].astype(F32)
                shift = (h * rows - offset) % LANES
                if shift:
                    piece = pltpu.roll(piece, shift, 1)
                inside = (lanes_at >= h * rows) & (lanes_at < (h + 1) * rows)
                joined = jnp.where(inside, piece, joined)
            w_regrouped[m, n] = joined.astype(BF16)

    spot = lax.broadcasted_iota(jnp.int32, (rows, rows), 0)
    lane = lax.broadcasted_iota(jnp.int32, (rows, rows), 1)
    bias_column = jnp.sum(jnp.where(spot == lane, bias[...], 0.0), axis=1, keepdims=True)
    bias_wide[...] = jnp.broadcast_to(bias_column, (rows, LANES))
    x_self[zh, nr] = feats[:, aligned(zh, quarter)]
    wrow[dom, :, zh] = w_both[:, :, aligned(dom, chunk)]
    cot_part[zh] = cot[:, aligned(zh, quarter)]
    bias_part[zh] = bias_wide[...]
    table[pl.ds(own_tiles + 2 * dom, 2)] = picked[dom]


    @pl.when(nr == dom)
    def _():
        w_columns[:, zh] = w_regrouped[...]

    given = src[...]
    outside = given - own_tiles
    placed = own_tiles + 2 * lax.rem(outside, doms) + lax.div(outside, doms)
    placed = jnp.where(outside < 0, given, placed)
    key_dst = dst[...]
    links[0:key_rows, :] = key_dst
    links[key_rows : 2 * key_rows, :] = placed
    prev_dst, prev_src, last_dst = 2 * key_rows, 3 * key_rows, 4 * key_rows
    last_src = last_dst + 1
    link_tiles(key_dst, count_ref[0], links, prev_dst, last_dst)
    link_tiles(placed, count_ref[0], links, prev_src, last_src)
    link_copy = pltpu.make_async_copy(links, links_s, link_sem)
    link_copy.start()

    pl.semaphore_wait(barrier, (doms - 1) + (ZH - 1) + (near - 1))

    def halo_copy(i, source, target):
        return remote(
            picked.at[target],
            table.at[pl.ds(own_tiles + 2 * source, 2)],
            halo_s.at[i],
            halo_r.at[i],
            {"dom": target},
        )

    for i in range(1, doms):
        halo_copy(i, dom, lax.rem(dom + i, doms)).start()

    def far_copy(which, i, source, target):
        sources = (
            feats.at[:, aligned(target, quarter)],
            w_both.at[:, :, aligned(dom, chunk)],
            cot.at[:, aligned(target, quarter)],
            bias_wide,
        )
        targets = (
            x_self.at[source, nr],
            wrow.at[dom, :, source],
            cot_part.at[source],
            bias_part.at[source],
        )
        return remote(
            sources[which],
            targets[which],
            far_s.at[which, i],
            far_r.at[which, i],
            {"feat": target * near + nr},
        )

    for i in range(1, ZH):
        far_copy(0, i, zh, lax.rem(zh + i, ZH)).start()
    for i in range(1, ZH):
        far_copy(1, i, zh, lax.rem(zh + i, ZH)).start()

    def col_far_copy(i, source, target):
        return remote(
            w_regrouped,
            w_columns.at[:, source],
            col_s.at[0, i],
            col_r.at[i],
            {"feat": target * near + nr},
        )

    def col_near_copy(i, target):
        return remote(
            w_columns.at[:, :, target],
            wcol.at[dom],
            col_s.at[1, i],
            col_near_r,
            {"feat": zh * near + target},
        )

    @pl.when(nr == dom)
    def _():
        for i in range(1, ZH):
            col_far_copy(i, zh, lax.rem(zh + i, ZH)).start()


    for b in range(blocks):
        vals_loads[b].wait()

        def flip(k, carry):
            flipped[k] = jnp.transpose(vals[k])
            return carry

        lax.fori_loop(b * block, (b + 1) * block, flip, 0, unroll=True)

    def near_copy(which, i, source, target):
        buffer = (x_self, x_agg, g_all)[which]
        return remote(
            buffer.at[:, source],
            buffer.at[:, source],
            near_s.at[which, i],
            near_r.at[which, i],
            {"feat": zh * near + target},
        )

    for i in range(1, ZH):
        far_copy(0, i, lax.rem(zh + ZH - i, ZH), zh).wait_recv()
    for i in range(1, near):
        near_copy(0, i, nr, lax.rem(nr + i, near)).start()
    link_copy.wait()
    for i in range(1, doms):
        halo_copy(i, lax.rem(dom + doms - i, doms), dom).wait_recv()

    runs[tile_total] = jnp.zeros((rows, LANES), F32)

    def chain(left, left_row, tiles, prev_row, first, last):
        def some(j, carry):
            row = lax.div(j * SUB, LANES)
            start = lax.rem(j * SUB, LANES)
            for t in range(SUB):
                product = jnp.dot(
                    left[links_s[left_row + row, start + t]],
                    tiles[j * SUB + t],
                    preferred_element_type=F32,
                )
                runs[j * SUB + t] = runs[links_s[prev_row + row, start + t]] + product
            return carry

        lax.fori_loop(first, last, some, 0)

    steps = tile_total // SUB
    chain(table, key_rows, flipped, prev_dst, 0, steps)
    for u in range(dst_tiles):
        agg[:, u * LANES : (u + 1) * LANES] = runs[links_s[last_dst, u]].astype(BF16)

    def agg_copy(i, source, target):
        return remote(
            agg.at[:, aligned(target, quarter)],
            x_agg.at[source, nr],
            agg_s.at[i],
            agg_r.at[i],
            {"feat": target * near + nr},
        )

    for i in range(1, ZH):
        agg_copy(i, zh, lax.rem(zh + i, ZH)).start()
    x_agg[zh, nr] = agg[:, aligned(zh, quarter)]

    def share_copy(which, i, source, target):
        part = (wrow, wcol)[which].at[source]
        return remote(part, part, share_s.at[which, i], share_r.at[which, i], {"dom": target})


    @pl.when(nr == dom)
    def _():
        for i in range(1, ZH):
            col_far_copy(i, lax.rem(zh + ZH - i, ZH), zh).wait_recv()
        for i in range(1, near):
            col_near_copy(i, lax.rem(nr + i, near)).start()
        wcol[dom] = w_columns[:, :, nr]

    for i in range(1, ZH):
        far_copy(1, i, lax.rem(zh + ZH - i, ZH), zh).wait_recv()
    for i in range(1, doms):
        share_copy(0, i, dom, lax.rem(dom + i, doms)).start()

    for which in (2, 3):
        for i in range(1, ZH):
            far_copy(which, i, zh, lax.rem(zh + i, ZH)).start()

    for i in range(1, ZH):
        agg_copy(i, lax.rem(zh + ZH - i, ZH), zh).wait_recv()
    for i in range(1, near):
        near_copy(1, i, nr, lax.rem(nr + i, near)).start()

    @pl.when(nr != dom)
    def _():
        col_near_copy(0, nr).wait_recv()

    for i in range(1, doms):
        share_copy(1, i, dom, lax.rem(dom + i, doms)).start()
    for i in range(1, near):
        near_copy(0, i, lax.rem(nr + near - i, near), nr).wait_recv()
    for i in range(1, doms):
        share_copy(0, i, lax.rem(dom + doms - i, doms), dom).wait_recv()
    def row_block(m):
        return jnp.concatenate([wrow[d, m].reshape(mine, chunk) for d in range(doms)], axis=1)

    pre = jnp.dot(
        row_block(0),
        x_self[...].reshape(width, quarter),
        preferred_element_type=F32,
    )
    for which in (2, 3):
        for i in range(1, ZH):
            far_copy(which, i, lax.rem(zh + ZH - i, ZH), zh).wait_recv()
    bias_all = jnp.concatenate([bias_part[...].reshape(mine, LANES)] * halves, axis=1)
    pre = pre + bias_all
    for i in range(1, near):
        near_copy(1, i, lax.rem(nr + near - i, near), nr).wait_recv()
    pre = pre + jnp.dot(
        row_block(1),
        x_agg[...].reshape(width, quarter),
        preferred_element_type=F32,
    )
    sig = jax.nn.sigmoid(pre)
    grad = cot_part[...].reshape(mine, quarter).astype(F32) * sig * (1.0 + pre * (1.0 - sig))
    grad = grad.astype(BF16)
    g_part[...] = grad
    g_all[:, nr] = grad.reshape(ZH, rows, quarter)
    for i in range(1, near):
        near_copy(2, i, nr, lax.rem(nr + i, near)).start()

    act = (pre * sig).astype(BF16).reshape(ZH, rows, quarter)
    for h in range(halves):
        act_part[:, h] = act[:, :, h * LANES : (h + 1) * LANES]

    def back_copy(which, i, source, target):
        source_buffer = (act_part, in_parts.at[0], in_parts.at[1])[which]
        target_buffer = (act_out, grad_self, grad_agg)[which]
        return remote(
            source_buffer.at[target],
            target_buffer.at[aligned(source, halves)],
            back_s.at[which, i],
            back_r.at[which, i],
            {"feat": target * near + nr},
        )

    over_x = (((1,), (1,)), ((), ()))
    half_doms = doms // 2
    ones = jnp.ones((2 * SUBLANES, quarter), BF16)
    bias_sum = lax.dot_general(ones, g_part[...], over_x, preferred_element_type=F32)
    bias_sum = bias_sum.astype(BF16)
    for m, x_ref in enumerate((x_self, x_agg)):
        product = lax.dot_general(
            g_part[...],
            x_ref[...].reshape(width, quarter),
            over_x,
            preferred_element_type=F32,
        ).astype(BF16)
        for d in range(half_doms):
            w_parts[m * half_doms + d, 0:mine] = product[:, d * wide : (d + 1) * wide]
    for d in range(doms):
        w_parts[d, mine:, 0:mine] = bias_sum
        w_parts[d, mine:, mine:] = jnp.zeros((2 * SUBLANES, wide - mine), BF16)

    def sum_copy(i, source, target):
        return remote(
            w_parts.at[target],
            w_got.at[source],
            sum_s.at[0, i],
            sum_r.at[0, i],
            {"dom": target},
        )

    for i in range(1, doms):
        sum_copy(i, dom, lax.rem(dom + i, doms)).start()
    for i in range(1, doms):
        share_copy(1, i, lax.rem(dom + doms - i, doms), dom).wait_recv()

    for i in range(1, near):
        near_copy(2, i, lax.rem(nr + near - i, near), nr).wait_recv()
    over_out = (((0,), (0,)), ((), ()))
    for m, target_buffer in ((1, grad_agg), (0, grad_self)):
        back = lax.dot_general(
            jnp.concatenate(
                [wcol[n, m, h] for h in range(ZH) for n in range(near)], axis=0
            ),
            g_all[...].reshape(width, quarter),
            over_out,
            preferred_element_type=F32,
        )
        back = back.astype(BF16).reshape(ZH, rows, quarter)
        for h in range(halves):
            in_parts[m, :, h] = back[:, :, h * LANES : (h + 1) * LANES]
        for i in range(1, ZH):
            back_copy(1 + m, i, zh, lax.rem(zh + i, ZH)).start()
        target_buffer[aligned(zh, halves)] = in_parts[m, zh]
    for i in range(1, ZH):
        back_copy(0, i, zh, lax.rem(zh + i, ZH)).start()
    act_out[aligned(zh, halves)] = act_part[zh]

    for i in range(1, doms):
        sum_copy(i, lax.rem(dom + doms - i, doms), dom).wait_recv()
    w_got[dom] = w_parts[dom]
    total = w_got[0].astype(F32)
    for d in range(1, doms):
        total = total + w_got[d].astype(F32)
    w_sums[:, 0:rows] = total[0:mine].reshape(ZH, rows, wide)
    for h in range(ZH):
        w_sums[h, rows:] = total[mine : mine + SUBLANES]

    def zh_copy(i, source, target):
        return remote(
            w_sums.at[target],
            w_zh.at[source],
            sum_s.at[1, i],
            sum_r.at[1, i],
            {"feat": target * near + nr},
        )

    for i in range(1, ZH):
        zh_copy(i, zh, lax.rem(zh + i, ZH)).start()
    w_zh[zh] = w_sums[zh]

    for i in range(1, ZH):
        back_copy(2, i, lax.rem(zh + ZH - i, ZH), zh).wait_recv()
    def return_copy(which, i, source, target):
        pieces = ((away.at[pl.ds(2 * target, 2)], returned), (w_final.at[:, 0:wide], w_all))
        part, buffer = pieces[which]
        return remote(
            part, buffer.at[source], ret_s.at[which, i], ret_r.at[which, i], {"dom": target}
        )

    chain(grad_agg, 0, vals, prev_src, 0, steps // 2)

    for i in range(1, ZH):
        zh_copy(i, lax.rem(zh + ZH - i, ZH), zh).wait_recv()
    total = w_zh[0]
    for h in range(1, ZH):
        total = total + w_zh[h]
    spot = lax.broadcasted_iota(jnp.int32, (rows, mine), 0) + zh * rows
    lane = lax.broadcasted_iota(jnp.int32, (rows, mine), 1)
    bias_row = total[rows : rows + 1, 0:mine]
    bias_column = jnp.sum(jnp.where(spot == lane, bias_row, 0.0), axis=1, keepdims=True)
    w_final[:, 0:wide] = total[0:rows]
    w_final[:, wide:] = jnp.broadcast_to(bias_column, (rows, LANES))
    for i in range(1, doms):
        return_copy(1, i, dom, lax.rem(dom + i, doms)).start()
    chain(grad_agg, 0, vals, prev_src, steps // 2, steps)

    for t in range(2 * doms):
        away[t] = runs[links_s[last_src, own_tiles + t]].astype(BF16)

    for i in range(1, doms):
        return_copy(0, i, dom, lax.rem(dom + i, doms)).start()
    returned[dom] = away[pl.ds(2 * dom, 2)]
    w_all[dom] = w_final[:, 0:wide]

    for i in range(1, ZH):
        back_copy(1, i, lax.rem(zh + ZH - i, ZH), zh).wait_recv()
    for t in range(own_tiles):
        total = runs[links_s[last_src, t]]
        if t < dst_tiles:
            total = total + grad_self[t].astype(F32)
        grad_own[t] = total

    for i in range(1, ZH):
        back_copy(0, i, lax.rem(zh + ZH - i, ZH), zh).wait_recv()
    for i in range(1, doms):
        target = lax.rem(dom + i, doms)
        halo_copy(i, dom, target).wait_send()
        sum_copy(i, dom, target).wait_send()
        for which in (0, 1):
            share_copy(which, i, dom, target).wait_send()
    for i in range(1, ZH):
        target = lax.rem(zh + i, ZH)
        for which in range(4):
            far_copy(which, i, zh, target).wait_send()
        for which in range(3):
            back_copy(which, i, zh, target).wait_send()
        agg_copy(i, zh, target).wait_send()
        zh_copy(i, zh, target).wait_send()
    for i in range(1, near):
        for which in range(3):
            near_copy(which, i, nr, lax.rem(nr + i, near)).wait_send()

    @pl.when(nr == dom)
    def _():
        for i in range(1, ZH):
            col_far_copy(i, zh, lax.rem(zh + i, ZH)).wait_send()
        for i in range(1, near):
            col_near_copy(i, lax.rem(nr + i, near)).wait_send()

    for i in range(1, doms):
        source = lax.rem(dom + doms - i, doms)
        for which in (0, 1):
            return_copy(which, i, source, dom).wait_recv()
            return_copy(which, i, dom, lax.rem(dom + i, doms)).wait_send()


def finish_kernel(
    doms,
    own_ref,
    returned_ref,
    send_rows,
    hub_rows,
    w_all,
    w_final,
    act_ref,
    act_out,
    feats_out,
    w_self_out,
    w_neigh_out,
    bias_out,
    masked,
):
    own_tiles, rows, _ = own_ref.shape
    dst_tiles = act_ref.shape[0]
    wide = w_all.shape[2]
    hots = []
    for block in range(doms + 1):
        if block == doms:
            index_row = hub_rows[...]
            total = returned_ref[0, 1].astype(F32)
            for d in range(1, doms):
                total = total + returned_ref[d, 1].astype(F32)
            values = total.astype(BF16)
        else:
            index_row = send_rows[block : block + 1, :]
            values = returned_ref[block, 0]
        high = jnp.right_shift(index_row, 7)
        values = values.astype(F32)
        for t in range(own_tiles):
            masked[t, :, block * LANES : (block + 1) * LANES] = jnp.where(
                high == t, values, 0.0
            ).astype(BF16)
        hots.append(column_hot(index_row))
    hot = jnp.concatenate(hots, axis=1)
    added = lax.dot_general(
        masked[...].reshape(own_tiles * rows, (doms + 1) * LANES),
        hot,
        (((1,), (1,)), ((), ())),
        preferred_element_type=F32,
    ).reshape(own_tiles, rows, LANES)
    for t in range(own_tiles):
        feats_out[:, t * LANES : (t + 1) * LANES] = own_ref[t] + added[t]
    for t in range(dst_tiles):
        act_out[:, t * LANES : (t + 1) * LANES] = act_ref[t]
    half = doms // 2
    for d in range(half):
        w_self_out[:, d * wide : (d + 1) * wide] = w_all[d]
        w_neigh_out[:, d * wide : (d + 1) * wide] = w_all[half + d]
    spot = lax.broadcasted_iota(jnp.int32, (rows, LANES), 0)
    lane = lax.broadcasted_iota(jnp.int32, (rows, LANES), 1)
    picked = jnp.where(spot == lane, w_final[:, wide:], 0.0)
    bias_out[...] = jnp.sum(picked, axis=0, keepdims=True)[:, 0:rows]


def shape(dims, dtype):
    return jax.ShapeDtypeStruct(dims, dtype)


def body(
    doms,
    feat_total,
    node_feats,
    send_rows,
    hub_rows,
    tile_dst,
    tile_src,
    tile_count,
    tile_vals,
    w_self,
    w_neigh,
    bias_vec,
    cotangent,
):
    near = feat_total // ZH
    rows, own = node_feats.shape
    own_tiles = own // LANES
    columns = cotangent.shape[1]
    dst_tiles = columns // LANES
    quarter = columns // ZH
    halves = quarter // LANES
    width = w_self.shape[1]
    mine = ZH * rows
    wide = 2 * width // doms
    all_tiles = own_tiles + 2 * doms
    tile_total = tile_src.shape[0]
    key_rows = tile_total // LANES
    dma = pltpu.SemaphoreType.DMA
    in_vmem = pl.BlockSpec(memory_space=pltpu.VMEM)

    send_grid = send_rows.reshape(doms, LANES)
    hub_grid = hub_rows.reshape(1, LANES)

    act_tiles, grad_own, returned, w_all, w_final = pl.pallas_call(
        functools.partial(layer_kernel, doms, near),
        name="layer",
        out_shape=(
            shape((dst_tiles, rows, LANES), BF16),
            shape((own_tiles, rows, LANES), F32),
            shape((doms, 2, rows, LANES), BF16),
            shape((doms, rows, wide), F32),
            shape((rows, wide + LANES), F32),
        ),
        in_specs=[pl.BlockSpec(memory_space=pltpu.SMEM)]
        + [pl.BlockSpec(memory_space=pltpu.HBM)] * 10,
        out_specs=(in_vmem,) * 5,
        scratch_shapes=[
            pltpu.VMEM((rows, own), BF16),
            pltpu.VMEM((doms, LANES), jnp.int32),
            pltpu.VMEM((1, LANES), jnp.int32),
            pltpu.VMEM((key_rows, LANES), jnp.int32),
            pltpu.VMEM((key_rows, LANES), jnp.int32),
            pltpu.VMEM((tile_total, LANES, LANES), BF16),
            pltpu.VMEM((tile_total, LANES, LANES), BF16),
            pltpu.VMEM((tile_total + 1, rows, LANES), F32),
            pltpu.VMEM((4 * key_rows + 8, LANES), jnp.int32),
            pltpu.SMEM((4 * key_rows + 8, LANES), jnp.int32),
            pltpu.VMEM((all_tiles, rows, LANES), BF16),
            pltpu.VMEM((doms, 2, rows, LANES), BF16),
            pltpu.VMEM((2, rows, width), BF16),
            pltpu.VMEM((2, near, rows, mine), BF16),
            pltpu.VMEM((2, ZH, near, rows, mine), BF16),
            pltpu.VMEM((1, rows), F32),
            pltpu.VMEM((rows, LANES), F32),
            pltpu.VMEM((ZH, rows, LANES), F32),
            pltpu.VMEM((rows, columns), BF16),
            pltpu.VMEM((ZH, rows, quarter), BF16),
            pltpu.VMEM((doms, 2, ZH, rows, width // doms), BF16),
            pltpu.VMEM((near, 2, ZH, rows, mine), BF16),
            pltpu.VMEM((ZH, near, rows, quarter), BF16),
            pltpu.VMEM((ZH, near, rows, quarter), BF16),
            pltpu.VMEM((rows, columns), BF16),
            pltpu.VMEM((mine, quarter), BF16),
            pltpu.VMEM((ZH, near, rows, quarter), BF16),
            pltpu.VMEM((ZH, halves, rows, LANES), BF16),
            pltpu.VMEM((2, ZH, halves, rows, LANES), BF16),
            pltpu.VMEM((dst_tiles, rows, LANES), BF16),
            pltpu.VMEM((dst_tiles, rows, LANES), BF16),
            pltpu.VMEM((2 * doms, rows, LANES), BF16),
            pltpu.VMEM((doms, mine + 2 * SUBLANES, wide), BF16),
            pltpu.VMEM((doms, mine + 2 * SUBLANES, wide), BF16),
            pltpu.VMEM((ZH, rows + SUBLANES, wide), F32),
            pltpu.VMEM((ZH, rows + SUBLANES, wide), F32),
            dma((9,)),
            dma((16,)),
            dma,
            dma((doms,)),
            dma((doms,)),
            dma((4, ZH)),
            dma((4, ZH)),
            dma((3, near)),
            dma((3, near)),
            dma((2, max(near, ZH))),
            dma((ZH,)),
            dma,
            dma((2, doms)),
            dma((2, doms)),
            dma((ZH,)),
            dma((ZH,)),
            dma((3, ZH)),
            dma((3, ZH)),
            dma((2, max(doms, ZH))),
            dma((2, max(doms, ZH))),
            dma((2, doms)),
            dma((2, doms)),
        ],
        compiler_params=pltpu.CompilerParams(
            collective_id=0, has_side_effects=True, vmem_limit_bytes=VMEM_LIMIT
        ),
    )(
        tile_count,
        *[
            pltpu.with_memory_space_constraint(array, pltpu.HBM)
            for array in (
                node_feats,
                send_grid,
                hub_grid,
                tile_dst.reshape(key_rows, LANES),
                tile_src.reshape(key_rows, LANES),
                tile_vals,
                w_self,
                w_neigh,
                bias_vec.reshape(1, rows),
                cotangent,
            )
        ],
    )

    activations, grad_feats, grad_w_self, grad_w_neigh, grad_bias = pl.pallas_call(
        functools.partial(finish_kernel, doms),
        name="finish",
        out_shape=(
            shape((rows, columns), BF16),
            shape((rows, own), F32),
            shape((rows, width), F32),
            shape((rows, width), F32),
            shape((1, rows), F32),
        ),
        in_specs=[in_vmem] * 7,
        out_specs=(in_vmem,) * 5,
        scratch_shapes=[pltpu.VMEM((own_tiles, rows, (doms + 1) * LANES), BF16)],
        compiler_params=pltpu.CompilerParams(vmem_limit_bytes=VMEM_LIMIT),
    )(grad_own, returned, send_grid, hub_grid, w_all, w_final, act_tiles)
    return (activations, grad_feats, grad_w_self, grad_w_neigh, grad_bias.reshape(rows))


def solution(mesh):
    return jax.shard_map(
        functools.partial(body, mesh.shape["dom"], mesh.shape["feat"]),
        mesh=mesh,
        in_specs=(
            P("feat", "dom"),
            P("dom"),
            P("dom"),
            P("dom"),
            P("dom"),
            P("dom"),
            P("dom", None, None),
            P("feat", None),
            P("feat", None),
            P("feat"),
            P("feat", "dom"),
        ),
        out_specs=(P("feat", "dom"), P("feat", "dom"), P("feat", None), P("feat", None), P("feat")),
        check_vma=False,
    )
```

```python
import functools

import jax
import jax.numpy as jnp
from jax import lax
from jax.experimental import pallas as pl
from jax.experimental.pallas import tpu as pltpu
from jax.sharding import PartitionSpec as P

MESH = pl.DeviceIdType.MESH
F32 = jnp.float32
BF16 = jnp.bfloat16
ZH = 4
LANES = 128
VMEM_LIMIT = 52 * 1024 * 1024
SUB = 128
SUBLANES = 8


def remote(src, dst, send_sem, recv_sem, where):
    return pltpu.make_async_remote_copy(
        src_ref=src,
        dst_ref=dst,
        send_sem=send_sem,
        recv_sem=recv_sem,
        device_id=where,
        device_id_type=MESH,
    )


def place(near):
    dom = lax.axis_index("dom")
    feat = lax.axis_index("feat")
    return dom, feat, lax.div(feat, near), lax.rem(feat, near)


def aligned(index, size):
    return pl.ds(pl.multiple_of(index * size, size), size)


def column_hot(index_row):
    low = jnp.bitwise_and(index_row, LANES - 1)
    rows = lax.broadcasted_iota(jnp.int32, (LANES, LANES), 0)
    return jnp.where(rows == low, 1.0, 0.0).astype(BF16)


def link_tiles(keys, count, links, first_row, last_row):
    blocks = keys.shape[0]
    none = blocks * LANES
    above = lax.broadcasted_iota(jnp.int32, (LANES, LANES), 0)
    lane = lax.broadcasted_iota(jnp.int32, (LANES, LANES), 1)
    spread = [
        jnp.transpose(jnp.broadcast_to(keys[b : b + 1, :], (LANES, LANES))) for b in range(blocks)
    ]
    for c in range(blocks):
        best = jnp.full((1, LANES), -1, jnp.int32)
        for b in range(c + 1):
            same = spread[b] == keys[c : c + 1, :]
            if b == c:
                same = same & (above < lane)
            found = jnp.where(same, above + b * LANES, -1)
            best = jnp.maximum(best, jnp.max(found, axis=0, keepdims=True))
        links[first_row + c : first_row + c + 1, :] = jnp.where(best < 0, none, best)
    best = jnp.full((1, LANES), -1, jnp.int32)
    for b in range(blocks):
        same = (spread[b] == lane) & (above + b * LANES < count)
        found = jnp.where(same, above + b * LANES, -1)
        best = jnp.maximum(best, jnp.max(found, axis=0, keepdims=True))
    links[last_row : last_row + 1, :] = jnp.where(best < 0, none, best)


def layer_kernel(
    doms,
    near,
    count_ref,
    feats_hbm,
    send_hbm,
    hub_hbm,
    dst_hbm,
    src_hbm,
    vals_hbm,
    w_self_hbm,
    w_neigh_hbm,
    bias_hbm,
    cot_hbm,
    act_out,
    grad_own,
    returned,
    w_all,
    w_final,
    feats,
    send,
    hub,
    dst,
    src,
    vals,
    flipped,
    runs,
    links,
    links_s,
    table,
    picked,
    w_both,
    w_regrouped,
    w_columns,
    bias,
    bias_wide,
    bias_part,
    cot,
    cot_part,
    wrow,
    wcol,
    x_self,
    x_agg,
    agg,
    g_part,
    g_all,
    act_part,
    in_parts,
    grad_agg,
    grad_self,
    away,
    w_parts,
    w_got,
    w_sums,
    w_zh,
    load_sem,
    vals_sem,
    link_sem,
    halo_s,
    halo_r,
    far_s,
    far_r,
    near_s,
    near_r,
    col_s,
    col_r,
    col_near_r,
    share_s,
    share_r,
    agg_s,
    agg_r,
    back_s,
    back_r,
    sum_s,
    sum_r,
    ret_s,
    ret_r,
):
    rows = feats.shape[0]
    own_tiles = feats.shape[1] // LANES
    columns = cot.shape[1]
    dst_tiles = columns // LANES
    quarter = columns // ZH
    halves = quarter // LANES
    width = w_both.shape[2]
    chunk = width // doms
    mine = ZH * rows
    wide = 2 * width // doms
    tile_total = vals.shape[0]
    key_rows = tile_total // LANES
    dom, feat, zh, nr = place(near)

    loads = [
        pltpu.make_async_copy(source, target, load_sem.at[i])
        for i, (source, target) in enumerate(
            (
                (feats_hbm, feats),
                (send_hbm, send),
                (hub_hbm, hub),
                (dst_hbm, dst),
                (src_hbm, src),
                (w_self_hbm, w_both.at[0]),
                (w_neigh_hbm, w_both.at[1]),
                (bias_hbm, bias),
                (cot_hbm, cot),
            )
        )
    ]
    for load in loads:
        load.start()
    blocks = vals_sem.shape[0]
    block = tile_total // blocks
    vals_loads = [
        pltpu.make_async_copy(
            vals_hbm.at[b * block : (b + 1) * block],
            vals.at[b * block : (b + 1) * block],
            vals_sem.at[b],
        )
        for b in range(blocks)
    ]
    for load in vals_loads:
        load.start()

    barrier = pltpu.get_barrier_semaphore()
    for i in range(1, doms):
        pl.semaphore_signal(
            barrier, inc=1, device_id={"dom": lax.rem(dom + i, doms)}, device_id_type=MESH
        )
    for i in range(1, ZH):
        pl.semaphore_signal(
            barrier,
            inc=1,
            device_id={"feat": lax.rem(zh + i, ZH) * near + nr},
            device_id_type=MESH,
        )
    for i in range(1, near):
        pl.semaphore_signal(
            barrier,
            inc=1,
            device_id={"feat": zh * near + lax.rem(nr + i, near)},
            device_id_type=MESH,
        )

    for load in loads:
        load.wait()

    for t in range(own_tiles):
        table[t] = feats[:, t * LANES : (t + 1) * LANES]
    stacked = table[0:own_tiles].reshape(own_tiles * rows, LANES)
    for reader in range(doms + 1):
        index_row = hub[...] if reader == doms else send[reader : reader + 1, :]
        high = jnp.right_shift(index_row, 7)
        found = jnp.dot(stacked, column_hot(index_row), preferred_element_type=F32)
        found = found.reshape(own_tiles, rows, LANES)
        total = jnp.zeros((rows, LANES), F32)
        for t in range(own_tiles):
            total = total + jnp.where(high == t, found[t], 0.0)
        total = total.astype(BF16)
        if reader < doms:
            picked[reader, 0] = total
        else:
            for d in range(doms):
                picked[d, 1] = total

    lanes_at = lax.broadcasted_iota(jnp.int32, (rows, LANES), 1)
    for m in range(2):
        for n in range(near):
            joined = jnp.zeros((rows, LANES), F32)
            for h in range(ZH):
                first = (h * near + n) * rows
                base, offset = first // LANES * LANES, first % LANES
                piece = w_both[m, :, base : base + LANES].astype(F32)
                shift = (h * rows - offset) % LANES
                if shift:
                    piece = pltpu.roll(piece, shift, 1)
                inside = (lanes_at >= h * rows) & (lanes_at < (h + 1) * rows)
                joined = jnp.where(inside, piece, joined)
            w_regrouped[m, n] = joined.astype(BF16)

    spot = lax.broadcasted_iota(jnp.int32, (rows, rows), 0)
    lane = lax.broadcasted_iota(jnp.int32, (rows, rows), 1)
    bias_column = jnp.sum(jnp.where(spot == lane, bias[...], 0.0), axis=1, keepdims=True)
    bias_wide[...] = jnp.broadcast_to(bias_column, (rows, LANES))
    x_self[zh, nr] = feats[:, aligned(zh, quarter)]
    wrow[dom, :, zh] = w_both[:, :, aligned(dom, chunk)]
    cot_part[zh] = cot[:, aligned(zh, quarter)]
    bias_part[zh] = bias_wide[...]
    table[pl.ds(own_tiles + 2 * dom, 2)] = picked[dom]


    @pl.when(nr == dom)
    def _():
        w_columns[:, zh] = w_regrouped[...]

    given = src[...]
    outside = given - own_tiles
    placed = own_tiles + 2 * lax.rem(outside, doms) + lax.div(outside, doms)
    placed = jnp.where(outside < 0, given, placed)
    key_dst = dst[...]
    links[0:key_rows, :] = key_dst
    links[key_rows : 2 * key_rows, :] = placed
    prev_dst, prev_src, last_dst = 2 * key_rows, 3 * key_rows, 4 * key_rows
    last_src = last_dst + 1
    link_tiles(key_dst, count_ref[0], links, prev_dst, last_dst)
    link_tiles(placed, count_ref[0], links, prev_src, last_src)
    link_copy = pltpu.make_async_copy(links, links_s, link_sem)
    link_copy.start()

    pl.semaphore_wait(barrier, (doms - 1) + (ZH - 1) + (near - 1))

    def halo_copy(i, source, target):
        return remote(
            picked.at[target],
            table.at[pl.ds(own_tiles + 2 * source, 2)],
            halo_s.at[i],
            halo_r.at[i],
            {"dom": target},
        )

    for i in range(1, doms):
        halo_copy(i, dom, lax.rem(dom + i, doms)).start()

    def far_copy(which, i, source, target):
        sources = (
            feats.at[:, aligned(target, quarter)],
            w_both.at[:, :, aligned(dom, chunk)],
            cot.at[:, aligned(target, quarter)],
            bias_wide,
        )
        targets = (
            x_self.at[source, nr],
            wrow.at[dom, :, source],
            cot_part.at[source],
            bias_part.at[source],
        )
        return remote(
            sources[which],
            targets[which],
            far_s.at[which, i],
            far_r.at[which, i],
            {"feat": target * near + nr},
        )

    for i in range(1, ZH):
        far_copy(0, i, zh, lax.rem(zh + i, ZH)).start()

    def col_far_copy(i, source, target):
        return remote(
            w_regrouped,
            w_columns.at[:, source],
            col_s.at[0, i],
            col_r.at[i],
            {"feat": target * near + nr},
        )

    def col_near_copy(i, target):
        return remote(
            w_columns.at[:, :, target],
            wcol.at[dom],
            col_s.at[1, i],
            col_near_r,
            {"feat": zh * near + target},
        )


    for b in range(blocks):
        vals_loads[b].wait()

        def flip(k, carry):
            flipped[k] = jnp.transpose(vals[k])
            return carry

        lax.fori_loop(b * block, (b + 1) * block, flip, 0, unroll=True)

    def near_copy(which, i, source, target):
        buffer = (x_self, x_agg, g_all)[which]
        return remote(
            buffer.at[:, source],
            buffer.at[:, source],
            near_s.at[which, i],
            near_r.at[which, i],
            {"feat": zh * near + target},
        )

    for i in range(1, ZH):
        far_copy(0, i, lax.rem(zh + ZH - i, ZH), zh).wait_recv()
    for i in range(1, near):
        near_copy(0, i, nr, lax.rem(nr + i, near)).start()
    link_copy.wait()
    for i in range(1, doms):
        halo_copy(i, lax.rem(dom + doms - i, doms), dom).wait_recv()

    for i in range(1, ZH):
        far_copy(1, i, zh, lax.rem(zh + i, ZH)).start()

    @pl.when(nr == dom)
    def _():
        for i in range(1, ZH):
            col_far_copy(i, zh, lax.rem(zh + i, ZH)).start()

    runs[tile_total] = jnp.zeros((rows, LANES), F32)

    def chain(left, left_row, tiles, prev_row, first, last):
        def some(j, carry):
            row = lax.div(j * SUB, LANES)
            start = lax.rem(j * SUB, LANES)
            for t in range(SUB):
                product = jnp.dot(
                    left[links_s[left_row + row, start + t]],
                    tiles[j * SUB + t],
                    preferred_element_type=F32,
                )
                runs[j * SUB + t] = runs[links_s[prev_row + row, start + t]] + product
            return carry

        lax.fori_loop(first, last, some, 0)

    steps = tile_total // SUB
    chain(table, key_rows, flipped, prev_dst, 0, steps)
    for u in range(dst_tiles):
        agg[:, u * LANES : (u + 1) * LANES] = runs[links_s[last_dst, u]].astype(BF16)

    def agg_copy(i, source, target):
        return remote(
            agg.at[:, aligned(target, quarter)],
            x_agg.at[source, nr],
            agg_s.at[i],
            agg_r.at[i],
            {"feat": target * near + nr},
        )

    for i in range(1, ZH):
        agg_copy(i, zh, lax.rem(zh + i, ZH)).start()
    x_agg[zh, nr] = agg[:, aligned(zh, quarter)]

    def share_copy(which, i, source, target):
        part = (wrow, wcol)[which].at[source]
        return remote(part, part, share_s.at[which, i], share_r.at[which, i], {"dom": target})


    @pl.when(nr == dom)
    def _():
        for i in range(1, ZH):
            col_far_copy(i, lax.rem(zh + ZH - i, ZH), zh).wait_recv()
        for i in range(1, near):
            col_near_copy(i, lax.rem(nr + i, near)).start()
        wcol[dom] = w_columns[:, :, nr]

    for i in range(1, ZH):
        far_copy(1, i, lax.rem(zh + ZH - i, ZH), zh).wait_recv()
    for i in range(1, doms):
        share_copy(0, i, dom, lax.rem(dom + i, doms)).start()

    for which in (2, 3):
        for i in range(1, ZH):
            far_copy(which, i, zh, lax.rem(zh + i, ZH)).start()

    for i in range(1, ZH):
        agg_copy(i, lax.rem(zh + ZH - i, ZH), zh).wait_recv()
    for i in range(1, near):
        near_copy(1, i, nr, lax.rem(nr + i, near)).start()

    @pl.when(nr != dom)
    def _():
        col_near_copy(0, nr).wait_recv()

    for i in range(1, doms):
        share_copy(1, i, dom, lax.rem(dom + i, doms)).start()
    for i in range(1, near):
        near_copy(0, i, lax.rem(nr + near - i, near), nr).wait_recv()
    for i in range(1, doms):
        share_copy(0, i, lax.rem(dom + doms - i, doms), dom).wait_recv()
    def row_block(m):
        return jnp.concatenate([wrow[d, m].reshape(mine, chunk) for d in range(doms)], axis=1)

    pre = jnp.dot(
        row_block(0),
        x_self[...].reshape(width, quarter),
        preferred_element_type=F32,
    )
    for which in (2, 3):
        for i in range(1, ZH):
            far_copy(which, i, lax.rem(zh + ZH - i, ZH), zh).wait_recv()
    bias_all = jnp.concatenate([bias_part[...].reshape(mine, LANES)] * halves, axis=1)
    pre = pre + bias_all
    for i in range(1, near):
        near_copy(1, i, lax.rem(nr + near - i, near), nr).wait_recv()
    pre = pre + jnp.dot(
        row_block(1),
        x_agg[...].reshape(width, quarter),
        preferred_element_type=F32,
    )
    sig = jax.nn.sigmoid(pre)
    grad = cot_part[...].reshape(mine, quarter).astype(F32) * sig * (1.0 + pre * (1.0 - sig))
    grad = grad.astype(BF16)
    g_part[...] = grad
    g_all[:, nr] = grad.reshape(ZH, rows, quarter)
    for i in range(1, near):
        near_copy(2, i, nr, lax.rem(nr + i, near)).start()

    act = (pre * sig).astype(BF16).reshape(ZH, rows, quarter)
    for h in range(halves):
        act_part[:, h] = act[:, :, h * LANES : (h + 1) * LANES]

    def back_copy(which, i, source, target):
        source_buffer = (act_part, in_parts.at[0], in_parts.at[1])[which]
        target_buffer = (act_out, grad_self, grad_agg)[which]
        return remote(
            source_buffer.at[target],
            target_buffer.at[aligned(source, halves)],
            back_s.at[which, i],
            back_r.at[which, i],
            {"feat": target * near + nr},
        )

    over_x = (((1,), (1,)), ((), ()))
    half_doms = doms // 2
    ones = jnp.ones((2 * SUBLANES, quarter), BF16)
    bias_sum = lax.dot_general(ones, g_part[...], over_x, preferred_element_type=F32)
    bias_sum = bias_sum.astype(BF16)
    for m, x_ref in enumerate((x_self, x_agg)):
        product = lax.dot_general(
            g_part[...],
            x_ref[...].reshape(width, quarter),
            over_x,
            preferred_element_type=F32,
        ).astype(BF16)
        for d in range(half_doms):
            w_parts[m * half_doms + d, 0:mine] = product[:, d * wide : (d + 1) * wide]
    for d in range(doms):
        w_parts[d, mine:, 0:mine] = bias_sum
        w_parts[d, mine:, mine:] = jnp.zeros((2 * SUBLANES, wide - mine), BF16)

    def sum_copy(i, source, target):
        return remote(
            w_parts.at[target],
            w_got.at[source],
            sum_s.at[0, i],
            sum_r.at[0, i],
            {"dom": target},
        )

    for i in range(1, doms):
        sum_copy(i, dom, lax.rem(dom + i, doms)).start()
    for i in range(1, doms):
        share_copy(1, i, lax.rem(dom + doms - i, doms), dom).wait_recv()

    for i in range(1, near):
        near_copy(2, i, lax.rem(nr + near - i, near), nr).wait_recv()
    over_out = (((0,), (0,)), ((), ()))
    for m, target_buffer in ((1, grad_agg), (0, grad_self)):
        back = lax.dot_general(
            jnp.concatenate(
                [wcol[n, m, h] for h in range(ZH) for n in range(near)], axis=0
            ),
            g_all[...].reshape(width, quarter),
            over_out,
            preferred_element_type=F32,
        )
        back = back.astype(BF16).reshape(ZH, rows, quarter)
        for h in range(halves):
            in_parts[m, :, h] = back[:, :, h * LANES : (h + 1) * LANES]
        for i in range(1, ZH):
            back_copy(1 + m, i, zh, lax.rem(zh + i, ZH)).start()
        target_buffer[aligned(zh, halves)] = in_parts[m, zh]
    for i in range(1, ZH):
        back_copy(0, i, zh, lax.rem(zh + i, ZH)).start()
    act_out[aligned(zh, halves)] = act_part[zh]

    for i in range(1, doms):
        sum_copy(i, lax.rem(dom + doms - i, doms), dom).wait_recv()
    w_got[dom] = w_parts[dom]
    total = w_got[0].astype(F32)
    for d in range(1, doms):
        total = total + w_got[d].astype(F32)
    w_sums[:, 0:rows] = total[0:mine].reshape(ZH, rows, wide)
    for h in range(ZH):
        w_sums[h, rows:] = total[mine : mine + SUBLANES]

    def zh_copy(i, source, target):
        return remote(
            w_sums.at[target],
            w_zh.at[source],
            sum_s.at[1, i],
            sum_r.at[1, i],
            {"feat": target * near + nr},
        )

    for i in range(1, ZH):
        zh_copy(i, zh, lax.rem(zh + i, ZH)).start()
    w_zh[zh] = w_sums[zh]

    for i in range(1, ZH):
        back_copy(2, i, lax.rem(zh + ZH - i, ZH), zh).wait_recv()
    def return_copy(which, i, source, target):
        pieces = ((away.at[pl.ds(2 * target, 2)], returned), (w_final.at[:, 0:wide], w_all))
        part, buffer = pieces[which]
        return remote(
            part, buffer.at[source], ret_s.at[which, i], ret_r.at[which, i], {"dom": target}
        )

    chain(grad_agg, 0, vals, prev_src, 0, steps // 2)

    for i in range(1, ZH):
        zh_copy(i, lax.rem(zh + ZH - i, ZH), zh).wait_recv()
    total = w_zh[0]
    for h in range(1, ZH):
        total = total + w_zh[h]
    spot = lax.broadcasted_iota(jnp.int32, (rows, mine), 0) + zh * rows
    lane = lax.broadcasted_iota(jnp.int32, (rows, mine), 1)
    bias_row = total[rows : rows + 1, 0:mine]
    bias_column = jnp.sum(jnp.where(spot == lane, bias_row, 0.0), axis=1, keepdims=True)
    w_final[:, 0:wide] = total[0:rows]
    w_final[:, wide:] = jnp.broadcast_to(bias_column, (rows, LANES))
    for i in range(1, doms):
        return_copy(1, i, dom, lax.rem(dom + i, doms)).start()
    chain(grad_agg, 0, vals, prev_src, steps // 2, steps)

    for t in range(2 * doms):
        away[t] = runs[links_s[last_src, own_tiles + t]].astype(BF16)

    for i in range(1, doms):
        return_copy(0, i, dom, lax.rem(dom + i, doms)).start()
    returned[dom] = away[pl.ds(2 * dom, 2)]
    w_all[dom] = w_final[:, 0:wide]

    for i in range(1, ZH):
        back_copy(1, i, lax.rem(zh + ZH - i, ZH), zh).wait_recv()
    for t in range(own_tiles):
        total = runs[links_s[last_src, t]]
        if t < dst_tiles:
            total = total + grad_self[t].astype(F32)
        grad_own[t] = total

    for i in range(1, ZH):
        back_copy(0, i, lax.rem(zh + ZH - i, ZH), zh).wait_recv()
    for i in range(1, doms):
        target = lax.rem(dom + i, doms)
        halo_copy(i, dom, target).wait_send()
        sum_copy(i, dom, target).wait_send()
        for which in (0, 1):
            share_copy(which, i, dom, target).wait_send()
    for i in range(1, ZH):
        target = lax.rem(zh + i, ZH)
        for which in range(4):
            far_copy(which, i, zh, target).wait_send()
        for which in range(3):
            back_copy(which, i, zh, target).wait_send()
        agg_copy(i, zh, target).wait_send()
        zh_copy(i, zh, target).wait_send()
    for i in range(1, near):
        for which in range(3):
            near_copy(which, i, nr, lax.rem(nr + i, near)).wait_send()

    @pl.when(nr == dom)
    def _():
        for i in range(1, ZH):
            col_far_copy(i, zh, lax.rem(zh + i, ZH)).wait_send()
        for i in range(1, near):
            col_near_copy(i, lax.rem(nr + i, near)).wait_send()

    for i in range(1, doms):
        source = lax.rem(dom + doms - i, doms)
        for which in (0, 1):
            return_copy(which, i, source, dom).wait_recv()
            return_copy(which, i, dom, lax.rem(dom + i, doms)).wait_send()


def finish_kernel(
    doms,
    own_ref,
    returned_ref,
    send_rows,
    hub_rows,
    w_all,
    w_final,
    act_ref,
    act_out,
    feats_out,
    w_self_out,
    w_neigh_out,
    bias_out,
    masked,
):
    own_tiles, rows, _ = own_ref.shape
    dst_tiles = act_ref.shape[0]
    wide = w_all.shape[2]
    hots = []
    for block in range(doms + 1):
        if block == doms:
            index_row = hub_rows[...]
            total = returned_ref[0, 1].astype(F32)
            for d in range(1, doms):
                total = total + returned_ref[d, 1].astype(F32)
            values = total.astype(BF16)
        else:
            index_row = send_rows[block : block + 1, :]
            values = returned_ref[block, 0]
        high = jnp.right_shift(index_row, 7)
        values = values.astype(F32)
        for t in range(own_tiles):
            masked[t, :, block * LANES : (block + 1) * LANES] = jnp.where(
                high == t, values, 0.0
            ).astype(BF16)
        hots.append(column_hot(index_row))
    hot = jnp.concatenate(hots, axis=1)
    added = lax.dot_general(
        masked[...].reshape(own_tiles * rows, (doms + 1) * LANES),
        hot,
        (((1,), (1,)), ((), ())),
        preferred_element_type=F32,
    ).reshape(own_tiles, rows, LANES)
    for t in range(own_tiles):
        feats_out[:, t * LANES : (t + 1) * LANES] = own_ref[t] + added[t]
    for t in range(dst_tiles):
        act_out[:, t * LANES : (t + 1) * LANES] = act_ref[t]
    half = doms // 2
    for d in range(half):
        w_self_out[:, d * wide : (d + 1) * wide] = w_all[d]
        w_neigh_out[:, d * wide : (d + 1) * wide] = w_all[half + d]
    spot = lax.broadcasted_iota(jnp.int32, (rows, LANES), 0)
    lane = lax.broadcasted_iota(jnp.int32, (rows, LANES), 1)
    picked = jnp.where(spot == lane, w_final[:, wide:], 0.0)
    bias_out[...] = jnp.sum(picked, axis=0, keepdims=True)[:, 0:rows]


def shape(dims, dtype):
    return jax.ShapeDtypeStruct(dims, dtype)


def body(
    doms,
    feat_total,
    node_feats,
    send_rows,
    hub_rows,
    tile_dst,
    tile_src,
    tile_count,
    tile_vals,
    w_self,
    w_neigh,
    bias_vec,
    cotangent,
):
    near = feat_total // ZH
    rows, own = node_feats.shape
    own_tiles = own // LANES
    columns = cotangent.shape[1]
    dst_tiles = columns // LANES
    quarter = columns // ZH
    halves = quarter // LANES
    width = w_self.shape[1]
    mine = ZH * rows
    wide = 2 * width // doms
    all_tiles = own_tiles + 2 * doms
    tile_total = tile_src.shape[0]
    key_rows = tile_total // LANES
    dma = pltpu.SemaphoreType.DMA
    in_vmem = pl.BlockSpec(memory_space=pltpu.VMEM)

    send_grid = send_rows.reshape(doms, LANES)
    hub_grid = hub_rows.reshape(1, LANES)

    act_tiles, grad_own, returned, w_all, w_final = pl.pallas_call(
        functools.partial(layer_kernel, doms, near),
        name="layer",
        out_shape=(
            shape((dst_tiles, rows, LANES), BF16),
            shape((own_tiles, rows, LANES), F32),
            shape((doms, 2, rows, LANES), BF16),
            shape((doms, rows, wide), F32),
            shape((rows, wide + LANES), F32),
        ),
        in_specs=[pl.BlockSpec(memory_space=pltpu.SMEM)]
        + [pl.BlockSpec(memory_space=pltpu.HBM)] * 10,
        out_specs=(in_vmem,) * 5,
        scratch_shapes=[
            pltpu.VMEM((rows, own), BF16),
            pltpu.VMEM((doms, LANES), jnp.int32),
            pltpu.VMEM((1, LANES), jnp.int32),
            pltpu.VMEM((key_rows, LANES), jnp.int32),
            pltpu.VMEM((key_rows, LANES), jnp.int32),
            pltpu.VMEM((tile_total, LANES, LANES), BF16),
            pltpu.VMEM((tile_total, LANES, LANES), BF16),
            pltpu.VMEM((tile_total + 1, rows, LANES), F32),
            pltpu.VMEM((4 * key_rows + 8, LANES), jnp.int32),
            pltpu.SMEM((4 * key_rows + 8, LANES), jnp.int32),
            pltpu.VMEM((all_tiles, rows, LANES), BF16),
            pltpu.VMEM((doms, 2, rows, LANES), BF16),
            pltpu.VMEM((2, rows, width), BF16),
            pltpu.VMEM((2, near, rows, mine), BF16),
            pltpu.VMEM((2, ZH, near, rows, mine), BF16),
            pltpu.VMEM((1, rows), F32),
            pltpu.VMEM((rows, LANES), F32),
            pltpu.VMEM((ZH, rows, LANES), F32),
            pltpu.VMEM((rows, columns), BF16),
            pltpu.VMEM((ZH, rows, quarter), BF16),
            pltpu.VMEM((doms, 2, ZH, rows, width // doms), BF16),
            pltpu.VMEM((near, 2, ZH, rows, mine), BF16),
            pltpu.VMEM((ZH, near, rows, quarter), BF16),
            pltpu.VMEM((ZH, near, rows, quarter), BF16),
            pltpu.VMEM((rows, columns), BF16),
            pltpu.VMEM((mine, quarter), BF16),
            pltpu.VMEM((ZH, near, rows, quarter), BF16),
            pltpu.VMEM((ZH, halves, rows, LANES), BF16),
            pltpu.VMEM((2, ZH, halves, rows, LANES), BF16),
            pltpu.VMEM((dst_tiles, rows, LANES), BF16),
            pltpu.VMEM((dst_tiles, rows, LANES), BF16),
            pltpu.VMEM((2 * doms, rows, LANES), BF16),
            pltpu.VMEM((doms, mine + 2 * SUBLANES, wide), BF16),
            pltpu.VMEM((doms, mine + 2 * SUBLANES, wide), BF16),
            pltpu.VMEM((ZH, rows + SUBLANES, wide), F32),
            pltpu.VMEM((ZH, rows + SUBLANES, wide), F32),
            dma((9,)),
            dma((16,)),
            dma,
            dma((doms,)),
            dma((doms,)),
            dma((4, ZH)),
            dma((4, ZH)),
            dma((3, near)),
            dma((3, near)),
            dma((2, max(near, ZH))),
            dma((ZH,)),
            dma,
            dma((2, doms)),
            dma((2, doms)),
            dma((ZH,)),
            dma((ZH,)),
            dma((3, ZH)),
            dma((3, ZH)),
            dma((2, max(doms, ZH))),
            dma((2, max(doms, ZH))),
            dma((2, doms)),
            dma((2, doms)),
        ],
        compiler_params=pltpu.CompilerParams(
            collective_id=0, has_side_effects=True, vmem_limit_bytes=VMEM_LIMIT
        ),
    )(
        tile_count,
        *[
            pltpu.with_memory_space_constraint(array, pltpu.HBM)
            for array in (
                node_feats,
                send_grid,
                hub_grid,
                tile_dst.reshape(key_rows, LANES),
                tile_src.reshape(key_rows, LANES),
                tile_vals,
                w_self,
                w_neigh,
                bias_vec.reshape(1, rows),
                cotangent,
            )
        ],
    )

    activations, grad_feats, grad_w_self, grad_w_neigh, grad_bias = pl.pallas_call(
        functools.partial(finish_kernel, doms),
        name="finish",
        out_shape=(
            shape((rows, columns), BF16),
            shape((rows, own), F32),
            shape((rows, width), F32),
            shape((rows, width), F32),
            shape((1, rows), F32),
        ),
        in_specs=[in_vmem] * 7,
        out_specs=(in_vmem,) * 5,
        scratch_shapes=[pltpu.VMEM((own_tiles, rows, (doms + 1) * LANES), BF16)],
        compiler_params=pltpu.CompilerParams(vmem_limit_bytes=VMEM_LIMIT),
    )(grad_own, returned, send_grid, hub_grid, w_all, w_final, act_tiles)
    return (activations, grad_feats, grad_w_self, grad_w_neigh, grad_bias.reshape(rows))


def solution(mesh):
    return jax.shard_map(
        functools.partial(body, mesh.shape["dom"], mesh.shape["feat"]),
        mesh=mesh,
        in_specs=(
            P("feat", "dom"),
            P("dom"),
            P("dom"),
            P("dom"),
            P("dom"),
            P("dom"),
            P("dom", None, None),
            P("feat", None),
            P("feat", None),
            P("feat"),
            P("feat", "dom"),
        ),
        out_specs=(P("feat", "dom"), P("feat", "dom"), P("feat", None), P("feat", None), P("feat")),
        check_vma=False,
    )
```
